256 devices in a mesh: dp: 32 (over y, z_hi, core), seq: 8 (over x, z_lo).
Axes of the slice: x: 4, y: 4, z: 8 (z_hi: 4, z_lo: 2; z = z_hi * 2 + z_lo), core: 2. Of those that a mesh axis runs over, the one named last changes fastest.
Arguments:
- qkv_input: bfloat16 [32768, 3, 3072], P(('dp', 'seq')), may hold values from -40 to 40
- latents: bfloat16 [32768, 3072], P(('dp', 'seq')), may hold values from -0.29882812 to 0.29882812
- cotangent: bfloat16 [32768, 3072], P(('dp', 'seq')), may hold values from -6 to 6
- out_weight: bfloat16 [3072, 3072], P('seq', 'dp'), may hold values from -0.109375 to 0.109375
- gate_table: float32 [64, 3072], replicated, may hold values from -8 to 8
- timesteps: int32 [32, 3], P('dp'), may hold values from 0 to 63
- frames: int32 [32, 3], P('dp'), may hold values from 1 to 10, 16 in all within a row
Outputs:
- output: bfloat16 [32768, 3072], P(('dp', 'seq'))
- grad_qkv: bfloat16 [32768, 3, 3072], P(('dp', 'seq'))
- grad_weight: float32 [3072, 3072], P('seq', 'dp')
The draws below stay inside these ranges and needn't reach their ends.
Inputs may be any that keep to these rules, and one draw needn't show every extreme that they name: Each pack's 3 clips cover its 16 frames exactly; in every pack the longest clip has 10 frames.
All inputs are finite; a program needn't handle non-finite values.
Results may differ from the reference program's by a relative error of at most 0.019.
Values may be sent and summed in bfloat16 or wider, within the bound.
No kernel may reach another device: no remote copies, remote signals or barrier semaphores. Data moves between devices by JAX's collectives and lax.ppermute only.
A program may use at most 192 MiB of HBM per device.

```python
import math
import jax
import jax.numpy as jnp
import numpy as np
from jax import lax

D = 3072
HD = 128
FRAME_TOK = 64
CLIPS = 3
NT = 64
PACK = 1024
PACKF = 16
MOSTF = 10
GROUPS = 32
TOKENS = 32768
N_SEQ = 8


def draw_qkv_input(key, part):
    first = jax.random.fold_in(key, 0)
    return jnp.clip(jax.random.normal(first, (TOKENS, 3, D), jnp.float32), -6.0, 6.0).astype(jnp.bfloat16)


def touch_ends(entries, rng, low, largest):
    dims = entries.shape
    spot = [jax.random.randint(jax.random.fold_in(rng, axis), (), 0, dims[axis]) for axis in range(len(dims))]
    entries = entries.at[tuple(spot)].set(low)
    longest = dims.index(max(dims))
    spot[longest] = (spot[longest] + 1) % dims[longest]
    return entries.at[tuple(spot)].set(largest)


def levels(key, extent, shards, smallest, high):
    gain, own = 1.0, jax.random.fold_in(key, 6)
    for dim, shards_of in shards:
        draws = jnp.exp(jax.random.uniform(jax.random.fold_in(own, dim), (shards_of,), jnp.float32, smallest / len(shards), high / len(shards)))
        gain = gain * jnp.repeat(draws, extent[dim] // shards_of).reshape([-1 if axis == dim else 1 for axis in range(len(extent))])
    return gain


def split_up(count, total, reach, lean):
    loads = [(1 << 20) // math.isqrt(rank ** lean) + 1 for rank in range(2, count + 1)]
    surplus, holding = total - reach - (count - 1), [1] * (count - 1)
    while surplus > 0:
        movable = [i for i in range(count - 1) if holding[i] < reach]
        mass, remaining = sum([loads[i] for i in movable]), surplus
        for i in movable:
            extra = min(reach - holding[i], max(1, remaining * loads[i] // mass), surplus)
            holding[i] = holding[i] + extra
            surplus = surplus - extra
    return np.array([reach] + holding)


def uneven_parts(rng, count, total, limit, lean):
    if count == 2:
        one = jax.random.randint(rng, (), max(1, total - limit), min(limit, total - 1) + 1)
        return jnp.stack([one, total - one])
    sizes = jnp.asarray(split_up(count, total, limit, lean), jnp.int32)
    twos = (count - 1) // 2
    donor, taker = sizes[1:1 + 2 * twos:2], sizes[2:2 + 2 * twos:2]
    slack = jnp.minimum(donor - 1, limit - taker)
    moved = jax.random.randint(jax.random.fold_in(rng, 1), (twos,), 0, 1 << 20) % (slack + 1)
    sizes = sizes.at[1:1 + 2 * twos:2].set(donor - moved).at[2:2 + 2 * twos:2].set(taker + moved)
    return sizes[jax.random.permutation(jax.random.fold_in(rng, 2), count)]


def gaussian(own_key, dims, scale, limit, cuts=(), kind=jnp.bfloat16):
    values = scale * jax.random.normal(own_key, dims, jnp.float32)
    if cuts:
        values = values * levels(own_key, dims, cuts, -0.22, 0.18)
    return jnp.clip(values, -limit, limit).astype(kind)


def setup_inputs(seed: int = 0) -> dict:
    streams_of = jax.random.split(jax.random.key(seed), 8)
    qkv_input = draw_qkv_input(jax.random.fold_in(streams_of[7], 71), 0)
    latents = gaussian(streams_of[1], (TOKENS, D), 0.05, 0.29882812, ((0, 256),))
    cotangent = gaussian(streams_of[2], (TOKENS, D), 1.0, 6.0, ((0, 256),))
    out_weight = gaussian(streams_of[3], (D, D), D ** -0.5, 0.109375, ((0, 8), (1, 32)))
    gate_table = gaussian(streams_of[4], (NT, D), 2.0, 8.0, (), jnp.float32)
    timesteps = touch_ends(jax.random.randint(streams_of[5], (GROUPS, CLIPS), 0, NT), jax.random.fold_in(streams_of[5], 1), 0, NT - 1).astype(jnp.int32)
    frames = jax.vmap(lambda own: uneven_parts(own, CLIPS, PACKF, MOSTF, 2))(jax.random.split(streams_of[6], GROUPS)).reshape((GROUPS, CLIPS)).astype(jnp.int32)
    return {"qkv_input": qkv_input, "latents": latents, "cotangent": cotangent, "out_weight": out_weight, "gate_table": gate_table, "timesteps": timesteps, "frames": frames}


def clip_index(frame_row, start, count):
    ends = jnp.cumsum(frame_row) * FRAME_TOK
    places = start + jnp.arange(count, dtype=jnp.int32)
    return lax.optimization_barrier(jnp.sum((places[:, None] >= ends[None, :]).astype(jnp.int32), axis=1))

def token_gate(frame_row, step_row, table, start, count):
    bins = jnp.arange(table.shape[0], dtype=jnp.int32)
    pick = (step_row[:, None] == bins[None, :]).astype(jnp.float32)
    clip_rows = jnp.dot(pick, table, precision=lax.Precision.HIGHEST)
    which = clip_index(frame_row, start, count)
    member = (which[:, None] == jnp.arange(frame_row.shape[0], dtype=jnp.int32)[None, :]).astype(jnp.float32)
    return jnp.dot(member, clip_rows, precision=lax.Precision.HIGHEST)

def attend(query, keys, values, which):
    rows = query.shape[0]
    count = query.shape[1] // HD
    qf = query.reshape(rows, count, HD).astype(jnp.float32)
    kf = keys.reshape(rows, count, HD).astype(jnp.float32)
    vf = values.reshape(rows, count, HD).astype(jnp.float32)
    scores = jnp.einsum('qhd,khd->hqk', qf, kf) / jnp.sqrt(jnp.float32(HD))
    same = which[:, None] == which[None, :]
    scores = jnp.where(same[None], scores, jnp.float32(-1e+30))
    top = lax.optimization_barrier(jnp.max(scores, axis=-1, keepdims=True))
    expo = jnp.exp(scores - top)
    probs = expo / lax.optimization_barrier(jnp.sum(expo, axis=-1, keepdims=True))
    probs_b = probs.astype(jnp.bfloat16)
    mixed = jnp.einsum('hqk,khd->qhd', probs_b.astype(jnp.float32), vf)
    return mixed.reshape(rows, count * HD)

def reference(qkv_input, latents, cotangent, out_weight, gate_table, timesteps, frames):
    width = D // N_SEQ
    grouped = qkv_input.reshape(GROUPS, PACK, 3, D)
    lat_groups = latents.reshape(GROUPS, PACK, D)
    cot_groups = cotangent.reshape(GROUPS, PACK, D)

    def one_pack(total, items):
        qkv_g, lat_g, cot_g, frame_row, step_row = items
        which = clip_index(frame_row, 0, PACK)
        gate = token_gate(frame_row, step_row, gate_table, 0, PACK)
        attn_f, back = jax.vjp(lambda a, b, c: attend(a, b, c, which), qkv_g[:, 0], qkv_g[:, 1], qkv_g[:, 2])
        attn = attn_f.astype(jnp.bfloat16)
        proj = jnp.zeros((PACK, D), jnp.float32)
        for index in range(N_SEQ):
            part = jnp.dot(attn[:, index * width:(index + 1) * width], out_weight[index * width:(index + 1) * width], preferred_element_type=jnp.float32).astype(jnp.bfloat16)
            part = lax.optimization_barrier(part)
            proj = proj + part.astype(jnp.float32)
        output = (lat_g.astype(jnp.float32) + gate * proj).astype(jnp.bfloat16)
        dproj = (gate * cot_g.astype(jnp.float32)).astype(jnp.bfloat16)
        total = total + jnp.dot(attn.T, dproj, preferred_element_type=jnp.float32)
        dattn = jnp.dot(dproj, out_weight.T, preferred_element_type=jnp.float32).astype(jnp.bfloat16)
        dattn = lax.optimization_barrier(dattn)
        grad_q, grad_k, grad_v = back(dattn.astype(jnp.float32))
        return (total, (output, jnp.stack([grad_q, grad_k, grad_v], axis=1)))
    start = jnp.zeros((D, D), jnp.float32)
    total, (outputs, grads) = lax.scan(one_pack, start, (grouped, lat_groups, cot_groups, frames, timesteps))
    return (outputs.reshape(TOKENS, D), grads.reshape(TOKENS, 3, D), total)
```

```python
import jax
import jax.numpy as jnp
from jax import lax
from jax.experimental import pallas as pl
from jax.experimental.pallas import tpu as pltpu
from jax.sharding import PartitionSpec as P

HD = 128
FRAME = 64
LONG = 640
REST = 384
LOG2E = 1.4426950408889634
VMEM_LIMIT = 56 * 1024 * 1024

BF = jnp.bfloat16
F32 = jnp.float32


def dot_nt(a, b):
    return lax.dot_general(a, b, (((1,), (1,)), ((), ())), preferred_element_type=F32)


def dot_nn(a, b):
    return lax.dot_general(a, b, (((1,), (0,)), ((), ())), preferred_element_type=F32)


def dot_tn(a, b):
    return lax.dot_general(a, b, (((0,), (0,)), ((), ())), preferred_element_type=F32)


def clip_places(frames_ref):
    f0, f1, f2 = frames_ref[0, 0], frames_ref[0, 1], frames_ref[0, 2]
    first = jnp.logical_and(f0 > f1, f0 > f2)
    second = f1 > f2
    start = jnp.where(first, 0, jnp.where(second, f0, f0 + f1)) * FRAME
    lead = jnp.where(first, f1, f0)
    return start, lead


def gate_bins(frames_ref, steps_ref, seq_ref):
    f0, f1 = frames_ref[0, 0], frames_ref[0, 1]
    bins = []
    for k in range(2):
        frame = seq_ref[0] * 2 + k
        clip = jnp.where(frame >= f0, 1, 0) + jnp.where(frame >= f0 + f1, 1, 0)
        bins.append(steps_ref[0, clip])
    return bins


def spans(total):
    out, at = [], 0
    while at < total:
        size = min(256, total - at)
        out.append((at, size))
        at += size
    return out


def rest_places(start):
    return [
        pl.multiple_of(jnp.where(t * FRAME >= start, t * FRAME + LONG, t * FRAME), FRAME)
        for t in range(REST // FRAME)
    ]


def load_split(src, start):
    main = src[pl.ds(start, LONG), :]
    rest = jnp.concatenate([src[pl.ds(p, FRAME), :] for p in rest_places(start)], axis=0)
    return main, rest


def rest_mask(lead, at, size):
    rows = lax.broadcasted_iota(jnp.int32, (REST, size), 0)
    cols = lax.broadcasted_iota(jnp.int32, (REST, size), 1) + at
    edge = lead * FRAME
    return (rows < edge) == (cols < edge)


def fwd_kernel(frames_ref, qkv_ref, attn_ref, p1_ref, p2_ref, q_s, k_s, v_s):
    start, lead = clip_places(frames_ref)
    start = pl.multiple_of(start, FRAME)
    q_s[...] = qkv_ref[:, 0].reshape(1024, HD)
    k_s[...] = qkv_ref[:, 1].reshape(1024, HD)
    v_s[...] = qkv_ref[:, 2].reshape(1024, HD)
    factor = LOG2E / (HD**0.5)
    q1, q2 = load_split(q_s, start)
    k1, k2 = load_split(k_s, start)
    v1, v2 = load_split(v_s, start)
    places = rest_places(start)
    for long, (q, k, v, p_ref) in ((True, (q1, k1, v1, p1_ref)), (False, (q2, k2, v2, p2_ref))):
        vt = v.astype(F32).T.astype(BF)
        for at, size in spans(LONG if long else REST):
            s = dot_nt(k, q[at : at + size])
            if not long:
                s = jnp.where(rest_mask(lead, at, size), s, F32(-1e30))
            top = jnp.max(s, axis=0, keepdims=True)
            e = jnp.exp2((s - top) * F32(factor))
            total = jnp.sum(e, axis=0, keepdims=True)
            p = (e * (1.0 / total)).astype(BF)
            p_ref[0, :, at : at + size] = p
            o = dot_nn(vt, p).T.astype(BF)
            if long:
                attn_ref[pl.ds(start + at, size), :] = o
            else:
                for t in range(size // FRAME):
                    attn_ref[pl.ds(places[at // FRAME + t], FRAME), :] = o[
                        t * FRAME : (t + 1) * FRAME
                    ]


def attention_forward(frames, heads):
    return pl.pallas_call(
        fwd_kernel,
        out_shape=(
            jax.ShapeDtypeStruct((1024, 3 * HD), BF),
            jax.ShapeDtypeStruct((3, LONG, LONG), BF),
            jax.ShapeDtypeStruct((3, REST, REST), BF),
        ),
        grid_spec=pltpu.PrefetchScalarGridSpec(
            num_scalar_prefetch=1,
            grid=(3,),
            in_specs=[pl.BlockSpec((8, 3, 128, HD), lambda h, f: (0, 0, 0, h))],
            out_specs=(
                pl.BlockSpec((1024, HD), lambda h, f: (0, h)),
                pl.BlockSpec((1, LONG, LONG), lambda h, f: (h, 0, 0)),
                pl.BlockSpec((1, REST, REST), lambda h, f: (h, 0, 0)),
            ),
            scratch_shapes=[pltpu.VMEM((1024, HD), BF)] * 3,
        ),
        compiler_params=pltpu.CompilerParams(vmem_limit_bytes=VMEM_LIMIT),
        name="attention_forward",
    )(frames, heads)


def bwd_kernel(
    frames_ref, qkv_ref, own_ref, other_ref, p1_ref, p2_ref, out_ref, q_s, k_s, v_s, d_s, ds1, ds2, g_s
):
    start, lead = clip_places(frames_ref)
    start = pl.multiple_of(start, FRAME)
    q_s[...] = qkv_ref[:, 0].reshape(1024, HD)
    k_s[...] = qkv_ref[:, 1].reshape(1024, HD)
    v_s[...] = qkv_ref[:, 2].reshape(1024, HD)
    d_s[...] = (own_ref[...] + other_ref[...].astype(F32)).astype(BF)
    scale = 1.0 / (HD**0.5)
    q1, q2 = load_split(q_s, start)
    k1, k2 = load_split(k_s, start)
    v1, v2 = load_split(v_s, start)
    d1, d2 = load_split(d_s, start)
    places = rest_places(start)

    def put(which, long, value):
        if long:
            g_s[which, pl.ds(start, LONG), :] = value
        else:
            for t in range(REST // FRAME):
                g_s[which, pl.ds(places[t], FRAME), :] = value[t * FRAME : (t + 1) * FRAME]

    for long, (q, k, v, d, p_ref, ds_ref) in (
        (True, (q1, k1, v1, d1, p1_ref, ds1)),
        (False, (q2, k2, v2, d2, p2_ref, ds2)),
    ):
        kt = k.astype(F32).T.astype(BF)
        parts = []
        for at, size in spans(LONG if long else REST):
            dp = dot_nt(v, d[at : at + size]).astype(BF).astype(F32)
            p = p_ref[0, :, at : at + size].astype(F32)
            pd = p * dp
            delta = jnp.sum(pd, axis=0, keepdims=True)
            ds = ((pd - p * delta) * F32(scale)).astype(BF)
            ds_ref[:, at : at + size] = ds
            parts.append(dot_nn(kt, ds).T.astype(BF))
        put(0, long, jnp.concatenate(parts, axis=0))
        put(1, long, dot_nn(ds_ref[...], q).astype(BF))
        put(2, long, dot_nn(p_ref[0], d).astype(BF))
    for which in range(3):
        out_ref[:, which] = g_s[which].reshape(8, 128, HD)


def attention_backward(frames, heads, own, other, p1, p2):
    return pl.pallas_call(
        bwd_kernel,
        out_shape=jax.ShapeDtypeStruct((8, 3, 128, 3 * HD), BF),
        grid_spec=pltpu.PrefetchScalarGridSpec(
            num_scalar_prefetch=1,
            grid=(3,),
            in_specs=[
                pl.BlockSpec((8, 3, 128, HD), lambda h, f: (0, 0, 0, h)),
                pl.BlockSpec((1024, HD), lambda h, f: (0, h)),
                pl.BlockSpec((1024, HD), lambda h, f: (0, h)),
                pl.BlockSpec((1, LONG, LONG), lambda h, f: (h, 0, 0)),
                pl.BlockSpec((1, REST, REST), lambda h, f: (h, 0, 0)),
            ],
            out_specs=pl.BlockSpec((8, 3, 128, HD), lambda h, f: (0, 0, 0, h)),
            scratch_shapes=[pltpu.VMEM((1024, HD), BF)] * 4
            + [
                pltpu.VMEM((LONG, LONG), BF),
                pltpu.VMEM((REST, REST), BF),
                pltpu.VMEM((3, 1024, HD), BF),
            ],
        ),
        compiler_params=pltpu.CompilerParams(vmem_limit_bytes=VMEM_LIMIT),
        name="attention_backward",
    )(frames, heads, own, other, p1, p2)


def pack_kernel(in_ref, out_ref):
    out_ref[0] = in_ref[...]


def pack_heads(qkv):
    return pl.pallas_call(
        pack_kernel,
        out_shape=jax.ShapeDtypeStruct((8, 3, 128, 384), BF),
        grid=(8,),
        in_specs=[pl.BlockSpec((3, 128, 384), lambda j: (0, 0, j))],
        out_specs=pl.BlockSpec((1, 3, 128, 384), lambda j: (j, 0, 0, 0)),
        name="pack_heads",
    )(qkv)


def unpack_kernel(in_ref, out_ref):
    out_ref[...] = in_ref[0]


def unpack_heads(grads):
    return pl.pallas_call(
        unpack_kernel,
        out_shape=jax.ShapeDtypeStruct((3, 128, 3072), BF),
        grid=(8,),
        in_specs=[pl.BlockSpec((1, 3, 128, 384), lambda j: (j, 0, 0, 0))],
        out_specs=pl.BlockSpec((3, 128, 384), lambda j: (0, 0, j)),
        name="unpack_heads",
    )(grads)


def gated_kernel(frames_ref, steps_ref, seq_ref, table_ref, cot_ref, out_ref):
    b0, b1 = gate_bins(frames_ref, steps_ref, seq_ref)
    for k, b in enumerate((b0, b1)):
        rows = slice(k * FRAME, (k + 1) * FRAME)
        out_ref[0, rows, :] = (table_ref[pl.ds(b, 1), :] * cot_ref[rows, :].astype(F32)).astype(BF)


def gated_cotangent(frames, steps, seq, table, cotangent):
    return pl.pallas_call(
        gated_kernel,
        out_shape=jax.ShapeDtypeStruct((8, 128, 1536), BF),
        grid_spec=pltpu.PrefetchScalarGridSpec(
            num_scalar_prefetch=3,
            grid=(2, 4),
            in_specs=[
                pl.BlockSpec((64, 1536), lambda z, x, *_: (0, z)),
                pl.BlockSpec((128, 1536), lambda z, x, *_: (0, z)),
            ],
            out_specs=pl.BlockSpec((1, 128, 1536), lambda z, x, *_: (2 * x + z, 0, 0)),
        ),
        name="gated_cotangent",
    )(frames, steps, seq, table, cotangent)


def output_kernel(frames_ref, steps_ref, seq_ref, table_ref, lat_ref, part_ref, out_ref):
    b0, b1 = gate_bins(frames_ref, steps_ref, seq_ref)
    for k, b in enumerate((b0, b1)):
        rows = slice(k * FRAME, (k + 1) * FRAME)
        proj = part_ref[0, 0, rows, :].astype(F32)
        for x in range(1, 4):
            proj = proj + part_ref[x, 0, rows, :].astype(F32)
        out = lat_ref[rows, :].astype(F32) + table_ref[pl.ds(b, 1), :] * proj
        out_ref[rows, :] = out.astype(BF)


def gated_output(frames, steps, seq, table, latents, parts):
    return pl.pallas_call(
        output_kernel,
        out_shape=jax.ShapeDtypeStruct((128, 3072), BF),
        grid_spec=pltpu.PrefetchScalarGridSpec(
            num_scalar_prefetch=3,
            grid=(2, 2),
            in_specs=[
                pl.BlockSpec((64, 768), lambda z, n, *_: (0, 2 * z + n)),
                pl.BlockSpec((128, 768), lambda z, n, *_: (0, 2 * z + n)),
                pl.BlockSpec((4, 1, 128, 768), lambda z, n, *_: (0, z, 0, n)),
            ],
            out_specs=pl.BlockSpec((128, 768), lambda z, n, *_: (0, 2 * z + n)),
        ),
        name="gated_output",
    )(frames, steps, seq, table, latents, parts.reshape(4, 2, 128, 1536))


def dattn_kernel(d_ref, w_ref, out_ref):
    out_ref[...] = dot_nn(d_ref[...], w_ref[0]).astype(out_ref.dtype)


def dattn_part(dproj, weights, which, dtype):
    return pl.pallas_call(
        dattn_kernel,
        out_shape=jax.ShapeDtypeStruct((1024, 384), dtype),
        grid=(4,),
        in_specs=[
            pl.BlockSpec((256, 1536), lambda m: (m, 0)),
            pl.BlockSpec((1, 1536, 384), lambda m: (which, 0, 0)),
        ],
        out_specs=pl.BlockSpec((256, 384), lambda m: (m, 0)),
        name="dattn_part",
    )(dproj, weights)


def weave_kernel(core_ref, mine_ref, theirs_ref, out_ref):
    even = core_ref[0] == 0
    mine, theirs = mine_ref[...], theirs_ref[...]
    out_ref[:, 0] = jnp.where(even, mine, theirs)
    out_ref[:, 1] = jnp.where(even, theirs, mine)


def weave(core, mine, theirs):
    return pl.pallas_call(
        weave_kernel,
        out_shape=jax.ShapeDtypeStruct((16, 2, 96, 384), BF),
        grid_spec=pltpu.PrefetchScalarGridSpec(
            num_scalar_prefetch=1,
            grid=(4,),
            in_specs=[pl.BlockSpec((4, 96, 384), lambda n, c: (n, 0, 0))] * 2,
            out_specs=pl.BlockSpec((4, 2, 96, 384), lambda n, c: (n, 0, 0, 0)),
        ),
        name="weave",
    )(core, mine, theirs)


def proj_kernel(a0_ref, a1_ref, w_ref, out_ref):
    out_ref[...] = (dot_nt(a0_ref[...], w_ref[0]) + dot_nt(a1_ref[...], w_ref[1])).astype(BF)


def proj_part(own, other, weights):
    return pl.pallas_call(
        proj_kernel,
        out_shape=jax.ShapeDtypeStruct((1024, 1536), BF),
        grid=(4,),
        in_specs=[
            pl.BlockSpec((256, 384), lambda m: (m, 0)),
            pl.BlockSpec((256, 384), lambda m: (m, 0)),
            pl.BlockSpec((2, 1536, 384), lambda m: (0, 0, 0)),
        ],
        out_specs=pl.BlockSpec((256, 1536), lambda m: (m, 0)),
        compiler_params=pltpu.CompilerParams(vmem_limit_bytes=VMEM_LIMIT),
        name="proj_part",
    )(own, other, weights)


def dweight_kernel(core_ref, d_ref, a0_ref, a1_ref, keep_ref, send_ref):
    d = d_ref[...]
    even = core_ref[0] == 0
    for z, a_ref in enumerate((a0_ref, a1_ref)):
        g = dot_tn(d, a_ref[...]).astype(BF)
        for i in range(2):
            p0, p1 = g[i * 192 : i * 192 + 96], g[i * 192 + 96 : i * 192 + 192]
            keep_ref[z, i] = jnp.where(even, p0, p1)
            send_ref[z, i] = jnp.where(even, p1, p0)


def dweight_part(core, dproj, own, other):
    pieces = jax.ShapeDtypeStruct((2, 8, 96, 384), BF)
    return pl.pallas_call(
        dweight_kernel,
        out_shape=(pieces, pieces),
        grid_spec=pltpu.PrefetchScalarGridSpec(
            num_scalar_prefetch=1,
            grid=(4,),
            in_specs=[
                pl.BlockSpec((1024, 384), lambda n, c: (0, n)),
                pl.BlockSpec((1024, 384), lambda n, c: (0, 0)),
                pl.BlockSpec((1024, 384), lambda n, c: (0, 0)),
            ],
            out_specs=(
                pl.BlockSpec((2, 2, 96, 384), lambda n, c: (0, n, 0, 0)),
                pl.BlockSpec((2, 2, 96, 384), lambda n, c: (0, n, 0, 0)),
            ),
        ),
        compiler_params=pltpu.CompilerParams(vmem_limit_bytes=VMEM_LIMIT),
        name="dweight_part",
    )(core, dproj, own, other)


def piece_moves(dp_count, seq_count):
    half = dp_count // 2
    moves = []
    for dp in range(dp_count):
        for seq in range(seq_count):
            top, z = dp // half, seq % 2
            to_dp = (dp % half) + half * (z ^ top)
            to_seq = seq - z + top
            moves.append((dp * seq_count + seq, to_dp * seq_count + to_seq))
    return moves


def body(qkv_input, latents, cotangent, out_weight, gate_table, timesteps, frames):
    dp_count, seq_count = lax.axis_size("dp"), lax.axis_size("seq")
    seq = lax.axis_index("seq").astype(jnp.int32).reshape(1)
    both = ("dp", "seq")
    moves = piece_moves(dp_count, seq_count)
    swap = [(i, i ^ 1) for i in range(seq_count)]

    core = (lax.axis_index("dp") % 2).astype(jnp.int32).reshape(1)
    cores = [(i, i ^ 1) for i in range(dp_count)]
    same_core = [list(range(c, dp_count, 2)) for c in range(2)]

    piece = lax.ppermute(out_weight.T, both, moves)
    packed = pack_heads(qkv_input.transpose(1, 0, 2))
    packed, piece = lax.optimization_barrier((packed, piece))
    mine = lax.all_gather(piece, "dp", axis=0, axis_index_groups=same_core, tiled=False)
    heads = lax.all_to_all(packed, "seq", split_axis=0, concat_axis=0, tiled=True)

    gated = gated_cotangent(frames, timesteps, seq, gate_table, cotangent)
    gated, heads, mine = lax.optimization_barrier((gated, heads, mine))
    theirs = lax.ppermute(mine, "dp", cores)
    dproj = lax.all_to_all(gated, "seq", split_axis=0, concat_axis=0, tiled=True)
    dproj = dproj.reshape(1024, 1536)

    attn, p1, p2 = attention_forward(frames, heads)
    attn_other = lax.ppermute(attn, "seq", swap)
    weights = weave(core, mine, theirs).reshape(2, 1536, 384)

    part = proj_part(attn, attn_other, weights)
    parts = lax.all_to_all(
        part.reshape(8, 128, 1536), "seq", split_axis=0, concat_axis=0, tiled=True
    )
    dproj, part = lax.optimization_barrier((dproj, part))

    d_send = dattn_part(dproj, weights, 1, BF)
    d_recv = lax.ppermute(d_send, "seq", swap)
    d_own = dattn_part(dproj, weights, 0, F32)

    keep, send = dweight_part(core, dproj, attn, attn_other)
    got = lax.ppermute(send, "dp", cores)
    pair = (keep.astype(F32) + got.astype(F32)).astype(BF).reshape(16 * 96, 384)
    total = lax.psum_scatter(
        pair, "dp", scatter_dimension=0, axis_index_groups=same_core, tiled=True
    )

    grads = attention_backward(frames, heads, d_own, d_recv, p1, p2)
    grads = lax.all_to_all(grads, "seq", split_axis=0, concat_axis=0, tiled=True)

    output = gated_output(frames, timesteps, seq, gate_table, latents, parts)
    total = lax.ppermute(total, both, [(b, a) for a, b in moves])
    grad_weight = total.astype(F32).T
    grad_qkv = unpack_heads(grads).transpose(1, 0, 2)
    return (output, grad_qkv, grad_weight)


def solution(mesh):
    placed = (
        P(("dp", "seq"), None, None),
        P(("dp", "seq"), None),
        P(("dp", "seq"), None),
        P("seq", "dp"),
        P(),
        P("dp", None),
        P("dp", None),
    )
    return jax.shard_map(
        body,
        mesh=mesh,
        in_specs=placed,
        out_specs=(P(("dp", "seq"), None), P(("dp", "seq"), None, None), P("seq", "dp")),
        check_vma=False,
    )
```

```python
import jax
import jax.numpy as jnp
from jax import lax
from jax.experimental import pallas as pl
from jax.experimental.pallas import tpu as pltpu
from jax.sharding import PartitionSpec as P

HD = 128
FRAME = 64
LONG = 640
REST = 384
LOG2E = 1.4426950408889634
VMEM_LIMIT = 56 * 1024 * 1024

BF = jnp.bfloat16
F32 = jnp.float32


def dot_nt(a, b):
    return lax.dot_general(a, b, (((1,), (1,)), ((), ())), preferred_element_type=F32)


def dot_nn(a, b):
    return lax.dot_general(a, b, (((1,), (0,)), ((), ())), preferred_element_type=F32)


def dot_tn(a, b):
    return lax.dot_general(a, b, (((0,), (0,)), ((), ())), preferred_element_type=F32)


def clip_places(frames_ref):
    f0, f1, f2 = frames_ref[0, 0], frames_ref[0, 1], frames_ref[0, 2]
    first = jnp.logical_and(f0 > f1, f0 > f2)
    second = f1 > f2
    start = jnp.where(first, 0, jnp.where(second, f0, f0 + f1)) * FRAME
    lead = jnp.where(first, f1, f0)
    return start, lead


def gate_bins(frames_ref, steps_ref, seq_ref):
    f0, f1 = frames_ref[0, 0], frames_ref[0, 1]
    bins = []
    for k in range(2):
        frame = seq_ref[0] * 2 + k
        clip = jnp.where(frame >= f0, 1, 0) + jnp.where(frame >= f0 + f1, 1, 0)
        bins.append(steps_ref[0, clip])
    return bins


def spans(total):
    out, at = [], 0
    while at < total:
        size = min(256, total - at)
        out.append((at, size))
        at += size
    return out


def rest_places(start):
    return [
        pl.multiple_of(jnp.where(t * FRAME >= start, t * FRAME + LONG, t * FRAME), FRAME)
        for t in range(REST // FRAME)
    ]


def load_split(src, start):
    main = src[pl.ds(start, LONG), :]
    rest = jnp.concatenate([src[pl.ds(p, FRAME), :] for p in rest_places(start)], axis=0)
    return main, rest


def rest_mask(lead, at, size):
    rows = lax.broadcasted_iota(jnp.int32, (REST, size), 0)
    cols = lax.broadcasted_iota(jnp.int32, (REST, size), 1) + at
    edge = lead * FRAME
    return (rows < edge) == (cols < edge)


def fwd_kernel(frames_ref, qkv_ref, attn_ref, p1_ref, p2_ref, q_s, k_s, v_s):
    start, lead = clip_places(frames_ref)
    start = pl.multiple_of(start, FRAME)
    q_s[...] = qkv_ref[:, 0].reshape(1024, HD)
    k_s[...] = qkv_ref[:, 1].reshape(1024, HD)
    v_s[...] = qkv_ref[:, 2].reshape(1024, HD)
    factor = LOG2E / (HD**0.5)
    q1, q2 = load_split(q_s, start)
    k1, k2 = load_split(k_s, start)
    v1, v2 = load_split(v_s, start)
    places = rest_places(start)
    for long, (q, k, v, p_ref) in ((True, (q1, k1, v1, p1_ref)), (False, (q2, k2, v2, p2_ref))):
        vt = v.astype(F32).T.astype(BF)
        for at, size in spans(LONG if long else REST):
            s = dot_nt(k, q[at : at + size])
            if not long:
                s = jnp.where(rest_mask(lead, at, size), s, F32(-1e30))
            top = jnp.max(s, axis=0, keepdims=True)
            e = jnp.exp2((s - top) * F32(factor))
            total = jnp.sum(e, axis=0, keepdims=True)
            p = (e * (1.0 / total)).astype(BF)
            p_ref[0, :, at : at + size] = p
            o = dot_nn(vt, p).T.astype(BF)
            if long:
                attn_ref[pl.ds(start + at, size), :] = o
            else:
                for t in range(size // FRAME):
                    attn_ref[pl.ds(places[at // FRAME + t], FRAME), :] = o[
                        t * FRAME : (t + 1) * FRAME
                    ]


def attention_forward(frames, heads):
    return pl.pallas_call(
        fwd_kernel,
        out_shape=(
            jax.ShapeDtypeStruct((1024, 3 * HD), BF),
            jax.ShapeDtypeStruct((3, LONG, LONG), BF),
            jax.ShapeDtypeStruct((3, REST, REST), BF),
        ),
        grid_spec=pltpu.PrefetchScalarGridSpec(
            num_scalar_prefetch=1,
            grid=(3,),
            in_specs=[pl.BlockSpec((8, 3, 128, HD), lambda h, f: (0, 0, 0, h))],
            out_specs=(
                pl.BlockSpec((1024, HD), lambda h, f: (0, h)),
                pl.BlockSpec((1, LONG, LONG), lambda h, f: (h, 0, 0)),
                pl.BlockSpec((1, REST, REST), lambda h, f: (h, 0, 0)),
            ),
            scratch_shapes=[pltpu.VMEM((1024, HD), BF)] * 3,
        ),
        compiler_params=pltpu.CompilerParams(vmem_limit_bytes=VMEM_LIMIT),
        name="attention_forward",
    )(frames, heads)


def bwd_kernel(
    frames_ref, qkv_ref, own_ref, other_ref, p1_ref, p2_ref, out_ref, q_s, k_s, v_s, d_s, ds1, ds2, g_s
):
    start, lead = clip_places(frames_ref)
    start = pl.multiple_of(start, FRAME)
    q_s[...] = qkv_ref[:, 0].reshape(1024, HD)
    k_s[...] = qkv_ref[:, 1].reshape(1024, HD)
    v_s[...] = qkv_ref[:, 2].reshape(1024, HD)
    d_s[...] = (own_ref[...] + other_ref[...].astype(F32)).astype(BF)
    scale = 1.0 / (HD**0.5)
    q1, q2 = load_split(q_s, start)
    k1, k2 = load_split(k_s, start)
    v1, v2 = load_split(v_s, start)
    d1, d2 = load_split(d_s, start)
    places = rest_places(start)

    def put(which, long, value):
        if long:
            g_s[which, pl.ds(start, LONG), :] = value
        else:
            for t in range(REST // FRAME):
                g_s[which, pl.ds(places[t], FRAME), :] = value[t * FRAME : (t + 1) * FRAME]

    for long, (q, k, v, d, p_ref, ds_ref) in (
        (True, (q1, k1, v1, d1, p1_ref, ds1)),
        (False, (q2, k2, v2, d2, p2_ref, ds2)),
    ):
        kt = k.astype(F32).T.astype(BF)
        parts = []
        for at, size in spans(LONG if long else REST):
            dp = dot_nt(v, d[at : at + size]).astype(BF).astype(F32)
            p = p_ref[0, :, at : at + size].astype(F32)
            pd = p * dp
            delta = jnp.sum(pd, axis=0, keepdims=True)
            ds = ((pd - p * delta) * F32(scale)).astype(BF)
            ds_ref[:, at : at + size] = ds
            parts.append(dot_nn(kt, ds).T.astype(BF))
        put(0, long, jnp.concatenate(parts, axis=0))
        put(1, long, dot_nn(ds_ref[...], q).astype(BF))
        put(2, long, dot_nn(p_ref[0], d).astype(BF))
    for which in range(3):
        out_ref[:, which] = g_s[which].reshape(8, 128, HD)


def attention_backward(frames, heads, own, other, p1, p2):
    return pl.pallas_call(
        bwd_kernel,
        out_shape=jax.ShapeDtypeStruct((8, 3, 128, 3 * HD), BF),
        grid_spec=pltpu.PrefetchScalarGridSpec(
            num_scalar_prefetch=1,
            grid=(3,),
            in_specs=[
                pl.BlockSpec((8, 3, 128, HD), lambda h, f: (0, 0, 0, h)),
                pl.BlockSpec((1024, HD), lambda h, f: (0, h)),
                pl.BlockSpec((1024, HD), lambda h, f: (0, h)),
                pl.BlockSpec((1, LONG, LONG), lambda h, f: (h, 0, 0)),
                pl.BlockSpec((1, REST, REST), lambda h, f: (h, 0, 0)),
            ],
            out_specs=pl.BlockSpec((8, 3, 128, HD), lambda h, f: (0, 0, 0, h)),
            scratch_shapes=[pltpu.VMEM((1024, HD), BF)] * 4
            + [
                pltpu.VMEM((LONG, LONG), BF),
                pltpu.VMEM((REST, REST), BF),
                pltpu.VMEM((3, 1024, HD), BF),
            ],
        ),
        compiler_params=pltpu.CompilerParams(vmem_limit_bytes=VMEM_LIMIT),
        name="attention_backward",
    )(frames, heads, own, other, p1, p2)


def pack_kernel(in_ref, out_ref):
    out_ref[0] = in_ref[...]


def pack_heads(qkv):
    return pl.pallas_call(
        pack_kernel,
        out_shape=jax.ShapeDtypeStruct((8, 3, 128, 384), BF),
        grid=(8,),
        in_specs=[pl.BlockSpec((3, 128, 384), lambda j: (0, 0, j))],
        out_specs=pl.BlockSpec((1, 3, 128, 384), lambda j: (j, 0, 0, 0)),
        name="pack_heads",
    )(qkv)


def unpack_kernel(in_ref, out_ref):
    out_ref[...] = in_ref[0]


def unpack_heads(grads):
    return pl.pallas_call(
        unpack_kernel,
        out_shape=jax.ShapeDtypeStruct((3, 128, 3072), BF),
        grid=(8,),
        in_specs=[pl.BlockSpec((1, 3, 128, 384), lambda j: (j, 0, 0, 0))],
        out_specs=pl.BlockSpec((3, 128, 384), lambda j: (0, 0, j)),
        name="unpack_heads",
    )(grads)


def gated_kernel(frames_ref, steps_ref, seq_ref, t0_ref, t1_ref, c0_ref, c1_ref, keep_ref, send_ref):
    bins = gate_bins(frames_ref, steps_ref, seq_ref)
    for table_ref, cot_ref, out_ref in ((t0_ref, c0_ref, keep_ref), (t1_ref, c1_ref, send_ref)):
        for k, b in enumerate(bins):
            rows = slice(k * FRAME, (k + 1) * FRAME)
            out_ref[rows, :] = (table_ref[pl.ds(b, 1), :] * cot_ref[rows, :].astype(F32)).astype(BF)


def gated_cotangent(frames, steps, seq, table, cotangent):
    def half(rows, flip):
        return pl.BlockSpec((rows, 768), lambda n, f, t, s: (0, 2 * (s[0] % 2 ^ flip) + n))

    out = pl.BlockSpec((128, 768), lambda n, *_: (0, n))
    return pl.pallas_call(
        gated_kernel,
        out_shape=(jax.ShapeDtypeStruct((128, 1536), BF),) * 2,
        grid_spec=pltpu.PrefetchScalarGridSpec(
            num_scalar_prefetch=3,
            grid=(2,),
            in_specs=[half(64, 0), half(64, 1), half(128, 0), half(128, 1)],
            out_specs=(out, out),
        ),
        name="gated_cotangent",
    )(frames, steps, seq, table, table, cotangent, cotangent)


def assemble_kernel(seq_ref, *refs):
    blocks, out_ref, sems = refs[:8], refs[8], refs[9]
    x, z = seq_ref[0] // 2, seq_ref[0] % 2
    copies = []
    for i, block in enumerate(blocks):
        place = 2 * ((x + i // 2) % 4) + (z ^ (i % 2))
        copies.append(pltpu.make_async_copy(block, out_ref.at[place], sems.at[i]))
        copies[-1].start()
    for copy in copies:
        copy.wait()


def assemble(seq, blocks):
    return pl.pallas_call(
        assemble_kernel,
        out_shape=jax.ShapeDtypeStruct((8, 128, 1536), BF),
        in_specs=[pl.BlockSpec(memory_space=pltpu.SMEM)] + [pl.BlockSpec(memory_space=pl.ANY)] * 8,
        out_specs=pl.BlockSpec(memory_space=pl.ANY),
        scratch_shapes=[pltpu.SemaphoreType.DMA((8,))],
        name="assemble",
    )(seq, *blocks)


def output_kernel(
    frames_ref, steps_ref, seq_ref, t0_ref, t1_ref, l0_ref, l1_ref, own_ref, other_ref, out_ref
):
    bins = gate_bins(frames_ref, steps_ref, seq_ref)
    z = seq_ref[0] % 2
    halves = ((z, t0_ref, l0_ref, own_ref), (1 - z, t1_ref, l1_ref, other_ref))
    for place, table_ref, lat_ref, proj_ref in halves:
        at = pl.multiple_of(place * 1536, 1536)
        for k, b in enumerate(bins):
            rows = slice(k * FRAME, (k + 1) * FRAME)
            proj = proj_ref[rows, :].astype(F32)
            out = lat_ref[rows, :].astype(F32) + table_ref[pl.ds(b, 1), :] * proj
            out_ref[rows, pl.ds(at, 1536)] = out.astype(BF)


def gated_output(frames, steps, seq, table, latents, own, other):
    def half(rows, flip):
        return pl.BlockSpec((rows, 1536), lambda n, f, t, s: (0, s[0] % 2 ^ flip))

    whole = pl.BlockSpec((128, 1536), lambda n, *_: (0, 0))
    return pl.pallas_call(
        output_kernel,
        out_shape=jax.ShapeDtypeStruct((128, 3072), BF),
        grid_spec=pltpu.PrefetchScalarGridSpec(
            num_scalar_prefetch=3,
            grid=(1,),
            in_specs=[half(64, 0), half(64, 1), half(128, 0), half(128, 1), whole, whole],
            out_specs=pl.BlockSpec((128, 3072), lambda n, *_: (0, 0)),
        ),
        name="gated_output",
    )(frames, steps, seq, table, table, latents, latents, own, other)


def dattn_kernel(d_ref, w_ref, out_ref):
    out_ref[...] = dot_nn(d_ref[...], w_ref[0]).astype(out_ref.dtype)


def dattn_part(dproj, weights, which, dtype):
    return pl.pallas_call(
        dattn_kernel,
        out_shape=jax.ShapeDtypeStruct((1024, 384), dtype),
        grid=(2,),
        in_specs=[
            pl.BlockSpec((512, 1536), lambda m: (m, 0)),
            pl.BlockSpec((1, 1536, 384), lambda m: (which, 0, 0)),
        ],
        out_specs=pl.BlockSpec((512, 384), lambda m: (m, 0)),
        compiler_params=pltpu.CompilerParams(vmem_limit_bytes=VMEM_LIMIT),
        name="dattn_part",
    )(dproj, weights)


def weave_kernel(dp_ref, *refs):
    out_ref = refs[8]
    y, zh, core = dp_ref[0] // 8, dp_ref[0] // 2 % 4, dp_ref[0] % 2
    for flip in range(2):
        for k in range(4):
            for m in range(4):
                place = 4 * ((y + k) % 4) + (zh + m) % 4
                out_ref[place, core ^ flip] = refs[4 * flip + k][m]


def weave(dp, mine, theirs):
    return pl.pallas_call(
        weave_kernel,
        out_shape=jax.ShapeDtypeStruct((16, 2, 96, 384), BF),
        in_specs=[pl.BlockSpec(memory_space=pltpu.SMEM)]
        + [pl.BlockSpec((4, 96, 384), lambda: (0, 0, 0))] * 8,
        out_specs=pl.BlockSpec((16, 2, 96, 384), lambda: (0, 0, 0, 0)),
        name="weave",
    )(dp, *mine, *theirs)


def stack_kernel(*refs):
    for i, ref in enumerate(refs[:-1]):
        refs[-1][i] = ref[...]


def stack_pieces(pieces):
    return pl.pallas_call(
        stack_kernel, out_shape=jax.ShapeDtypeStruct((4, 96, 384), BF), name="stack_pieces"
    )(*pieces)


def rows_spec(k):
    return pl.BlockSpec((256, 384), lambda n, s: ((s[0] // 2 + k) % 4, 0))


W_SPEC = pl.BlockSpec((2, 512, 384), lambda n, s: (0, n, 0))
TWO_SPEC = pl.BlockSpec((256, 512), lambda n, s: (0, n))
ONE_SPEC = pl.BlockSpec((128, 512), lambda n, s: (0, n))
ONE_BF = jax.ShapeDtypeStruct((128, 1536), BF)
TWO_BF = jax.ShapeDtypeStruct((256, 1536), BF)


def project(own_ref, other_ref, w_ref):
    return dot_nt(own_ref[...], w_ref[0]) + dot_nt(other_ref[...], w_ref[1])


def far_kernel(seq_ref, a_ref, b_ref, w_ref, up_ref, down_ref):
    part = project(a_ref, b_ref, w_ref).astype(BF)
    up_ref[...] = part[:128]
    down_ref[...] = part[128:]


def near_kernel(seq_ref, a1_ref, b1_ref, a3_ref, b3_ref, w_ref, up_ref, down_ref, t1_ref, t3_ref):
    p1 = project(a1_ref, b1_ref, w_ref)
    t1_ref[:128] = (p1[:128] + up_ref[...].astype(F32)).astype(BF)
    t1_ref[128:] = p1[128:].astype(BF)
    p3 = project(a3_ref, b3_ref, w_ref)
    t3_ref[:128] = p3[:128].astype(BF)
    t3_ref[128:] = (p3[128:] + down_ref[...].astype(F32)).astype(BF)


def home_kernel(seq_ref, a_ref, b_ref, w_ref, c1_ref, c3_ref, keep_ref, send_ref):
    part = project(a_ref, b_ref, w_ref)
    part = part + c1_ref[...].astype(F32) + c3_ref[...].astype(F32)
    first = seq_ref[0] % 2 == 0
    keep_ref[...] = jnp.where(first, part[:128], part[128:])
    send_ref[...] = jnp.where(first, part[128:], part[:128]).astype(BF)


def project_call(kernel, name, in_specs, out_shape, out_specs):
    return pl.pallas_call(
        kernel,
        out_shape=out_shape,
        grid_spec=pltpu.PrefetchScalarGridSpec(
            num_scalar_prefetch=1, grid=(3,), in_specs=in_specs, out_specs=out_specs
        ),
        compiler_params=pltpu.CompilerParams(vmem_limit_bytes=VMEM_LIMIT),
        name=name,
    )


def project_far(seq, own, other, weights):
    return project_call(
        far_kernel,
        "project_far",
        [rows_spec(2), rows_spec(2), W_SPEC],
        (ONE_BF, ONE_BF),
        (ONE_SPEC, ONE_SPEC),
    )(seq, own, other, weights)


def project_near(seq, own, other, weights, up, down):
    return project_call(
        near_kernel,
        "project_near",
        [rows_spec(1), rows_spec(1), rows_spec(3), rows_spec(3), W_SPEC, ONE_SPEC, ONE_SPEC],
        (TWO_BF, TWO_BF),
        (TWO_SPEC, TWO_SPEC),
    )(seq, own, other, own, other, weights, up, down)


def project_home(seq, own, other, weights, c1, c3):
    return project_call(
        home_kernel,
        "project_home",
        [rows_spec(0), rows_spec(0), W_SPEC, TWO_SPEC, TWO_SPEC],
        (jax.ShapeDtypeStruct((128, 1536), F32), ONE_BF),
        (ONE_SPEC, ONE_SPEC),
    )(seq, own, other, weights, c1, c3)


def dweight_kernel(core_ref, d_ref, a0_ref, a1_ref, keep_ref, send_ref):
    d = d_ref[...]
    even = core_ref[0] % 2 == 0
    for z, a_ref in enumerate((a0_ref, a1_ref)):
        g = dot_tn(d, a_ref[...]).astype(BF)
        for i in range(2):
            p0, p1 = g[i * 192 : i * 192 + 96], g[i * 192 + 96 : i * 192 + 192]
            keep_ref[z, i] = jnp.where(even, p0, p1)
            send_ref[z, i] = jnp.where(even, p1, p0)


def dweight_part(core, dproj, own, other):
    pieces = jax.ShapeDtypeStruct((2, 8, 96, 384), BF)
    return pl.pallas_call(
        dweight_kernel,
        out_shape=(pieces, pieces),
        grid_spec=pltpu.PrefetchScalarGridSpec(
            num_scalar_prefetch=1,
            grid=(4,),
            in_specs=[
                pl.BlockSpec((1024, 384), lambda n, c: (0, n)),
                pl.BlockSpec((1024, 384), lambda n, c: (0, 0)),
                pl.BlockSpec((1024, 384), lambda n, c: (0, 0)),
            ],
            out_specs=(
                pl.BlockSpec((2, 2, 96, 384), lambda n, c: (0, n, 0, 0)),
                pl.BlockSpec((2, 2, 96, 384), lambda n, c: (0, n, 0, 0)),
            ),
        ),
        compiler_params=pltpu.CompilerParams(vmem_limit_bytes=VMEM_LIMIT),
        name="dweight_part",
    )(core, dproj, own, other)


def pair_kernel(dp_ref, keep_ref, got_ref, *out_refs):
    y = dp_ref[0] // 8
    for k, out_ref in enumerate(out_refs):
        at = (y + k) % 4
        out_ref[...] = (keep_ref[at].astype(F32) + got_ref[at].astype(F32)).astype(BF)


def pair_sum(dp, keep, got):
    return pl.pallas_call(
        pair_kernel,
        out_shape=(jax.ShapeDtypeStruct((4, 96, 384), BF),) * 4,
        in_specs=[pl.BlockSpec(memory_space=pltpu.SMEM)]
        + [pl.BlockSpec((4, 4, 96, 384), lambda: (0, 0, 0, 0))] * 2,
        out_specs=(pl.BlockSpec((4, 96, 384), lambda: (0, 0, 0)),) * 4,
        name="pair_sum",
    )(dp, keep.reshape(4, 4, 96, 384), got.reshape(4, 4, 96, 384))


def ring_kernel(dp_ref, a_ref, b_ref, c_ref, d_ref, *out_refs):
    zh = dp_ref[0] // 2 % 4
    for k, out_ref in enumerate(out_refs):
        at = (zh + k) % 4
        total = a_ref[at].astype(F32) + b_ref[at].astype(F32)
        out_ref[...] = (total + c_ref[at].astype(F32) + d_ref[at].astype(F32)).astype(BF)


def ring_sum(dp, parts):
    return pl.pallas_call(
        ring_kernel,
        out_shape=(jax.ShapeDtypeStruct((96, 384), BF),) * 4,
        in_specs=[pl.BlockSpec(memory_space=pltpu.SMEM)]
        + [pl.BlockSpec((4, 96, 384), lambda: (0, 0, 0))] * 4,
        out_specs=(pl.BlockSpec((96, 384), lambda: (0, 0)),) * 4,
        name="ring_sum",
    )(dp, *parts)


def piece_moves(dp_count, seq_count):
    half = dp_count // 2
    moves = []
    for dp in range(dp_count):
        for seq in range(seq_count):
            top, z = dp // half, seq % 2
            to_dp = (dp % half) + half * (z ^ top)
            to_seq = seq - z + top
            moves.append((dp * seq_count + seq, to_dp * seq_count + to_seq))
    return moves


def along(x, axis, stride, places):
    size = lax.axis_size(axis)
    moves = []
    for i in range(size):
        at = i // stride % 4
        moves.append((i, i + ((at + places) % 4 - at) * stride))
    return lax.ppermute(x, axis, moves)


def along_x(x, places):
    return along(x, "seq", 2, places)


def along_y(x, places):
    return along(x, "dp", 8, places)


def along_z(x, places):
    return along(x, "dp", 2, places)


def swap_z(x):
    return lax.ppermute(x, "seq", [(i, i ^ 1) for i in range(lax.axis_size("seq"))])


def swap_core(x):
    return lax.ppermute(x, "dp", [(i, i ^ 1) for i in range(lax.axis_size("dp"))])


def body(qkv_input, latents, cotangent, out_weight, gate_table, timesteps, frames):
    seq = lax.axis_index("seq").astype(jnp.int32).reshape(1)
    dp = lax.axis_index("dp").astype(jnp.int32).reshape(1)
    both = ("dp", "seq")
    moves = piece_moves(lax.axis_size("dp"), lax.axis_size("seq"))

    piece = lax.ppermute(out_weight.T, both, moves)
    keep, send = gated_cotangent(frames, timesteps, seq, gate_table, cotangent)
    packed = pack_heads(qkv_input.transpose(1, 0, 2))
    packed, piece, keep, send = lax.optimization_barrier((packed, piece, keep, send))
    heads = lax.all_to_all(packed, "seq", split_axis=0, concat_axis=0, tiled=True)
    got = swap_z(send)

    pieces = stack_pieces([piece] + [along_z(piece, -k) for k in range(1, 4)])
    mine = [pieces] + [along_y(pieces, -k) for k in range(1, 4)]
    heads, keep, got, mine = lax.optimization_barrier((heads, keep, got, mine))

    b1 = [along_x(keep, -1), along_x(got, -1)]
    b3 = [along_x(keep, 1), along_x(got, 1)]
    b2 = [along_x(b3[0], 1), along_x(b1[1], -1)]
    theirs = [swap_core(p) for p in mine]
    attn, p1, p2 = attention_forward(frames, heads)
    attn_other = swap_z(attn)
    weights = weave(dp, mine, theirs).reshape(2, 1536, 384)
    dproj = assemble(seq, [keep, got, *b1, *b2, *b3]).reshape(1024, 1536)

    d_recv = swap_z(dattn_part(dproj, weights, 1, BF))
    up, down = project_far(seq, attn, attn_other, weights)
    up, down = along_x(up, 1), along_x(down, -1)
    d_own = dattn_part(dproj, weights, 0, F32)
    w_keep, w_send = dweight_part(dp, dproj, attn, attn_other)
    w_got = swap_core(w_send)
    t1, t3 = project_near(seq, attn, attn_other, weights, up, down)
    d_own, d_recv, t1, t3, w_got = lax.optimization_barrier((d_own, d_recv, t1, t3, w_got))
    c1, c3 = along_x(t1, 1), along_x(t3, -1)
    terms = pair_sum(dp, w_keep, w_got)
    terms = [terms[0]] + [along_y(terms[k], k) for k in range(1, 4)]

    grads = attention_backward(frames, heads, d_own, d_recv, p1, p2)
    grads = lax.all_to_all(grads, "seq", split_axis=0, concat_axis=0, tiled=True)

    o_keep, o_send = project_home(seq, attn, attn_other, weights, c1, c3)
    o_got = swap_z(o_send)
    output = gated_output(frames, timesteps, seq, gate_table, latents, o_keep, o_got)

    terms = ring_sum(dp, terms)
    terms = [terms[0]] + [along_z(terms[k], k) for k in range(1, 4)]
    total = terms[0].astype(F32) + terms[1].astype(F32)
    total = total + terms[2].astype(F32) + terms[3].astype(F32)
    total = lax.ppermute(total, both, [(b, a) for a, b in moves])
    grad_weight = total.T
    grad_qkv = unpack_heads(grads).transpose(1, 0, 2)
    return (output, grad_qkv, grad_weight)


def solution(mesh):
    placed = (
        P(("dp", "seq"), None, None),
        P(("dp", "seq"), None),
        P(("dp", "seq"), None),
        P("seq", "dp"),
        P(),
        P("dp", None),
        P("dp", None),
    )
    return jax.shard_map(
        body,
        mesh=mesh,
        in_specs=placed,
        out_specs=(P(("dp", "seq"), None), P(("dp", "seq"), None, None), P("seq", "dp")),
        check_vma=False,
    )
```

```python
import jax
import jax.numpy as jnp
from jax import lax
from jax.experimental import pallas as pl
from jax.experimental.pallas import tpu as pltpu
from jax.sharding import PartitionSpec as P

HD = 128
FRAME = 64
LONG = 640
REST = 384
LOG2E = 1.4426950408889634
VMEM_LIMIT = 56 * 1024 * 1024

BF = jnp.bfloat16
F32 = jnp.float32


def dot_nt(a, b):
    return lax.dot_general(a, b, (((1,), (1,)), ((), ())), preferred_element_type=F32)


def dot_nn(a, b):
    return lax.dot_general(a, b, (((1,), (0,)), ((), ())), preferred_element_type=F32)


def dot_tn(a, b):
    return lax.dot_general(a, b, (((0,), (0,)), ((), ())), preferred_element_type=F32)


def clip_places(frames_ref):
    f0, f1, f2 = frames_ref[0, 0], frames_ref[0, 1], frames_ref[0, 2]
    first = jnp.logical_and(f0 > f1, f0 > f2)
    second = f1 > f2
    start = jnp.where(first, 0, jnp.where(second, f0, f0 + f1)) * FRAME
    lead = jnp.where(first, f1, f0)
    return start, lead


def gate_bins(frames_ref, steps_ref, seq_ref):
    f0, f1 = frames_ref[0, 0], frames_ref[0, 1]
    bins = []
    for k in range(2):
        frame = seq_ref[0] * 2 + k
        clip = jnp.where(frame >= f0, 1, 0) + jnp.where(frame >= f0 + f1, 1, 0)
        bins.append(steps_ref[0, clip])
    return bins


def spans(total):
    out, at = [], 0
    while at < total:
        size = min(256, total - at)
        out.append((at, size))
        at += size
    return out


def rest_places(start):
    return [
        pl.multiple_of(jnp.where(t * FRAME >= start, t * FRAME + LONG, t * FRAME), FRAME)
        for t in range(REST // FRAME)
    ]


def load_split(src, start):
    main = src[pl.ds(start, LONG), :]
    rest = jnp.concatenate([src[pl.ds(p, FRAME), :] for p in rest_places(start)], axis=0)
    return main, rest


def rest_mask(lead, at, size):
    rows = lax.broadcasted_iota(jnp.int32, (REST, size), 0)
    cols = lax.broadcasted_iota(jnp.int32, (REST, size), 1) + at
    edge = lead * FRAME
    return (rows < edge) == (cols < edge)


def fwd_kernel(frames_ref, qkv_ref, attn_ref, p1_ref, p2_ref, q_s, k_s, v_s):
    start, lead = clip_places(frames_ref)
    start = pl.multiple_of(start, FRAME)
    q_s[...] = qkv_ref[:, 0].reshape(1024, HD)
    k_s[...] = qkv_ref[:, 1].reshape(1024, HD)
    v_s[...] = qkv_ref[:, 2].reshape(1024, HD)
    factor = LOG2E / (HD**0.5)
    q1, q2 = load_split(q_s, start)
    k1, k2 = load_split(k_s, start)
    v1, v2 = load_split(v_s, start)
    places = rest_places(start)
    for long, (q, k, v, p_ref) in ((True, (q1, k1, v1, p1_ref)), (False, (q2, k2, v2, p2_ref))):
        vt = v.astype(F32).T.astype(BF)
        for at, size in spans(LONG if long else REST):
            s = dot_nt(k, q[at : at + size])
            if not long:
                s = jnp.where(rest_mask(lead, at, size), s, F32(-1e30))
            top = jnp.max(s, axis=0, keepdims=True)
            e = jnp.exp2((s - top) * F32(factor))
            total = jnp.sum(e, axis=0, keepdims=True)
            p = (e * (1.0 / total)).astype(BF)
            p_ref[0, :, at : at + size] = p
            o = dot_nn(vt, p).T.astype(BF)
            if long:
                attn_ref[pl.ds(start + at, size), :] = o
            else:
                for t in range(size // FRAME):
                    attn_ref[pl.ds(places[at // FRAME + t], FRAME), :] = o[
                        t * FRAME : (t + 1) * FRAME
                    ]


def attention_forward(frames, heads):
    return pl.pallas_call(
        fwd_kernel,
        out_shape=(
            jax.ShapeDtypeStruct((1024, 3 * HD), BF),
            jax.ShapeDtypeStruct((3, LONG, LONG), BF),
            jax.ShapeDtypeStruct((3, REST, REST), BF),
        ),
        grid_spec=pltpu.PrefetchScalarGridSpec(
            num_scalar_prefetch=1,
            grid=(3,),
            in_specs=[pl.BlockSpec((8, 3, 128, HD), lambda h, f: (0, 0, 0, h))],
            out_specs=(
                pl.BlockSpec((1024, HD), lambda h, f: (0, h)),
                pl.BlockSpec((1, LONG, LONG), lambda h, f: (h, 0, 0)),
                pl.BlockSpec((1, REST, REST), lambda h, f: (h, 0, 0)),
            ),
            scratch_shapes=[pltpu.VMEM((1024, HD), BF)] * 3,
        ),
        compiler_params=pltpu.CompilerParams(vmem_limit_bytes=VMEM_LIMIT),
        name="attention_forward",
    )(frames, heads)


def bwd_kernel(
    frames_ref, qkv_ref, own_ref, other_ref, p1_ref, p2_ref, out_ref, q_s, k_s, v_s, d_s, ds1, ds2, g_s
):
    start, lead = clip_places(frames_ref)
    start = pl.multiple_of(start, FRAME)
    q_s[...] = qkv_ref[:, 0].reshape(1024, HD)
    k_s[...] = qkv_ref[:, 1].reshape(1024, HD)
    v_s[...] = qkv_ref[:, 2].reshape(1024, HD)
    d_s[...] = (own_ref[...] + other_ref[...].astype(F32)).astype(BF)
    scale = 1.0 / (HD**0.5)
    q1, q2 = load_split(q_s, start)
    k1, k2 = load_split(k_s, start)
    v1, v2 = load_split(v_s, start)
    d1, d2 = load_split(d_s, start)
    places = rest_places(start)

    def put(which, long, value):
        if long:
            g_s[which, pl.ds(start, LONG), :] = value
        else:
            for t in range(REST // FRAME):
                g_s[which, pl.ds(places[t], FRAME), :] = value[t * FRAME : (t + 1) * FRAME]

    for long, (q, k, v, d, p_ref, ds_ref) in (
        (True, (q1, k1, v1, d1, p1_ref, ds1)),
        (False, (q2, k2, v2, d2, p2_ref, ds2)),
    ):
        kt = k.astype(F32).T.astype(BF)
        parts = []
        for at, size in spans(LONG if long else REST):
            dp = dot_nt(v, d[at : at + size]).astype(BF).astype(F32)
            p = p_ref[0, :, at : at + size].astype(F32)
            pd = p * dp
            delta = jnp.sum(pd, axis=0, keepdims=True)
            ds = ((pd - p * delta) * F32(scale)).astype(BF)
            ds_ref[:, at : at + size] = ds
            parts.append(dot_nn(kt, ds).T.astype(BF))
        put(0, long, jnp.concatenate(parts, axis=0))
        put(1, long, dot_nn(ds_ref[...], q).astype(BF))
        put(2, long, dot_nn(p_ref[0], d).astype(BF))
    for which in range(3):
        out_ref[:, which] = g_s[which].reshape(8, 128, HD)


def attention_backward(frames, heads, own, other, p1, p2):
    return pl.pallas_call(
        bwd_kernel,
        out_shape=jax.ShapeDtypeStruct((8, 3, 128, 3 * HD), BF),
        grid_spec=pltpu.PrefetchScalarGridSpec(
            num_scalar_prefetch=1,
            grid=(3,),
            in_specs=[
                pl.BlockSpec((8, 3, 128, HD), lambda h, f: (0, 0, 0, h)),
                pl.BlockSpec((1024, HD), lambda h, f: (0, h)),
                pl.BlockSpec((1024, HD), lambda h, f: (0, h)),
                pl.BlockSpec((1, LONG, LONG), lambda h, f: (h, 0, 0)),
                pl.BlockSpec((1, REST, REST), lambda h, f: (h, 0, 0)),
            ],
            out_specs=pl.BlockSpec((8, 3, 128, HD), lambda h, f: (0, 0, 0, h)),
            scratch_shapes=[pltpu.VMEM((1024, HD), BF)] * 4
            + [
                pltpu.VMEM((LONG, LONG), BF),
                pltpu.VMEM((REST, REST), BF),
                pltpu.VMEM((3, 1024, HD), BF),
            ],
        ),
        compiler_params=pltpu.CompilerParams(vmem_limit_bytes=VMEM_LIMIT),
        name="attention_backward",
    )(frames, heads, own, other, p1, p2)


def pack_kernel(in_ref, out_ref):
    out_ref[0] = in_ref[...]


def pack_heads(qkv):
    return pl.pallas_call(
        pack_kernel,
        out_shape=jax.ShapeDtypeStruct((8, 3, 128, 384), BF),
        grid=(8,),
        in_specs=[pl.BlockSpec((3, 128, 384), lambda j: (0, 0, j))],
        out_specs=pl.BlockSpec((1, 3, 128, 384), lambda j: (j, 0, 0, 0)),
        name="pack_heads",
    )(qkv)


def unpack_kernel(in_ref, out_ref):
    out_ref[...] = in_ref[0]


def unpack_heads(grads):
    return pl.pallas_call(
        unpack_kernel,
        out_shape=jax.ShapeDtypeStruct((3, 128, 3072), BF),
        grid=(8,),
        in_specs=[pl.BlockSpec((1, 3, 128, 384), lambda j: (j, 0, 0, 0))],
        out_specs=pl.BlockSpec((3, 128, 384), lambda j: (0, 0, j)),
        name="unpack_heads",
    )(grads)


def gated_kernel(frames_ref, steps_ref, seq_ref, t0_ref, t1_ref, c0_ref, c1_ref, keep_ref, send_ref):
    bins = gate_bins(frames_ref, steps_ref, seq_ref)
    for table_ref, cot_ref, out_ref in ((t0_ref, c0_ref, keep_ref), (t1_ref, c1_ref, send_ref)):
        for k, b in enumerate(bins):
            rows = slice(k * FRAME, (k + 1) * FRAME)
            out_ref[rows, :] = (table_ref[pl.ds(b, 1), :] * cot_ref[rows, :].astype(F32)).astype(BF)


def gated_cotangent(frames, steps, seq, table, cotangent):
    def half(rows, flip):
        return pl.BlockSpec((rows, 768), lambda n, f, t, s: (0, 2 * (s[0] % 2 ^ flip) + n))

    out = pl.BlockSpec((128, 768), lambda n, *_: (0, n))
    return pl.pallas_call(
        gated_kernel,
        out_shape=(jax.ShapeDtypeStruct((128, 1536), BF),) * 2,
        grid_spec=pltpu.PrefetchScalarGridSpec(
            num_scalar_prefetch=3,
            grid=(2,),
            in_specs=[half(64, 0), half(64, 1), half(128, 0), half(128, 1)],
            out_specs=(out, out),
        ),
        name="gated_cotangent",
    )(frames, steps, seq, table, table, cotangent, cotangent)


def output_kernel(
    frames_ref, steps_ref, seq_ref, t0_ref, t1_ref, l0_ref, l1_ref, own_ref, other_ref, out_ref
):
    bins = gate_bins(frames_ref, steps_ref, seq_ref)
    z = seq_ref[0] % 2
    halves = ((z, t0_ref, l0_ref, own_ref), (1 - z, t1_ref, l1_ref, other_ref))
    for place, table_ref, lat_ref, proj_ref in halves:
        at = pl.multiple_of(place * 1536, 1536)
        for k, b in enumerate(bins):
            rows = slice(k * FRAME, (k + 1) * FRAME)
            proj = proj_ref[rows, :].astype(F32)
            out = lat_ref[rows, :].astype(F32) + table_ref[pl.ds(b, 1), :] * proj
            out_ref[rows, pl.ds(at, 1536)] = out.astype(BF)


def gated_output(frames, steps, seq, table, latents, own, other):
    def half(rows, flip):
        return pl.BlockSpec((rows, 1536), lambda n, f, t, s: (0, s[0] % 2 ^ flip))

    whole = pl.BlockSpec((128, 1536), lambda n, *_: (0, 0))
    return pl.pallas_call(
        output_kernel,
        out_shape=jax.ShapeDtypeStruct((128, 3072), BF),
        grid_spec=pltpu.PrefetchScalarGridSpec(
            num_scalar_prefetch=3,
            grid=(1,),
            in_specs=[half(64, 0), half(64, 1), half(128, 0), half(128, 1), whole, whole],
            out_specs=pl.BlockSpec((128, 3072), lambda n, *_: (0, 0)),
        ),
        name="gated_output",
    )(frames, steps, seq, table, table, latents, latents, own, other)


def dattn_kernel(seq_ref, *refs):
    blocks, (w_ref, dproj_ref, other_ref, own_ref) = refs[:8], refs[8:]
    x, z = seq_ref[0] // 2, seq_ref[0] % 2
    for i, block in enumerate(blocks):
        place = 2 * ((x + i // 2) % 4) + (z ^ (i % 2))
        dproj_ref[pl.ds(pl.multiple_of(place * 128, 128), 128), :] = block[...]
    for m in range(2):
        rows = slice(m * 512, (m + 1) * 512)
        d = dproj_ref[rows, :]
        other_ref[rows, :] = dot_nn(d, w_ref[1]).astype(BF)
        own_ref[rows, :] = dot_nn(d, w_ref[0])


def dattn_parts(seq, blocks, weights):
    vmem = pl.BlockSpec(memory_space=pltpu.VMEM)
    return pl.pallas_call(
        dattn_kernel,
        out_shape=(
            jax.ShapeDtypeStruct((1024, 1536), BF),
            jax.ShapeDtypeStruct((1024, 384), BF),
            jax.ShapeDtypeStruct((1024, 384), F32),
        ),
        in_specs=[pl.BlockSpec(memory_space=pltpu.SMEM)] + [vmem] * 9,
        out_specs=(
            pl.BlockSpec((1024, 1536), lambda: (0, 0)),
            pl.BlockSpec((1024, 384), lambda: (0, 0)),
            pl.BlockSpec((1024, 384), lambda: (0, 0)),
        ),
        compiler_params=pltpu.CompilerParams(vmem_limit_bytes=VMEM_LIMIT),
        name="dattn_parts",
    )(seq, *blocks, weights)


def rows_spec(k):
    return pl.BlockSpec((256, 384), lambda n, s: ((s[0] // 2 + k) % 4, 0))


W_SPEC = pl.BlockSpec((2, 512, 384), lambda n, s: (0, n, 0))
TWO_SPEC = pl.BlockSpec((256, 512), lambda n, s: (0, n))
ONE_SPEC = pl.BlockSpec((128, 512), lambda n, s: (0, n))
ONE_BF = jax.ShapeDtypeStruct((128, 1536), BF)
TWO_BF = jax.ShapeDtypeStruct((256, 1536), BF)


def project(own_ref, other_ref, w_ref):
    return dot_nt(own_ref[...], w_ref[0]) + dot_nt(other_ref[...], w_ref[1])


def far_kernel(seq_ref, a_ref, b_ref, w_ref, up_ref, down_ref):
    part = project(a_ref, b_ref, w_ref).astype(BF)
    up_ref[...] = part[:128]
    down_ref[...] = part[128:]


def near_kernel(seq_ref, a1_ref, b1_ref, a3_ref, b3_ref, w_ref, up_ref, down_ref, t1_ref, t3_ref):
    p1 = project(a1_ref, b1_ref, w_ref)
    t1_ref[:128] = (p1[:128] + up_ref[...].astype(F32)).astype(BF)
    t1_ref[128:] = p1[128:].astype(BF)
    p3 = project(a3_ref, b3_ref, w_ref)
    t3_ref[:128] = p3[:128].astype(BF)
    t3_ref[128:] = (p3[128:] + down_ref[...].astype(F32)).astype(BF)


def home_kernel(seq_ref, a_ref, b_ref, w_ref, c1_ref, c3_ref, keep_ref, send_ref):
    part = project(a_ref, b_ref, w_ref)
    part = part + c1_ref[...].astype(F32) + c3_ref[...].astype(F32)
    first = seq_ref[0] % 2 == 0
    keep_ref[...] = jnp.where(first, part[:128], part[128:])
    send_ref[...] = jnp.where(first, part[128:], part[:128]).astype(BF)


def project_call(kernel, name, in_specs, out_shape, out_specs):
    return pl.pallas_call(
        kernel,
        out_shape=out_shape,
        grid_spec=pltpu.PrefetchScalarGridSpec(
            num_scalar_prefetch=1, grid=(3,), in_specs=in_specs, out_specs=out_specs
        ),
        compiler_params=pltpu.CompilerParams(vmem_limit_bytes=VMEM_LIMIT),
        name=name,
    )


def project_far(seq, own, other, weights):
    return project_call(
        far_kernel,
        "project_far",
        [rows_spec(2), rows_spec(2), W_SPEC],
        (ONE_BF, ONE_BF),
        (ONE_SPEC, ONE_SPEC),
    )(seq, own, other, weights)


def project_near(seq, own, other, weights, up, down):
    return project_call(
        near_kernel,
        "project_near",
        [rows_spec(1), rows_spec(1), rows_spec(3), rows_spec(3), W_SPEC, ONE_SPEC, ONE_SPEC],
        (TWO_BF, TWO_BF),
        (TWO_SPEC, TWO_SPEC),
    )(seq, own, other, own, other, weights, up, down)


def project_home(seq, own, other, weights, c1, c3):
    return project_call(
        home_kernel,
        "project_home",
        [rows_spec(0), rows_spec(0), W_SPEC, TWO_SPEC, TWO_SPEC],
        (jax.ShapeDtypeStruct((128, 1536), F32), ONE_BF),
        (ONE_SPEC, ONE_SPEC),
    )(seq, own, other, weights, c1, c3)


def dweight_kernel(core_ref, d_ref, a0_ref, a1_ref, keep_ref, send_ref):
    d = d_ref[...]
    even = core_ref[0] % 2 == 0
    for z, a_ref in enumerate((a0_ref, a1_ref)):
        g = dot_tn(d, a_ref[...]).astype(BF)
        for i in range(2):
            p0, p1 = g[i * 192 : i * 192 + 96], g[i * 192 + 96 : i * 192 + 192]
            keep_ref[z, i] = jnp.where(even, p0, p1)
            send_ref[z, i] = jnp.where(even, p1, p0)


def dweight_part(core, dproj, own, other):
    pieces = jax.ShapeDtypeStruct((2, 8, 96, 384), BF)
    return pl.pallas_call(
        dweight_kernel,
        out_shape=(pieces, pieces),
        grid_spec=pltpu.PrefetchScalarGridSpec(
            num_scalar_prefetch=1,
            grid=(4,),
            in_specs=[
                pl.BlockSpec((1024, 384), lambda n, c: (0, n)),
                pl.BlockSpec((1024, 384), lambda n, c: (0, 0)),
                pl.BlockSpec((1024, 384), lambda n, c: (0, 0)),
            ],
            out_specs=(
                pl.BlockSpec((2, 2, 96, 384), lambda n, c: (0, n, 0, 0)),
                pl.BlockSpec((2, 2, 96, 384), lambda n, c: (0, n, 0, 0)),
            ),
        ),
        compiler_params=pltpu.CompilerParams(vmem_limit_bytes=VMEM_LIMIT),
        name="dweight_part",
    )(core, dproj, own, other)


def pair_kernel(dp_ref, keep_ref, got_ref, *out_refs):
    y = dp_ref[0] // 8
    for k, out_ref in enumerate(out_refs):
        at = (y + k) % 4
        out_ref[...] = (keep_ref[at].astype(F32) + got_ref[at].astype(F32)).astype(BF)


def pair_sum(dp, keep, got):
    return pl.pallas_call(
        pair_kernel,
        out_shape=(jax.ShapeDtypeStruct((4, 96, 384), BF),) * 4,
        in_specs=[pl.BlockSpec(memory_space=pltpu.SMEM)]
        + [pl.BlockSpec((4, 4, 96, 384), lambda: (0, 0, 0, 0))] * 2,
        out_specs=(pl.BlockSpec((4, 96, 384), lambda: (0, 0, 0)),) * 4,
        name="pair_sum",
    )(dp, keep.reshape(4, 4, 96, 384), got.reshape(4, 4, 96, 384))


def ring_kernel(dp_ref, a_ref, b_ref, c_ref, d_ref, *out_refs):
    zh = dp_ref[0] // 2 % 4
    for k, out_ref in enumerate(out_refs):
        at = (zh + k) % 4
        total = a_ref[at].astype(F32) + b_ref[at].astype(F32)
        out_ref[...] = (total + c_ref[at].astype(F32) + d_ref[at].astype(F32)).astype(BF)


def ring_sum(dp, parts):
    return pl.pallas_call(
        ring_kernel,
        out_shape=(jax.ShapeDtypeStruct((96, 384), BF),) * 4,
        in_specs=[pl.BlockSpec(memory_space=pltpu.SMEM)]
        + [pl.BlockSpec((4, 96, 384), lambda: (0, 0, 0))] * 4,
        out_specs=(pl.BlockSpec((96, 384), lambda: (0, 0)),) * 4,
        name="ring_sum",
    )(dp, *parts)


def piece_moves(dp_count, seq_count):
    half = dp_count // 2
    moves = []
    for dp in range(dp_count):
        for seq in range(seq_count):
            top, z = dp // half, seq % 2
            to_dp = (dp % half) + half * (z ^ top)
            to_seq = seq - z + top
            moves.append((dp * seq_count + seq, to_dp * seq_count + to_seq))
    return moves


def along(x, axis, stride, places):
    size = lax.axis_size(axis)
    moves = []
    for i in range(size):
        at = i // stride % 4
        moves.append((i, i + ((at + places) % 4 - at) * stride))
    return lax.ppermute(x, axis, moves)


def along_x(x, places):
    return along(x, "seq", 2, places)


def along_y(x, places):
    return along(x, "dp", 8, places)


def along_z(x, places):
    return along(x, "dp", 2, places)


def swap_z(x):
    return lax.ppermute(x, "seq", [(i, i ^ 1) for i in range(lax.axis_size("seq"))])


def swap_core(x):
    return lax.ppermute(x, "dp", [(i, i ^ 1) for i in range(lax.axis_size("dp"))])


def body(qkv_input, latents, cotangent, out_weight, gate_table, timesteps, frames):
    seq = lax.axis_index("seq").astype(jnp.int32).reshape(1)
    dp = lax.axis_index("dp").astype(jnp.int32).reshape(1)
    both = ("dp", "seq")
    moves = piece_moves(lax.axis_size("dp"), lax.axis_size("seq"))

    piece = lax.ppermute(out_weight.T, both, moves)
    packed = pack_heads(qkv_input.transpose(1, 0, 2))
    packed, piece = lax.optimization_barrier((packed, piece))
    weights = lax.all_gather(piece, "dp", axis=0, tiled=True).reshape(2, 1536, 384)
    heads = lax.all_to_all(packed, "seq", split_axis=0, concat_axis=0, tiled=True)

    keep, send = gated_cotangent(frames, timesteps, seq, gate_table, cotangent)
    got = swap_z(send)
    b1 = [along_x(keep, -1), along_x(got, -1)]
    b3 = [along_x(keep, 1), along_x(got, 1)]
    b2 = [along_x(b3[0], 1), along_x(b1[1], -1)]

    heads, weights = lax.optimization_barrier((heads, weights))
    attn, p1, p2 = attention_forward(frames, heads)
    attn_other = swap_z(attn)
    dproj, d_send, d_own = dattn_parts(seq, [keep, got, *b1, *b2, *b3], weights)
    d_recv = swap_z(d_send)
    up, down = project_far(seq, attn, attn_other, weights)
    up, down = along_x(up, 1), along_x(down, -1)
    w_keep, w_send = dweight_part(dp, dproj, attn, attn_other)
    w_got = swap_core(w_send)
    t1, t3 = project_near(seq, attn, attn_other, weights, up, down)
    d_own, d_recv, t1, t3, w_got = lax.optimization_barrier((d_own, d_recv, t1, t3, w_got))
    c1, c3 = along_x(t1, 1), along_x(t3, -1)
    terms = pair_sum(dp, w_keep, w_got)
    terms = [terms[0]] + [along_y(terms[k], k) for k in range(1, 4)]

    grads = attention_backward(frames, heads, d_own, d_recv, p1, p2)
    grads = lax.all_to_all(grads, "seq", split_axis=0, concat_axis=0, tiled=True)

    o_keep, o_send = project_home(seq, attn, attn_other, weights, c1, c3)
    o_got = swap_z(o_send)
    output = gated_output(frames, timesteps, seq, gate_table, latents, o_keep, o_got)

    terms = ring_sum(dp, terms)
    terms = [terms[0]] + [along_z(terms[k], k) for k in range(1, 4)]
    total = terms[0].astype(F32) + terms[1].astype(F32)
    total = total + terms[2].astype(F32) + terms[3].astype(F32)
    total = lax.ppermute(total, both, [(b, a) for a, b in moves])
    grad_weight = total.T
    grad_qkv = unpack_heads(grads).transpose(1, 0, 2)
    return (output, grad_qkv, grad_weight)


def solution(mesh):
    placed = (
        P(("dp", "seq"), None, None),
        P(("dp", "seq"), None),
        P(("dp", "seq"), None),
        P("seq", "dp"),
        P(),
        P("dp", None),
        P("dp", None),
    )
    return jax.shard_map(
        body,
        mesh=mesh,
        in_specs=placed,
        out_specs=(P(("dp", "seq"), None), P(("dp", "seq"), None, None), P("seq", "dp")),
        check_vma=False,
    )
```

```python
import jax
import jax.numpy as jnp
from jax import lax
from jax.experimental import pallas as pl
from jax.experimental.pallas import tpu as pltpu
from jax.sharding import PartitionSpec as P

HD = 128
FRAME = 64
LONG = 640
REST = 384
LOG2E = 1.4426950408889634
VMEM_LIMIT = 56 * 1024 * 1024

BF = jnp.bfloat16
F32 = jnp.float32


def cost(us):
    return pl.CostEstimate(flops=int(us * 1e9), transcendentals=0, bytes_accessed=int(us * 3e6))


def dot_nt(a, b):
    return lax.dot_general(a, b, (((1,), (1,)), ((), ())), preferred_element_type=F32)


def dot_nn(a, b):
    return lax.dot_general(a, b, (((1,), (0,)), ((), ())), preferred_element_type=F32)


def dot_tn(a, b):
    return lax.dot_general(a, b, (((0,), (0,)), ((), ())), preferred_element_type=F32)


def clip_places(frames_ref):
    f0, f1, f2 = frames_ref[0, 0], frames_ref[0, 1], frames_ref[0, 2]
    first = jnp.logical_and(f0 > f1, f0 > f2)
    second = f1 > f2
    start = jnp.where(first, 0, jnp.where(second, f0, f0 + f1)) * FRAME
    lead = jnp.where(first, f1, f0)
    return start, lead


def gate_bins(frames_ref, steps_ref, seq_ref):
    f0, f1 = frames_ref[0, 0], frames_ref[0, 1]
    bins = []
    for k in range(2):
        frame = seq_ref[0] * 2 + k
        clip = jnp.where(frame >= f0, 1, 0) + jnp.where(frame >= f0 + f1, 1, 0)
        bins.append(steps_ref[0, clip])
    return bins


def spans(total):
    out, at = [], 0
    while at < total:
        size = min(256, total - at)
        out.append((at, size))
        at += size
    return out


def rest_places(start):
    return [
        pl.multiple_of(jnp.where(t * FRAME >= start, t * FRAME + LONG, t * FRAME), FRAME)
        for t in range(REST // FRAME)
    ]


def load_split(src, start):
    main = src[pl.ds(start, LONG), :]
    rest = jnp.concatenate([src[pl.ds(p, FRAME), :] for p in rest_places(start)], axis=0)
    return main, rest


def rest_mask(lead, at, size):
    rows = lax.broadcasted_iota(jnp.int32, (REST, size), 0)
    cols = lax.broadcasted_iota(jnp.int32, (REST, size), 1) + at
    edge = lead * FRAME
    return (rows < edge) == (cols < edge)


def fwd_kernel(frames_ref, qkv_ref, attn_ref, p1_ref, p2_ref, q_s, k_s, v_s):
    start, lead = clip_places(frames_ref)
    start = pl.multiple_of(start, FRAME)
    q_s[...] = qkv_ref[:, 0].reshape(1024, HD)
    k_s[...] = qkv_ref[:, 1].reshape(1024, HD)
    v_s[...] = qkv_ref[:, 2].reshape(1024, HD)
    factor = LOG2E / (HD**0.5)
    q1, q2 = load_split(q_s, start)
    k1, k2 = load_split(k_s, start)
    v1, v2 = load_split(v_s, start)
    places = rest_places(start)
    for long, (q, k, v, p_ref) in ((True, (q1, k1, v1, p1_ref)), (False, (q2, k2, v2, p2_ref))):
        vt = v.astype(F32).T.astype(BF)
        for at, size in spans(LONG if long else REST):
            s = dot_nt(k, q[at : at + size])
            if not long:
                s = jnp.where(rest_mask(lead, at, size), s, F32(-1e30))
            top = jnp.max(s, axis=0, keepdims=True)
            e = jnp.exp2((s - top) * F32(factor))
            total = jnp.sum(e, axis=0, keepdims=True)
            p = (e * (1.0 / total)).astype(BF)
            p_ref[0, :, at : at + size] = p
            o = dot_nn(vt, p).T.astype(BF)
            if long:
                attn_ref[pl.ds(start + at, size), :] = o
            else:
                for t in range(size // FRAME):
                    attn_ref[pl.ds(places[at // FRAME + t], FRAME), :] = o[
                        t * FRAME : (t + 1) * FRAME
                    ]


def attention_forward(frames, heads):
    return pl.pallas_call(
        fwd_kernel,
        out_shape=(
            jax.ShapeDtypeStruct((1024, 3 * HD), BF),
            jax.ShapeDtypeStruct((3, LONG, LONG), BF),
            jax.ShapeDtypeStruct((3, REST, REST), BF),
        ),
        grid_spec=pltpu.PrefetchScalarGridSpec(
            num_scalar_prefetch=1,
            grid=(3,),
            in_specs=[pl.BlockSpec((8, 3, 128, HD), lambda h, f: (0, 0, 0, h))],
            out_specs=(
                pl.BlockSpec((1024, HD), lambda h, f: (0, h)),
                pl.BlockSpec((1, LONG, LONG), lambda h, f: (h, 0, 0)),
                pl.BlockSpec((1, REST, REST), lambda h, f: (h, 0, 0)),
            ),
            scratch_shapes=[pltpu.VMEM((1024, HD), BF)] * 3,
        ),
        compiler_params=pltpu.CompilerParams(vmem_limit_bytes=VMEM_LIMIT),
        cost_estimate=cost(10),
        name="attention_forward",
    )(frames, heads)


def bwd_kernel(
    frames_ref, qkv_ref, own_ref, other_ref, p1_ref, p2_ref, out_ref, q_s, k_s, v_s, d_s, ds1, ds2, g_s
):
    start, lead = clip_places(frames_ref)
    start = pl.multiple_of(start, FRAME)
    q_s[...] = qkv_ref[:, 0].reshape(1024, HD)
    k_s[...] = qkv_ref[:, 1].reshape(1024, HD)
    v_s[...] = qkv_ref[:, 2].reshape(1024, HD)
    d_s[...] = (own_ref[...] + other_ref[...].astype(F32)).astype(BF)
    scale = 1.0 / (HD**0.5)
    q1, q2 = load_split(q_s, start)
    k1, k2 = load_split(k_s, start)
    v1, v2 = load_split(v_s, start)
    d1, d2 = load_split(d_s, start)
    places = rest_places(start)

    def put(which, long, value):
        if long:
            g_s[which, pl.ds(start, LONG), :] = value
        else:
            for t in range(REST // FRAME):
                g_s[which, pl.ds(places[t], FRAME), :] = value[t * FRAME : (t + 1) * FRAME]

    for long, (q, k, v, d, p_ref, ds_ref) in (
        (True, (q1, k1, v1, d1, p1_ref, ds1)),
        (False, (q2, k2, v2, d2, p2_ref, ds2)),
    ):
        kt = k.astype(F32).T.astype(BF)
        parts = []
        for at, size in spans(LONG if long else REST):
            dp = dot_nt(v, d[at : at + size]).astype(BF).astype(F32)
            p = p_ref[0, :, at : at + size].astype(F32)
            pd = p * dp
            delta = jnp.sum(pd, axis=0, keepdims=True)
            ds = ((pd - p * delta) * F32(scale)).astype(BF)
            ds_ref[:, at : at + size] = ds
            parts.append(dot_nn(kt, ds).T.astype(BF))
        put(0, long, jnp.concatenate(parts, axis=0))
        put(1, long, dot_nn(ds_ref[...], q).astype(BF))
        put(2, long, dot_nn(p_ref[0], d).astype(BF))
    for which in range(3):
        out_ref[:, which] = g_s[which].reshape(8, 128, HD)


def attention_backward(frames, heads, own, other, p1, p2):
    return pl.pallas_call(
        bwd_kernel,
        out_shape=jax.ShapeDtypeStruct((8, 3, 128, 3 * HD), BF),
        grid_spec=pltpu.PrefetchScalarGridSpec(
            num_scalar_prefetch=1,
            grid=(3,),
            in_specs=[
                pl.BlockSpec((8, 3, 128, HD), lambda h, f: (0, 0, 0, h)),
                pl.BlockSpec((1024, HD), lambda h, f: (0, h)),
                pl.BlockSpec((1024, HD), lambda h, f: (0, h)),
                pl.BlockSpec((1, LONG, LONG), lambda h, f: (h, 0, 0)),
                pl.BlockSpec((1, REST, REST), lambda h, f: (h, 0, 0)),
            ],
            out_specs=pl.BlockSpec((8, 3, 128, HD), lambda h, f: (0, 0, 0, h)),
            scratch_shapes=[pltpu.VMEM((1024, HD), BF)] * 4
            + [
                pltpu.VMEM((LONG, LONG), BF),
                pltpu.VMEM((REST, REST), BF),
                pltpu.VMEM((3, 1024, HD), BF),
            ],
        ),
        compiler_params=pltpu.CompilerParams(vmem_limit_bytes=VMEM_LIMIT),
        cost_estimate=cost(11),
        name="attention_backward",
    )(frames, heads, own, other, p1, p2)


def pack_kernel(in_ref, out_ref):
    out_ref[0] = in_ref[...]


def pack_heads(qkv):
    return pl.pallas_call(
        pack_kernel,
        out_shape=jax.ShapeDtypeStruct((8, 3, 128, 384), BF),
        grid=(8,),
        in_specs=[pl.BlockSpec((3, 128, 384), lambda j: (0, 0, j))],
        out_specs=pl.BlockSpec((1, 3, 128, 384), lambda j: (j, 0, 0, 0)),
        cost_estimate=cost(6),
        name="pack_heads",
    )(qkv)


def unpack_kernel(in_ref, out_ref):
    out_ref[...] = in_ref[0]


def unpack_heads(grads):
    return pl.pallas_call(
        unpack_kernel,
        out_shape=jax.ShapeDtypeStruct((3, 128, 3072), BF),
        grid=(8,),
        in_specs=[pl.BlockSpec((1, 3, 128, 384), lambda j: (j, 0, 0, 0))],
        out_specs=pl.BlockSpec((3, 128, 384), lambda j: (0, 0, j)),
        cost_estimate=cost(6),
        name="unpack_heads",
    )(grads)


def gated_kernel(frames_ref, steps_ref, seq_ref, t0_ref, t1_ref, c0_ref, c1_ref, keep_ref, send_ref):
    bins = gate_bins(frames_ref, steps_ref, seq_ref)
    for table_ref, cot_ref, out_ref in ((t0_ref, c0_ref, keep_ref), (t1_ref, c1_ref, send_ref)):
        for k, b in enumerate(bins):
            rows = slice(k * FRAME, (k + 1) * FRAME)
            out_ref[rows, :] = (table_ref[pl.ds(b, 1), :] * cot_ref[rows, :].astype(F32)).astype(BF)


def gated_cotangent(frames, steps, seq, table, cotangent):
    def half(rows, flip):
        return pl.BlockSpec((rows, 768), lambda n, f, t, s: (0, 2 * (s[0] % 2 ^ flip) + n))

    out = pl.BlockSpec((128, 768), lambda n, *_: (0, n))
    return pl.pallas_call(
        gated_kernel,
        out_shape=(jax.ShapeDtypeStruct((128, 1536), BF),) * 2,
        grid_spec=pltpu.PrefetchScalarGridSpec(
            num_scalar_prefetch=3,
            grid=(2,),
            in_specs=[half(64, 0), half(64, 1), half(128, 0), half(128, 1)],
            out_specs=(out, out),
        ),
        cost_estimate=cost(3),
        name="gated_cotangent",
    )(frames, steps, seq, table, table, cotangent, cotangent)


def output_kernel(
    frames_ref, steps_ref, seq_ref, t0_ref, t1_ref, l0_ref, l1_ref, own_ref, other_ref, out_ref
):
    bins = gate_bins(frames_ref, steps_ref, seq_ref)
    z = seq_ref[0] % 2
    halves = ((z, t0_ref, l0_ref, own_ref), (1 - z, t1_ref, l1_ref, other_ref))
    for place, table_ref, lat_ref, proj_ref in halves:
        at = pl.multiple_of(place * 1536, 1536)
        for k, b in enumerate(bins):
            rows = slice(k * FRAME, (k + 1) * FRAME)
            proj = proj_ref[rows, :].astype(F32)
            out = lat_ref[rows, :].astype(F32) + table_ref[pl.ds(b, 1), :] * proj
            out_ref[rows, pl.ds(at, 1536)] = out.astype(BF)


def gated_output(frames, steps, seq, table, latents, own, other):
    def half(rows, flip):
        return pl.BlockSpec((rows, 1536), lambda n, f, t, s: (0, s[0] % 2 ^ flip))

    whole = pl.BlockSpec((128, 1536), lambda n, *_: (0, 0))
    return pl.pallas_call(
        output_kernel,
        out_shape=jax.ShapeDtypeStruct((128, 3072), BF),
        grid_spec=pltpu.PrefetchScalarGridSpec(
            num_scalar_prefetch=3,
            grid=(1,),
            in_specs=[half(64, 0), half(64, 1), half(128, 0), half(128, 1), whole, whole],
            out_specs=pl.BlockSpec((128, 3072), lambda n, *_: (0, 0)),
        ),
        cost_estimate=cost(3),
        name="gated_output",
    )(frames, steps, seq, table, table, latents, latents, own, other)


def dattn_kernel(seq_ref, *refs):
    blocks, (w_ref, dproj_ref, other_ref, own_ref) = refs[:8], refs[8:]
    x, z = seq_ref[0] // 2, seq_ref[0] % 2
    for i, block in enumerate(blocks):
        place = 2 * ((x + i // 2) % 4) + (z ^ (i % 2))
        dproj_ref[pl.ds(pl.multiple_of(place * 128, 128), 128), :] = block[...]
    for m in range(2):
        rows = slice(m * 512, (m + 1) * 512)
        d = dproj_ref[rows, :]
        other_ref[rows, :] = dot_nn(d, w_ref[1]).astype(BF)
        own_ref[rows, :] = dot_nn(d, w_ref[0])


def dattn_parts(seq, blocks, weights):
    vmem = pl.BlockSpec(memory_space=pltpu.VMEM)
    return pl.pallas_call(
        dattn_kernel,
        out_shape=(
            jax.ShapeDtypeStruct((1024, 1536), BF),
            jax.ShapeDtypeStruct((1024, 384), BF),
            jax.ShapeDtypeStruct((1024, 384), F32),
        ),
        in_specs=[pl.BlockSpec(memory_space=pltpu.SMEM)] + [vmem] * 9,
        out_specs=(
            pl.BlockSpec((1024, 1536), lambda: (0, 0)),
            pl.BlockSpec((1024, 384), lambda: (0, 0)),
            pl.BlockSpec((1024, 384), lambda: (0, 0)),
        ),
        compiler_params=pltpu.CompilerParams(vmem_limit_bytes=VMEM_LIMIT),
        cost_estimate=cost(7),
        name="dattn_parts",
    )(seq, *blocks, weights)


def rows_spec(k):
    return pl.BlockSpec((256, 384), lambda n, s: ((s[0] // 2 + k) % 4, 0))


W_SPEC = pl.BlockSpec((2, 512, 384), lambda n, s: (0, n, 0))
TWO_SPEC = pl.BlockSpec((256, 512), lambda n, s: (0, n))
ONE_SPEC = pl.BlockSpec((128, 512), lambda n, s: (0, n))
ONE_BF = jax.ShapeDtypeStruct((128, 1536), BF)
TWO_BF = jax.ShapeDtypeStruct((256, 1536), BF)


def project(own_ref, other_ref, w_ref):
    return dot_nt(own_ref[...], w_ref[0]) + dot_nt(other_ref[...], w_ref[1])


def far_kernel(seq_ref, a_ref, b_ref, w_ref, up_ref, down_ref):
    part = project(a_ref, b_ref, w_ref).astype(BF)
    up_ref[...] = part[:128]
    down_ref[...] = part[128:]


def near_kernel(seq_ref, a1_ref, b1_ref, a3_ref, b3_ref, w_ref, up_ref, down_ref, t1_ref, t3_ref):
    p1 = project(a1_ref, b1_ref, w_ref)
    t1_ref[:128] = (p1[:128] + up_ref[...].astype(F32)).astype(BF)
    t1_ref[128:] = p1[128:].astype(BF)
    p3 = project(a3_ref, b3_ref, w_ref)
    t3_ref[:128] = p3[:128].astype(BF)
    t3_ref[128:] = (p3[128:] + down_ref[...].astype(F32)).astype(BF)


def home_kernel(seq_ref, a_ref, b_ref, w_ref, c1_ref, c3_ref, keep_ref, send_ref):
    part = project(a_ref, b_ref, w_ref)
    part = part + c1_ref[...].astype(F32) + c3_ref[...].astype(F32)
    first = seq_ref[0] % 2 == 0
    keep_ref[...] = jnp.where(first, part[:128], part[128:])
    send_ref[...] = jnp.where(first, part[128:], part[:128]).astype(BF)


def project_call(kernel, name, in_specs, out_shape, out_specs):
    return pl.pallas_call(
        kernel,
        out_shape=out_shape,
        grid_spec=pltpu.PrefetchScalarGridSpec(
            num_scalar_prefetch=1, grid=(3,), in_specs=in_specs, out_specs=out_specs
        ),
        compiler_params=pltpu.CompilerParams(vmem_limit_bytes=VMEM_LIMIT),
        cost_estimate=cost(4),
        name=name,
    )


def project_far(seq, own, other, weights):
    return project_call(
        far_kernel,
        "project_far",
        [rows_spec(2), rows_spec(2), W_SPEC],
        (ONE_BF, ONE_BF),
        (ONE_SPEC, ONE_SPEC),
    )(seq, own, other, weights)


def project_near(seq, own, other, weights, up, down):
    return project_call(
        near_kernel,
        "project_near",
        [rows_spec(1), rows_spec(1), rows_spec(3), rows_spec(3), W_SPEC, ONE_SPEC, ONE_SPEC],
        (TWO_BF, TWO_BF),
        (TWO_SPEC, TWO_SPEC),
    )(seq, own, other, own, other, weights, up, down)


def project_home(seq, own, other, weights, c1, c3):
    return project_call(
        home_kernel,
        "project_home",
        [rows_spec(0), rows_spec(0), W_SPEC, TWO_SPEC, TWO_SPEC],
        (jax.ShapeDtypeStruct((128, 1536), F32), ONE_BF),
        (ONE_SPEC, ONE_SPEC),
    )(seq, own, other, weights, c1, c3)


def dweight_kernel(core_ref, d_ref, a0_ref, a1_ref, keep_ref, send_ref):
    d = d_ref[...]
    even = core_ref[0] % 2 == 0
    for z, a_ref in enumerate((a0_ref, a1_ref)):
        g = dot_tn(d, a_ref[...]).astype(BF)
        for i in range(2):
            p0, p1 = g[i * 192 : i * 192 + 96], g[i * 192 + 96 : i * 192 + 192]
            keep_ref[z, i] = jnp.where(even, p0, p1)
            send_ref[z, i] = jnp.where(even, p1, p0)


def dweight_part(core, dproj, own, other):
    pieces = jax.ShapeDtypeStruct((2, 8, 96, 384), BF)
    return pl.pallas_call(
        dweight_kernel,
        out_shape=(pieces, pieces),
        grid_spec=pltpu.PrefetchScalarGridSpec(
            num_scalar_prefetch=1,
            grid=(4,),
            in_specs=[
                pl.BlockSpec((1024, 384), lambda n, c: (0, n)),
                pl.BlockSpec((1024, 384), lambda n, c: (0, 0)),
                pl.BlockSpec((1024, 384), lambda n, c: (0, 0)),
            ],
            out_specs=(
                pl.BlockSpec((2, 2, 96, 384), lambda n, c: (0, n, 0, 0)),
                pl.BlockSpec((2, 2, 96, 384), lambda n, c: (0, n, 0, 0)),
            ),
        ),
        compiler_params=pltpu.CompilerParams(vmem_limit_bytes=VMEM_LIMIT),
        cost_estimate=cost(7),
        name="dweight_part",
    )(core, dproj, own, other)


def pair_kernel(dp_ref, keep_ref, got_ref, *out_refs):
    y = dp_ref[0] // 8
    for k, out_ref in enumerate(out_refs):
        at = (y + k) % 4
        out_ref[...] = (keep_ref[at].astype(F32) + got_ref[at].astype(F32)).astype(BF)


def pair_sum(dp, keep, got):
    return pl.pallas_call(
        pair_kernel,
        out_shape=(jax.ShapeDtypeStruct((4, 96, 384), BF),) * 4,
        in_specs=[pl.BlockSpec(memory_space=pltpu.SMEM)]
        + [pl.BlockSpec((4, 4, 96, 384), lambda: (0, 0, 0, 0))] * 2,
        out_specs=(pl.BlockSpec((4, 96, 384), lambda: (0, 0, 0)),) * 4,
        cost_estimate=cost(3),
        name="pair_sum",
    )(dp, keep.reshape(4, 4, 96, 384), got.reshape(4, 4, 96, 384))


def ring_kernel(dp_ref, a_ref, b_ref, c_ref, d_ref, *out_refs):
    zh = dp_ref[0] // 2 % 4
    for k, out_ref in enumerate(out_refs):
        at = (zh + k) % 4
        total = a_ref[at].astype(F32) + b_ref[at].astype(F32)
        out_ref[...] = (total + c_ref[at].astype(F32) + d_ref[at].astype(F32)).astype(BF)


def ring_sum(dp, parts):
    return pl.pallas_call(
        ring_kernel,
        out_shape=(jax.ShapeDtypeStruct((96, 384), BF),) * 4,
        in_specs=[pl.BlockSpec(memory_space=pltpu.SMEM)]
        + [pl.BlockSpec((4, 96, 384), lambda: (0, 0, 0))] * 4,
        out_specs=(pl.BlockSpec((96, 384), lambda: (0, 0)),) * 4,
        cost_estimate=cost(2),
        name="ring_sum",
    )(dp, *parts)


def piece_moves(dp_count, seq_count):
    half = dp_count // 2
    moves = []
    for dp in range(dp_count):
        for seq in range(seq_count):
            top, z = dp // half, seq % 2
            to_dp = (dp % half) + half * (z ^ top)
            to_seq = seq - z + top
            moves.append((dp * seq_count + seq, to_dp * seq_count + to_seq))
    return moves


def along(x, axis, stride, places):
    size = lax.axis_size(axis)
    moves = []
    for i in range(size):
        at = i // stride % 4
        moves.append((i, i + ((at + places) % 4 - at) * stride))
    return lax.ppermute(x, axis, moves)


def along_x(x, places):
    return along(x, "seq", 2, places)


def along_y(x, places):
    return along(x, "dp", 8, places)


def along_z(x, places):
    return along(x, "dp", 2, places)


def swap_z(x):
    return lax.ppermute(x, "seq", [(i, i ^ 1) for i in range(lax.axis_size("seq"))])


def swap_core(x):
    return lax.ppermute(x, "dp", [(i, i ^ 1) for i in range(lax.axis_size("dp"))])


def body(qkv_input, latents, cotangent, out_weight, gate_table, timesteps, frames):
    seq = lax.axis_index("seq").astype(jnp.int32).reshape(1)
    dp = lax.axis_index("dp").astype(jnp.int32).reshape(1)
    both = ("dp", "seq")
    moves = piece_moves(lax.axis_size("dp"), lax.axis_size("seq"))

    piece = lax.ppermute(out_weight.T, both, moves)
    keep, send = gated_cotangent(frames, timesteps, seq, gate_table, cotangent)
    got = swap_z(send)
    b1_keep, b3_keep = along_x(keep, -1), along_x(keep, 1)
    packed = pack_heads(qkv_input.transpose(1, 0, 2))
    packed, piece, got, b1_keep, b3_keep = lax.optimization_barrier(
        (packed, piece, got, b1_keep, b3_keep)
    )
    weights = lax.all_gather(piece, "dp", axis=0, tiled=True).reshape(2, 1536, 384)
    heads = lax.all_to_all(packed, "seq", split_axis=0, concat_axis=0, tiled=True)

    b1 = [b1_keep, along_x(got, -1)]
    b3 = [b3_keep, along_x(got, 1)]
    late, weights = lax.optimization_barrier((b1[1], weights))
    b2 = [along_x(b3[0], 1), along_x(late, -1)]

    attn, p1, p2 = attention_forward(frames, heads)
    attn_other = swap_z(attn)
    dproj, d_send, d_own = dattn_parts(seq, [keep, got, *b1, *b2, *b3], weights)
    d_recv = swap_z(d_send)
    up, down = project_far(seq, attn, attn_other, weights)
    up, down = along_x(up, 1), along_x(down, -1)
    t1, t3 = project_near(seq, attn, attn_other, weights, up, down)
    d_own, d_recv, t1, t3 = lax.optimization_barrier((d_own, d_recv, t1, t3))
    c1, c3 = along_x(t1, 1), along_x(t3, -1)

    grads = attention_backward(frames, heads, d_own, d_recv, p1, p2)
    grads, c1, c3, dproj = lax.optimization_barrier((grads, c1, c3, dproj))
    w_keep, w_send = dweight_part(dp, dproj, attn, attn_other)
    w_got = swap_core(w_send)
    grads = lax.all_to_all(grads, "seq", split_axis=0, concat_axis=0, tiled=True)
    terms = pair_sum(dp, w_keep, w_got)
    terms = [terms[0]] + [along_y(terms[k], k) for k in range(1, 4)]

    o_keep, o_send = project_home(seq, attn, attn_other, weights, c1, c3)
    terms, o_send = lax.optimization_barrier((terms, o_send))
    terms = ring_sum(dp, terms)
    terms = [terms[0]] + [along_z(terms[k], k) for k in range(1, 4)]
    total = terms[0].astype(F32) + terms[1].astype(F32)
    total = total + terms[2].astype(F32) + terms[3].astype(F32)
    total = lax.ppermute(total, both, [(b, a) for a, b in moves])
    o_got = swap_z(o_send)
    grad_qkv = unpack_heads(grads)
    grad_qkv, o_got = lax.optimization_barrier((grad_qkv, o_got))
    output = gated_output(frames, timesteps, seq, gate_table, latents, o_keep, o_got)
    return (output, grad_qkv.transpose(1, 0, 2), total.T)


def solution(mesh):
    placed = (
        P(("dp", "seq"), None, None),
        P(("dp", "seq"), None),
        P(("dp", "seq"), None),
        P("seq", "dp"),
        P(),
        P("dp", None),
        P("dp", None),
    )
    return jax.shard_map(
        body,
        mesh=mesh,
        in_specs=placed,
        out_specs=(P(("dp", "seq"), None), P(("dp", "seq"), None, None), P("seq", "dp")),
        check_vma=False,
    )
```

```python
import jax
import jax.numpy as jnp
from jax import lax
from jax.experimental import pallas as pl
from jax.experimental.pallas import tpu as pltpu
from jax.sharding import PartitionSpec as P

HD = 128
FRAME = 64
LONG = 640
REST = 384
LOG2E = 1.4426950408889634
VMEM_LIMIT = 56 * 1024 * 1024

BF = jnp.bfloat16
F32 = jnp.float32


def cost(us):
    return pl.CostEstimate(flops=int(us * 1e9), transcendentals=0, bytes_accessed=int(us * 3e6))


def dot_nt(a, b):
    return lax.dot_general(a, b, (((1,), (1,)), ((), ())), preferred_element_type=F32)


def dot_nn(a, b):
    return lax.dot_general(a, b, (((1,), (0,)), ((), ())), preferred_element_type=F32)


def dot_tn(a, b):
    return lax.dot_general(a, b, (((0,), (0,)), ((), ())), preferred_element_type=F32)


def clip_places(frames_ref):
    f0, f1, f2 = frames_ref[0, 0], frames_ref[0, 1], frames_ref[0, 2]
    first = jnp.logical_and(f0 > f1, f0 > f2)
    second = f1 > f2
    start = jnp.where(first, 0, jnp.where(second, f0, f0 + f1)) * FRAME
    lead = jnp.where(first, f1, f0)
    return start, lead


def gate_bins(frames_ref, steps_ref, seq_ref):
    f0, f1 = frames_ref[0, 0], frames_ref[0, 1]
    bins = []
    for k in range(2):
        frame = seq_ref[0] * 2 + k
        clip = jnp.where(frame >= f0, 1, 0) + jnp.where(frame >= f0 + f1, 1, 0)
        bins.append(steps_ref[0, clip])
    return bins


def spans(total):
    out, at = [], 0
    while at < total:
        size = min(256, total - at)
        out.append((at, size))
        at += size
    return out


def rest_places(start):
    return [
        pl.multiple_of(jnp.where(t * FRAME >= start, t * FRAME + LONG, t * FRAME), FRAME)
        for t in range(REST // FRAME)
    ]


def load_split(src, start):
    main = src[pl.ds(start, LONG), :]
    rest = jnp.concatenate([src[pl.ds(p, FRAME), :] for p in rest_places(start)], axis=0)
    return main, rest


def rest_mask(lead, at, size):
    rows = lax.broadcasted_iota(jnp.int32, (REST, size), 0)
    cols = lax.broadcasted_iota(jnp.int32, (REST, size), 1) + at
    edge = lead * FRAME
    return (rows < edge) == (cols < edge)


def fwd_kernel(frames_ref, qkv_ref, attn_ref, p1_ref, p2_ref, q_s, k_s, v_s):
    start, lead = clip_places(frames_ref)
    start = pl.multiple_of(start, FRAME)
    q_s[...] = qkv_ref[:, 0].reshape(1024, HD)
    k_s[...] = qkv_ref[:, 1].reshape(1024, HD)
    v_s[...] = qkv_ref[:, 2].reshape(1024, HD)
    factor = LOG2E / (HD**0.5)
    q1, q2 = load_split(q_s, start)
    k1, k2 = load_split(k_s, start)
    v1, v2 = load_split(v_s, start)
    places = rest_places(start)
    for long, (q, k, v, p_ref) in ((True, (q1, k1, v1, p1_ref)), (False, (q2, k2, v2, p2_ref))):
        vt = v.astype(F32).T.astype(BF)
        for at, size in spans(LONG if long else REST):
            s = dot_nt(k, q[at : at + size])
            if not long:
                s = jnp.where(rest_mask(lead, at, size), s, F32(-1e30))
            top = jnp.max(s, axis=0, keepdims=True)
            e = jnp.exp2((s - top) * F32(factor))
            total = jnp.sum(e, axis=0, keepdims=True)
            p = (e * (1.0 / total)).astype(BF)
            p_ref[0, :, at : at + size] = p
            o = dot_nn(vt, p).T.astype(BF)
            if long:
                attn_ref[pl.ds(start + at, size), :] = o
            else:
                for t in range(size // FRAME):
                    attn_ref[pl.ds(places[at // FRAME + t], FRAME), :] = o[
                        t * FRAME : (t + 1) * FRAME
                    ]


def attention_forward(frames, heads):
    return pl.pallas_call(
        fwd_kernel,
        out_shape=(
            jax.ShapeDtypeStruct((1024, 3 * HD), BF),
            jax.ShapeDtypeStruct((3, LONG, LONG), BF),
            jax.ShapeDtypeStruct((3, REST, REST), BF),
        ),
        grid_spec=pltpu.PrefetchScalarGridSpec(
            num_scalar_prefetch=1,
            grid=(3,),
            in_specs=[pl.BlockSpec((8, 3, 128, HD), lambda h, f: (0, 0, 0, h))],
            out_specs=(
                pl.BlockSpec((1024, HD), lambda h, f: (0, h)),
                pl.BlockSpec((1, LONG, LONG), lambda h, f: (h, 0, 0)),
                pl.BlockSpec((1, REST, REST), lambda h, f: (h, 0, 0)),
            ),
            scratch_shapes=[pltpu.VMEM((1024, HD), BF)] * 3,
        ),
        compiler_params=pltpu.CompilerParams(vmem_limit_bytes=VMEM_LIMIT),
        cost_estimate=cost(10),
        name="attention_forward",
    )(frames, heads)


def bwd_kernel(
    frames_ref, qkv_ref, own_ref, other_ref, p1_ref, p2_ref, out_ref, q_s, k_s, v_s, d_s, ds1, ds2, g_s
):
    start, lead = clip_places(frames_ref)
    start = pl.multiple_of(start, FRAME)
    q_s[...] = qkv_ref[:, 0].reshape(1024, HD)
    k_s[...] = qkv_ref[:, 1].reshape(1024, HD)
    v_s[...] = qkv_ref[:, 2].reshape(1024, HD)
    d_s[...] = (own_ref[...] + other_ref[...].astype(F32)).astype(BF)
    scale = 1.0 / (HD**0.5)
    q1, q2 = load_split(q_s, start)
    k1, k2 = load_split(k_s, start)
    v1, v2 = load_split(v_s, start)
    d1, d2 = load_split(d_s, start)
    places = rest_places(start)

    def put(which, long, value):
        if long:
            g_s[which, pl.ds(start, LONG), :] = value
        else:
            for t in range(REST // FRAME):
                g_s[which, pl.ds(places[t], FRAME), :] = value[t * FRAME : (t + 1) * FRAME]

    for long, (q, k, v, d, p_ref, ds_ref) in (
        (True, (q1, k1, v1, d1, p1_ref, ds1)),
        (False, (q2, k2, v2, d2, p2_ref, ds2)),
    ):
        kt = k.astype(F32).T.astype(BF)
        parts = []
        for at, size in spans(LONG if long else REST):
            dp = dot_nt(v, d[at : at + size]).astype(BF).astype(F32)
            p = p_ref[0, :, at : at + size].astype(F32)
            pd = p * dp
            delta = jnp.sum(pd, axis=0, keepdims=True)
            ds = ((pd - p * delta) * F32(scale)).astype(BF)
            ds_ref[:, at : at + size] = ds
            parts.append(dot_nn(kt, ds).T.astype(BF))
        put(0, long, jnp.concatenate(parts, axis=0))
        put(1, long, dot_nn(ds_ref[...], q).astype(BF))
        put(2, long, dot_nn(p_ref[0], d).astype(BF))
    for which in range(3):
        out_ref[:, which] = g_s[which].reshape(8, 128, HD)


def attention_backward(frames, heads, own, other, p1, p2):
    return pl.pallas_call(
        bwd_kernel,
        out_shape=jax.ShapeDtypeStruct((8, 3, 128, 3 * HD), BF),
        grid_spec=pltpu.PrefetchScalarGridSpec(
            num_scalar_prefetch=1,
            grid=(3,),
            in_specs=[
                pl.BlockSpec((8, 3, 128, HD), lambda h, f: (0, 0, 0, h)),
                pl.BlockSpec((1024, HD), lambda h, f: (0, h)),
                pl.BlockSpec((1024, HD), lambda h, f: (0, h)),
                pl.BlockSpec((1, LONG, LONG), lambda h, f: (h, 0, 0)),
                pl.BlockSpec((1, REST, REST), lambda h, f: (h, 0, 0)),
            ],
            out_specs=pl.BlockSpec((8, 3, 128, HD), lambda h, f: (0, 0, 0, h)),
            scratch_shapes=[pltpu.VMEM((1024, HD), BF)] * 4
            + [
                pltpu.VMEM((LONG, LONG), BF),
                pltpu.VMEM((REST, REST), BF),
                pltpu.VMEM((3, 1024, HD), BF),
            ],
        ),
        compiler_params=pltpu.CompilerParams(vmem_limit_bytes=VMEM_LIMIT),
        cost_estimate=cost(11),
        name="attention_backward",
    )(frames, heads, own, other, p1, p2)


def pack_kernel(in_ref, out_ref):
    for j in range(4):
        out_ref[j] = in_ref[:, :, j * 384 : (j + 1) * 384]


def pack_heads(qkv):
    return pl.pallas_call(
        pack_kernel,
        out_shape=jax.ShapeDtypeStruct((8, 3, 128, 384), BF),
        grid=(2,),
        in_specs=[pl.BlockSpec((3, 128, 1536), lambda j: (0, 0, j))],
        out_specs=pl.BlockSpec((4, 3, 128, 384), lambda j: (j, 0, 0, 0)),
        cost_estimate=cost(3),
        name="pack_heads",
    )(qkv)


def unpack_kernel(in_ref, out_ref):
    for j in range(4):
        out_ref[:, :, j * 384 : (j + 1) * 384] = in_ref[j]


def unpack_heads(grads):
    return pl.pallas_call(
        unpack_kernel,
        out_shape=jax.ShapeDtypeStruct((3, 128, 3072), BF),
        grid=(2,),
        in_specs=[pl.BlockSpec((4, 3, 128, 384), lambda j: (j, 0, 0, 0))],
        out_specs=pl.BlockSpec((3, 128, 1536), lambda j: (0, 0, j)),
        cost_estimate=cost(3),
        name="unpack_heads",
    )(grads)


def gated_kernel(frames_ref, steps_ref, seq_ref, t0_ref, t1_ref, c0_ref, c1_ref, keep_ref, send_ref):
    bins = gate_bins(frames_ref, steps_ref, seq_ref)
    for table_ref, cot_ref, out_ref in ((t0_ref, c0_ref, keep_ref), (t1_ref, c1_ref, send_ref)):
        for k, b in enumerate(bins):
            rows = slice(k * FRAME, (k + 1) * FRAME)
            out_ref[rows, :] = (table_ref[pl.ds(b, 1), :] * cot_ref[rows, :].astype(F32)).astype(BF)


def gated_cotangent(frames, steps, seq, table, cotangent):
    def half(rows, flip):
        return pl.BlockSpec((rows, 768), lambda n, f, t, s: (0, 2 * (s[0] % 2 ^ flip) + n))

    out = pl.BlockSpec((128, 768), lambda n, *_: (0, n))
    return pl.pallas_call(
        gated_kernel,
        out_shape=(jax.ShapeDtypeStruct((128, 1536), BF),) * 2,
        grid_spec=pltpu.PrefetchScalarGridSpec(
            num_scalar_prefetch=3,
            grid=(2,),
            in_specs=[half(64, 0), half(64, 1), half(128, 0), half(128, 1)],
            out_specs=(out, out),
        ),
        cost_estimate=cost(3),
        name="gated_cotangent",
    )(frames, steps, seq, table, table, cotangent, cotangent)


def output_kernel(
    frames_ref, steps_ref, seq_ref, t0_ref, t1_ref, l0_ref, l1_ref, own_ref, other_ref, out_ref
):
    bins = gate_bins(frames_ref, steps_ref, seq_ref)
    z = seq_ref[0] % 2
    halves = ((z, t0_ref, l0_ref, own_ref), (1 - z, t1_ref, l1_ref, other_ref))
    for place, table_ref, lat_ref, proj_ref in halves:
        at = pl.multiple_of(place * 1536, 1536)
        for k, b in enumerate(bins):
            rows = slice(k * FRAME, (k + 1) * FRAME)
            proj = proj_ref[rows, :].astype(F32)
            out = lat_ref[rows, :].astype(F32) + table_ref[pl.ds(b, 1), :] * proj
            out_ref[rows, pl.ds(at, 1536)] = out.astype(BF)


def gated_output(frames, steps, seq, table, latents, own, other):
    def half(rows, flip):
        return pl.BlockSpec((rows, 1536), lambda n, f, t, s: (0, s[0] % 2 ^ flip))

    whole = pl.BlockSpec((128, 1536), lambda n, *_: (0, 0))
    return pl.pallas_call(
        output_kernel,
        out_shape=jax.ShapeDtypeStruct((128, 3072), BF),
        grid_spec=pltpu.PrefetchScalarGridSpec(
            num_scalar_prefetch=3,
            grid=(1,),
            in_specs=[half(64, 0), half(64, 1), half(128, 0), half(128, 1), whole, whole],
            out_specs=pl.BlockSpec((128, 3072), lambda n, *_: (0, 0)),
        ),
        cost_estimate=cost(3),
        name="gated_output",
    )(frames, steps, seq, table, table, latents, latents, own, other)


def dattn_kernel(seq_ref, *refs):
    blocks, (w_ref, dproj_ref, other_ref, own_ref) = refs[:8], refs[8:]
    x, z = seq_ref[0] // 2, seq_ref[0] % 2
    for i, block in enumerate(blocks):
        place = 2 * ((x + i // 2) % 4) + (z ^ (i % 2))
        dproj_ref[pl.ds(pl.multiple_of(place * 128, 128), 128), :] = block[...]
    for m in range(2):
        rows = slice(m * 512, (m + 1) * 512)
        d = dproj_ref[rows, :]
        other_ref[rows, :] = dot_nn(d, w_ref[1]).astype(BF)
        own_ref[rows, :] = dot_nn(d, w_ref[0])


def dattn_parts(seq, blocks, weights):
    vmem = pl.BlockSpec(memory_space=pltpu.VMEM)
    return pl.pallas_call(
        dattn_kernel,
        out_shape=(
            jax.ShapeDtypeStruct((1024, 1536), BF),
            jax.ShapeDtypeStruct((1024, 384), BF),
            jax.ShapeDtypeStruct((1024, 384), F32),
        ),
        in_specs=[pl.BlockSpec(memory_space=pltpu.SMEM)] + [vmem] * 9,
        out_specs=(
            pl.BlockSpec((1024, 1536), lambda: (0, 0)),
            pl.BlockSpec((1024, 384), lambda: (0, 0)),
            pl.BlockSpec((1024, 384), lambda: (0, 0)),
        ),
        compiler_params=pltpu.CompilerParams(vmem_limit_bytes=VMEM_LIMIT),
        cost_estimate=cost(7),
        name="dattn_parts",
    )(seq, *blocks, weights)


def rows_spec(k):
    return pl.BlockSpec((256, 384), lambda n, s: ((s[0] // 2 + k) % 4, 0))


W_SPEC = pl.BlockSpec((2, 512, 384), lambda n, s: (0, n, 0))
TWO_SPEC = pl.BlockSpec((256, 512), lambda n, s: (0, n))
ONE_SPEC = pl.BlockSpec((128, 512), lambda n, s: (0, n))
ONE_BF = jax.ShapeDtypeStruct((128, 1536), BF)
TWO_BF = jax.ShapeDtypeStruct((256, 1536), BF)


def project(own_ref, other_ref, w_ref):
    return dot_nt(own_ref[...], w_ref[0]) + dot_nt(other_ref[...], w_ref[1])


def far_kernel(seq_ref, a_ref, b_ref, w_ref, up_ref, down_ref):
    part = project(a_ref, b_ref, w_ref).astype(BF)
    up_ref[...] = part[:128]
    down_ref[...] = part[128:]


def near_kernel(seq_ref, a1_ref, b1_ref, a3_ref, b3_ref, w_ref, up_ref, down_ref, t1_ref, t3_ref):
    p1 = project(a1_ref, b1_ref, w_ref)
    t1_ref[:128] = (p1[:128] + up_ref[...].astype(F32)).astype(BF)
    t1_ref[128:] = p1[128:].astype(BF)
    p3 = project(a3_ref, b3_ref, w_ref)
    t3_ref[:128] = p3[:128].astype(BF)
    t3_ref[128:] = (p3[128:] + down_ref[...].astype(F32)).astype(BF)


def home_kernel(seq_ref, a_ref, b_ref, w_ref, c1_ref, c3_ref, keep_ref, send_ref):
    part = project(a_ref, b_ref, w_ref)
    part = part + c1_ref[...].astype(F32) + c3_ref[...].astype(F32)
    first = seq_ref[0] % 2 == 0
    keep_ref[...] = jnp.where(first, part[:128], part[128:])
    send_ref[...] = jnp.where(first, part[128:], part[:128]).astype(BF)


def project_call(kernel, name, in_specs, out_shape, out_specs):
    return pl.pallas_call(
        kernel,
        out_shape=out_shape,
        grid_spec=pltpu.PrefetchScalarGridSpec(
            num_scalar_prefetch=1, grid=(3,), in_specs=in_specs, out_specs=out_specs
        ),
        compiler_params=pltpu.CompilerParams(vmem_limit_bytes=VMEM_LIMIT),
        cost_estimate=cost(4),
        name=name,
    )


def project_far(seq, own, other, weights):
    return project_call(
        far_kernel,
        "project_far",
        [rows_spec(2), rows_spec(2), W_SPEC],
        (ONE_BF, ONE_BF),
        (ONE_SPEC, ONE_SPEC),
    )(seq, own, other, weights)


def project_near(seq, own, other, weights, up, down):
    return project_call(
        near_kernel,
        "project_near",
        [rows_spec(1), rows_spec(1), rows_spec(3), rows_spec(3), W_SPEC, ONE_SPEC, ONE_SPEC],
        (TWO_BF, TWO_BF),
        (TWO_SPEC, TWO_SPEC),
    )(seq, own, other, own, other, weights, up, down)


def project_home(seq, own, other, weights, c1, c3):
    return project_call(
        home_kernel,
        "project_home",
        [rows_spec(0), rows_spec(0), W_SPEC, TWO_SPEC, TWO_SPEC],
        (jax.ShapeDtypeStruct((128, 1536), F32), ONE_BF),
        (ONE_SPEC, ONE_SPEC),
    )(seq, own, other, weights, c1, c3)


def dweight_kernel(dp_ref, d_ref, a_ref, keep_ref, send_ref):
    even = dp_ref[0] % 2 == 0
    g = dot_tn(d_ref[...], a_ref[...]).astype(BF)
    for i in range(4):
        p0, p1 = g[i * 192 : i * 192 + 96], g[i * 192 + 96 : i * 192 + 192]
        keep_ref[i] = jnp.where(even, p0, p1)
        send_ref[i] = jnp.where(even, p1, p0)


def dweight_part(dp, dproj, attn):
    pieces = jax.ShapeDtypeStruct((8, 96, 384), BF)
    return pl.pallas_call(
        dweight_kernel,
        out_shape=(pieces, pieces),
        grid_spec=pltpu.PrefetchScalarGridSpec(
            num_scalar_prefetch=1,
            grid=(2,),
            in_specs=[
                pl.BlockSpec((1024, 768), lambda n, c: (0, n)),
                pl.BlockSpec((1024, 384), lambda n, c: (0, 0)),
            ],
            out_specs=(
                pl.BlockSpec((4, 96, 384), lambda n, c: (n, 0, 0)),
                pl.BlockSpec((4, 96, 384), lambda n, c: (n, 0, 0)),
            ),
        ),
        compiler_params=pltpu.CompilerParams(vmem_limit_bytes=VMEM_LIMIT),
        cost_estimate=cost(4),
        name="dweight_part",
    )(dp, dproj, attn)


def pair_kernel(dp_ref, k0_ref, g0_ref, k1_ref, g1_ref, *out_refs):
    y = dp_ref[0] // 8
    for k, out_ref in enumerate(out_refs):
        at = (y + k) % 4
        for half, (keep_ref, got_ref) in enumerate(((k0_ref, g0_ref), (k1_ref, g1_ref))):

            @pl.when(at // 2 == half)
            def _(keep_ref=keep_ref, got_ref=got_ref, out_ref=out_ref, at=at):
                total = keep_ref[at % 2].astype(F32) + got_ref[at % 2].astype(F32)
                out_ref[...] = total.astype(BF)


def pair_sum(dp, keep0, got0, keep1, got1):
    terms = [t.reshape(2, 4, 96, 384) for t in (keep0, got0, keep1, got1)]
    return pl.pallas_call(
        pair_kernel,
        out_shape=(jax.ShapeDtypeStruct((4, 96, 384), BF),) * 4,
        in_specs=[pl.BlockSpec(memory_space=pltpu.SMEM)]
        + [pl.BlockSpec((2, 4, 96, 384), lambda: (0, 0, 0, 0))] * 4,
        out_specs=(pl.BlockSpec((4, 96, 384), lambda: (0, 0, 0)),) * 4,
        cost_estimate=cost(3),
        name="pair_sum",
    )(dp, *terms)


def ring_kernel(dp_ref, a_ref, b_ref, c_ref, d_ref, *out_refs):
    zh = dp_ref[0] // 2 % 4
    for k, out_ref in enumerate(out_refs):
        at = (zh + k) % 4
        total = a_ref[at].astype(F32) + b_ref[at].astype(F32)
        out_ref[...] = (total + c_ref[at].astype(F32) + d_ref[at].astype(F32)).astype(BF)


def ring_sum(dp, parts):
    return pl.pallas_call(
        ring_kernel,
        out_shape=(jax.ShapeDtypeStruct((96, 384), BF),) * 4,
        in_specs=[pl.BlockSpec(memory_space=pltpu.SMEM)]
        + [pl.BlockSpec((4, 96, 384), lambda: (0, 0, 0))] * 4,
        out_specs=(pl.BlockSpec((96, 384), lambda: (0, 0)),) * 4,
        cost_estimate=cost(2),
        name="ring_sum",
    )(dp, *parts)


def piece_moves(dp_count, seq_count):
    half = dp_count // 2
    moves = []
    for dp in range(dp_count):
        for seq in range(seq_count):
            top, z = dp // half, seq % 2
            to_dp = (dp % half) + half * (z ^ top)
            to_seq = seq - z + top
            moves.append((dp * seq_count + seq, to_dp * seq_count + to_seq))
    return moves


def along(x, axis, stride, places):
    size = lax.axis_size(axis)
    moves = []
    for i in range(size):
        at = i // stride % 4
        moves.append((i, i + ((at + places) % 4 - at) * stride))
    return lax.ppermute(x, axis, moves)


def along_x(x, places):
    return along(x, "seq", 2, places)


def along_y(x, places):
    return along(x, "dp", 8, places)


def along_z(x, places):
    return along(x, "dp", 2, places)


def swap_z(x):
    return lax.ppermute(x, "seq", [(i, i ^ 1) for i in range(lax.axis_size("seq"))])


def swap_core(x):
    return lax.ppermute(x, "dp", [(i, i ^ 1) for i in range(lax.axis_size("dp"))])


def body(qkv_input, latents, cotangent, out_weight, gate_table, timesteps, frames):
    seq = lax.axis_index("seq").astype(jnp.int32).reshape(1)
    dp = lax.axis_index("dp").astype(jnp.int32).reshape(1)
    both = ("dp", "seq")
    moves = piece_moves(lax.axis_size("dp"), lax.axis_size("seq"))

    piece = lax.ppermute(out_weight.T, both, moves)
    packed = pack_heads(qkv_input.transpose(1, 0, 2))
    packed, piece, cotangent = lax.optimization_barrier((packed, piece, cotangent))
    weights = lax.all_gather(piece, "dp", axis=0, tiled=True).reshape(2, 1536, 384)
    keep, send = gated_cotangent(frames, timesteps, seq, gate_table, cotangent)
    got = swap_z(send)
    b1_keep, b3_keep = along_x(keep, -1), along_x(keep, 1)
    packed, got, b1_keep, b3_keep = lax.optimization_barrier((packed, got, b1_keep, b3_keep))
    heads = lax.all_to_all(packed, "seq", split_axis=0, concat_axis=0, tiled=True)

    b1 = [b1_keep, along_x(got, -1)]
    b3 = [b3_keep, along_x(got, 1)]
    late, weights = lax.optimization_barrier((b1[1], weights))
    b2 = [along_x(b3[0], 1), along_x(late, -1)]

    attn, p1, p2 = attention_forward(frames, heads)
    attn_other = swap_z(attn)
    dproj, d_send, d_own = dattn_parts(seq, [keep, got, *b1, *b2, *b3], weights)
    d_recv = swap_z(d_send)
    keep0, send0 = dweight_part(dp, dproj, attn)
    attn_other, keep0 = lax.optimization_barrier((attn_other, keep0))
    got0 = swap_core(send0)
    up, down = project_far(seq, attn, attn_other, weights)
    behind, _ = lax.optimization_barrier((dproj, up))
    keep1, send1 = dweight_part(dp, behind, attn_other)
    got1 = swap_core(send1)
    up, down = along_x(up, 1), along_x(down, -1)
    up, keep1 = lax.optimization_barrier((up, keep1))
    t1, t3 = project_near(seq, attn, attn_other, weights, up, down)
    d_own, d_recv, t1, t3 = lax.optimization_barrier((d_own, d_recv, t1, t3))
    c1, c3 = along_x(t1, 1), along_x(t3, -1)
    terms = pair_sum(dp, keep0, got0, keep1, got1)

    grads = attention_backward(frames, heads, d_own, d_recv, p1, p2)
    grads, c1, c3, terms = lax.optimization_barrier((grads, c1, c3, terms))
    grads = lax.all_to_all(grads, "seq", split_axis=0, concat_axis=0, tiled=True)
    terms = [terms[0]] + [along_y(terms[k], k) for k in range(1, 4)]

    o_keep, o_send = project_home(seq, attn, attn_other, weights, c1, c3)
    terms, o_send = lax.optimization_barrier((terms, o_send))
    terms = ring_sum(dp, terms)
    terms = [terms[0]] + [along_z(terms[k], k) for k in range(1, 4)]
    total = terms[0].astype(F32) + terms[1].astype(F32)
    total = total + terms[2].astype(F32) + terms[3].astype(F32)
    total = lax.ppermute(total, both, [(b, a) for a, b in moves])
    o_got = swap_z(o_send)
    grad_qkv = unpack_heads(grads)
    grad_qkv, o_got = lax.optimization_barrier((grad_qkv, o_got))
    output = gated_output(frames, timesteps, seq, gate_table, latents, o_keep, o_got)
    return (output, grad_qkv.transpose(1, 0, 2), total.T)


def solution(mesh):
    placed = (
        P(("dp", "seq"), None, None),
        P(("dp", "seq"), None),
        P(("dp", "seq"), None),
        P("seq", "dp"),
        P(),
        P("dp", None),
        P("dp", None),
    )
    return jax.shard_map(
        body,
        mesh=mesh,
        in_specs=placed,
        out_specs=(P(("dp", "seq"), None), P(("dp", "seq"), None, None), P("seq", "dp")),
        check_vma=False,
    )
```

```python
import jax
import jax.numpy as jnp
from jax import lax
from jax.experimental import pallas as pl
from jax.experimental.pallas import tpu as pltpu
from jax.sharding import PartitionSpec as P

HD = 128
FRAME = 64
LONG = 640
REST = 384
LOG2E = 1.4426950408889634
VMEM_LIMIT = 32 * 1024 * 1024

BF = jnp.bfloat16
F32 = jnp.float32
VMEM = pl.BlockSpec(memory_space=pltpu.VMEM)
SMEM = pl.BlockSpec(memory_space=pltpu.SMEM)
PARAMS = pltpu.CompilerParams(vmem_limit_bytes=VMEM_LIMIT)


def shape(dims, dtype=BF):
    return jax.ShapeDtypeStruct(dims, dtype)


def whole(dims):
    return pl.BlockSpec(dims, lambda: (0,) * len(dims))


def cost(us):
    return pl.CostEstimate(flops=int(us * 1e9), transcendentals=0, bytes_accessed=int(us * 3e6))


def dot_nt(a, b):
    return lax.dot_general(a, b, (((1,), (1,)), ((), ())), preferred_element_type=F32)


def dot_nn(a, b):
    return lax.dot_general(a, b, (((1,), (0,)), ((), ())), preferred_element_type=F32)


def dot_tn(a, b):
    return lax.dot_general(a, b, (((0,), (0,)), ((), ())), preferred_element_type=F32)


def clip_places(frames_ref):
    f0, f1, f2 = frames_ref[0, 0], frames_ref[0, 1], frames_ref[0, 2]
    first = jnp.logical_and(f0 > f1, f0 > f2)
    second = f1 > f2
    start = jnp.where(first, 0, jnp.where(second, f0, f0 + f1)) * FRAME
    lead = jnp.where(first, f1, f0)
    return start, lead


def gate_bins(frames_ref, steps_ref, seq_ref):
    f0, f1 = frames_ref[0, 0], frames_ref[0, 1]
    bins = []
    for k in range(2):
        frame = seq_ref[0] * 2 + k
        clip = jnp.where(frame >= f0, 1, 0) + jnp.where(frame >= f0 + f1, 1, 0)
        bins.append(steps_ref[0, clip])
    return bins


def spans(total):
    out, at = [], 0
    while at < total:
        size = min(256, total - at)
        out.append((at, size))
        at += size
    return out


def rest_places(start):
    return [
        pl.multiple_of(jnp.where(t * FRAME >= start, t * FRAME + LONG, t * FRAME), FRAME)
        for t in range(REST // FRAME)
    ]


def load_split(src, start):
    main = src[pl.ds(start, LONG), :]
    rest = jnp.concatenate([src[pl.ds(p, FRAME), :] for p in rest_places(start)], axis=0)
    return main, rest


def rest_mask(lead, at, size):
    rows = lax.broadcasted_iota(jnp.int32, (REST, size), 0)
    cols = lax.broadcasted_iota(jnp.int32, (REST, size), 1) + at
    edge = lead * FRAME
    return (rows < edge) == (cols < edge)


def fwd_kernel(frames_ref, qkv_ref, attn_ref, p1_ref, p2_ref, q_s, k_s, v_s):
    start, lead = clip_places(frames_ref)
    start = pl.multiple_of(start, FRAME)
    places = rest_places(start)
    factor = LOG2E / (HD**0.5)

    def head(h, carry):
        lanes = pl.ds(pl.multiple_of(h * HD, HD), HD)
        q_s[...] = qkv_ref[:, 0, :, lanes].reshape(1024, HD)
        k_s[...] = qkv_ref[:, 1, :, lanes].reshape(1024, HD)
        v_s[...] = qkv_ref[:, 2, :, lanes].reshape(1024, HD)
        q1, q2 = load_split(q_s, start)
        k1, k2 = load_split(k_s, start)
        v1, v2 = load_split(v_s, start)
        for long, (q, k, v, p_ref) in ((True, (q1, k1, v1, p1_ref)), (False, (q2, k2, v2, p2_ref))):
            vt = v.astype(F32).T.astype(BF)
            for at, size in spans(LONG if long else REST):
                s = dot_nt(k, q[at : at + size])
                if not long:
                    s = jnp.where(rest_mask(lead, at, size), s, F32(-1e30))
                top = jnp.max(s, axis=0, keepdims=True)
                e = jnp.exp2((s - top) * F32(factor))
                total = jnp.sum(e, axis=0, keepdims=True)
                p = (e * (1.0 / total)).astype(BF)
                p_ref[h, :, at : at + size] = p
                o = dot_nn(vt, p).T.astype(BF)
                if long:
                    attn_ref[pl.ds(start + at, size), lanes] = o
                else:
                    for t in range(size // FRAME):
                        attn_ref[pl.ds(places[at // FRAME + t], FRAME), lanes] = o[
                            t * FRAME : (t + 1) * FRAME
                        ]
        return carry

    lax.fori_loop(0, 3, head, 0)


def attention_forward(frames, heads):
    return pl.pallas_call(
        fwd_kernel,
        out_shape=(shape((1024, 3 * HD)), shape((3, LONG, LONG)), shape((3, REST, REST))),
        in_specs=[SMEM, VMEM],
        out_specs=(whole((1024, 3 * HD)), VMEM, VMEM),
        scratch_shapes=[pltpu.VMEM((1024, HD), BF)] * 3,
        compiler_params=PARAMS,
        cost_estimate=cost(0.1),
        name="attention_forward",
    )(frames, heads)


def bwd_kernel(
    frames_ref, qkv_ref, own_ref, other_ref, p1_ref, p2_ref, out_ref, q_s, k_s, v_s, d_s, ds1, ds2, g_s
):
    start, lead = clip_places(frames_ref)
    start = pl.multiple_of(start, FRAME)
    places = rest_places(start)
    scale = 1.0 / (HD**0.5)

    def put(which, long, value):
        if long:
            g_s[which, pl.ds(start, LONG), :] = value
        else:
            for t in range(REST // FRAME):
                g_s[which, pl.ds(places[t], FRAME), :] = value[t * FRAME : (t + 1) * FRAME]

    def head(h, carry):
        lanes = pl.ds(pl.multiple_of(h * HD, HD), HD)
        q_s[...] = qkv_ref[:, 0, :, lanes].reshape(1024, HD)
        k_s[...] = qkv_ref[:, 1, :, lanes].reshape(1024, HD)
        v_s[...] = qkv_ref[:, 2, :, lanes].reshape(1024, HD)
        d_s[...] = (own_ref[:, lanes] + other_ref[:, lanes].astype(F32)).astype(BF)
        q1, q2 = load_split(q_s, start)
        k1, k2 = load_split(k_s, start)
        v1, v2 = load_split(v_s, start)
        d1, d2 = load_split(d_s, start)
        for long, (q, k, v, d, p_ref, ds_ref) in (
            (True, (q1, k1, v1, d1, p1_ref, ds1)),
            (False, (q2, k2, v2, d2, p2_ref, ds2)),
        ):
            kt = k.astype(F32).T.astype(BF)
            parts = []
            for at, size in spans(LONG if long else REST):
                dp = dot_nt(v, d[at : at + size]).astype(BF).astype(F32)
                p = p_ref[h, :, at : at + size].astype(F32)
                pd = p * dp
                delta = jnp.sum(pd, axis=0, keepdims=True)
                ds = ((pd - p * delta) * F32(scale)).astype(BF)
                ds_ref[:, at : at + size] = ds
                parts.append(dot_nn(kt, ds).T.astype(BF))
            put(0, long, jnp.concatenate(parts, axis=0))
            put(1, long, dot_nn(ds_ref[...], q).astype(BF))
            put(2, long, dot_nn(p_ref[h], d).astype(BF))
        for which in range(3):
            out_ref[:, which, :, lanes] = g_s[which].reshape(8, 128, HD)
        return carry

    lax.fori_loop(0, 3, head, 0)


def attention_backward(frames, heads, own, other, p1, p2):
    return pl.pallas_call(
        bwd_kernel,
        out_shape=shape((8, 3, 128, 3 * HD)),
        in_specs=[SMEM, VMEM, VMEM, VMEM, VMEM, VMEM],
        out_specs=whole((8, 3, 128, 3 * HD)),
        scratch_shapes=[pltpu.VMEM((1024, HD), BF)] * 4
        + [
            pltpu.VMEM((LONG, LONG), BF),
            pltpu.VMEM((REST, REST), BF),
            pltpu.VMEM((3, 1024, HD), BF),
        ],
        compiler_params=PARAMS,
        cost_estimate=cost(10),
        name="attention_backward",
    )(frames, heads, own, other, p1, p2)


def pack_kernel(in_ref, out_ref):
    for j in range(4):
        out_ref[j] = in_ref[:, :, j * 384 : (j + 1) * 384]


def pack_heads(qkv):
    return pl.pallas_call(
        pack_kernel,
        out_shape=jax.ShapeDtypeStruct((8, 3, 128, 384), BF),
        grid=(2,),
        in_specs=[pl.BlockSpec((3, 128, 1536), lambda j: (0, 0, j))],
        out_specs=pl.BlockSpec((4, 3, 128, 384), lambda j: (j, 0, 0, 0)),
        cost_estimate=cost(3),
        name="pack_heads",
    )(qkv)


def unpack_kernel(in_ref, out_ref):
    for j in range(8):
        out_ref[:, :, j * 384 : (j + 1) * 384] = in_ref[j]


def unpack_heads(grads):
    return pl.pallas_call(
        unpack_kernel,
        out_shape=shape((3, 128, 3072)),
        in_specs=[VMEM],
        out_specs=whole((3, 128, 3072)),
        compiler_params=PARAMS,
        cost_estimate=cost(3),
        name="unpack_heads",
    )(grads)


def gated_kernel(frames_ref, steps_ref, seq_ref, t0_ref, t1_ref, c0_ref, c1_ref, keep_ref, send_ref):
    bins = gate_bins(frames_ref, steps_ref, seq_ref)
    for table_ref, cot_ref, out_ref in ((t0_ref, c0_ref, keep_ref), (t1_ref, c1_ref, send_ref)):
        for k, b in enumerate(bins):
            rows = slice(k * FRAME, (k + 1) * FRAME)
            out_ref[rows, :] = (table_ref[pl.ds(b, 1), :] * cot_ref[rows, :].astype(F32)).astype(BF)


def gated_cotangent(frames, steps, seq, table, cotangent):
    def half(rows, flip):
        return pl.BlockSpec((rows, 768), lambda n, f, t, s: (0, 2 * (s[0] % 2 ^ flip) + n))

    out = pl.BlockSpec((128, 768), lambda n, *_: (0, n))
    return pl.pallas_call(
        gated_kernel,
        out_shape=(jax.ShapeDtypeStruct((128, 1536), BF),) * 2,
        grid_spec=pltpu.PrefetchScalarGridSpec(
            num_scalar_prefetch=3,
            grid=(2,),
            in_specs=[half(64, 0), half(64, 1), half(128, 0), half(128, 1)],
            out_specs=(out, out),
        ),
        cost_estimate=cost(3),
        name="gated_cotangent",
    )(frames, steps, seq, table, table, cotangent, cotangent)


def output_kernel(
    frames_ref, steps_ref, seq_ref, t0_ref, t1_ref, l0_ref, l1_ref, own_ref, other_ref, out_ref
):
    bins = gate_bins(frames_ref, steps_ref, seq_ref)
    z = seq_ref[0] % 2
    halves = ((z, t0_ref, l0_ref, own_ref), (1 - z, t1_ref, l1_ref, other_ref))
    for place, table_ref, lat_ref, proj_ref in halves:
        at = pl.multiple_of(place * 1536, 1536)
        for k, b in enumerate(bins):
            rows = slice(k * FRAME, (k + 1) * FRAME)
            proj = proj_ref[rows, :].astype(F32)
            out = lat_ref[rows, :].astype(F32) + table_ref[pl.ds(b, 1), :] * proj
            out_ref[rows, pl.ds(at, 1536)] = out.astype(BF)


def gated_output(frames, steps, seq, table, latents, own, other):
    def half(rows, flip):
        return pl.BlockSpec((rows, 1536), lambda n, f, t, s: (0, s[0] % 2 ^ flip))

    return pl.pallas_call(
        output_kernel,
        out_shape=jax.ShapeDtypeStruct((128, 3072), BF),
        grid_spec=pltpu.PrefetchScalarGridSpec(
            num_scalar_prefetch=3,
            grid=(1,),
            in_specs=[half(64, 0), half(64, 1), half(128, 0), half(128, 1), VMEM, VMEM],
            out_specs=pl.BlockSpec((128, 3072), lambda n, *_: (0, 0)),
        ),
        cost_estimate=cost(3),
        name="gated_output",
    )(frames, steps, seq, table, table, latents, latents, own, other)


def dattn_kernel(seq_ref, *refs):
    blocks, (w_ref, dproj_ref, other_ref, own_ref) = refs[:8], refs[8:]
    x, z = seq_ref[0] // 2, seq_ref[0] % 2
    for i, block in enumerate(blocks):
        place = 2 * ((x + i // 2) % 4) + (z ^ (i % 2))
        dproj_ref[pl.ds(pl.multiple_of(place * 128, 128), 128), :] = block[...]
    for m in range(2):
        rows = slice(m * 512, (m + 1) * 512)
        d = dproj_ref[rows, :]
        other_ref[rows, :] = dot_nn(d, w_ref[1]).astype(BF)
        own_ref[rows, :] = dot_nn(d, w_ref[0])


def dattn_parts(seq, blocks, weights):
    return pl.pallas_call(
        dattn_kernel,
        out_shape=(
            jax.ShapeDtypeStruct((1024, 1536), BF),
            jax.ShapeDtypeStruct((1024, 384), BF),
            jax.ShapeDtypeStruct((1024, 384), F32),
        ),
        in_specs=[SMEM] + [VMEM] * 9,
        out_specs=(VMEM, whole((1024, 384)), VMEM),
        compiler_params=pltpu.CompilerParams(vmem_limit_bytes=VMEM_LIMIT),
        cost_estimate=cost(7),
        name="dattn_parts",
    )(seq, *blocks, weights)


def project(seq_ref, k, own_ref, other_ref, w_ref):
    rows = pl.ds(pl.multiple_of((seq_ref[0] // 2 + k) % 4 * 256, 256), 256)
    return dot_nt(own_ref[rows, :], w_ref[0]) + dot_nt(other_ref[rows, :], w_ref[1])


def far_kernel(seq_ref, a_ref, b_ref, w_ref, up_ref, down_ref):
    part = project(seq_ref, 2, a_ref, b_ref, w_ref).astype(BF)
    up_ref[...] = part[:128]
    down_ref[...] = part[128:]


def near_kernel(seq_ref, a_ref, b_ref, w_ref, up_ref, down_ref, t1_ref, t3_ref):
    p1 = project(seq_ref, 1, a_ref, b_ref, w_ref)
    t1_ref[:128] = (p1[:128] + up_ref[...].astype(F32)).astype(BF)
    t1_ref[128:] = p1[128:].astype(BF)
    p3 = project(seq_ref, 3, a_ref, b_ref, w_ref)
    t3_ref[:128] = p3[:128].astype(BF)
    t3_ref[128:] = (p3[128:] + down_ref[...].astype(F32)).astype(BF)


def home_kernel(seq_ref, a_ref, b_ref, w_ref, c1_ref, c3_ref, keep_ref, send_ref):
    part = project(seq_ref, 0, a_ref, b_ref, w_ref)
    part = part + c1_ref[...].astype(F32) + c3_ref[...].astype(F32)
    first = seq_ref[0] % 2 == 0
    keep_ref[...] = jnp.where(first, part[:128], part[128:])
    send_ref[...] = jnp.where(first, part[128:], part[:128]).astype(BF)


def project_call(kernel, name, inputs, out_shape, out_specs):
    return pl.pallas_call(
        kernel,
        out_shape=out_shape,
        in_specs=[SMEM] + [VMEM] * inputs,
        out_specs=out_specs,
        compiler_params=PARAMS,
        cost_estimate=cost(3),
        name=name,
    )


def project_far(seq, own, other, weights):
    one = whole((128, 1536))
    call = project_call(far_kernel, "project_far", 3, (shape((128, 1536)),) * 2, (one, one))
    return call(seq, own, other, weights)


def project_near(seq, own, other, weights, up, down):
    two = whole((256, 1536))
    call = project_call(near_kernel, "project_near", 5, (shape((256, 1536)),) * 2, (two, two))
    return call(seq, own, other, weights, up, down)


def project_home(seq, own, other, weights, c1, c3):
    call = project_call(
        home_kernel,
        "project_home",
        5,
        (shape((128, 1536), F32), shape((128, 1536))),
        (VMEM, whole((128, 1536))),
    )
    return call(seq, own, other, weights, c1, c3)


def dweight_kernel(dp_ref, d_ref, a_ref, keep_ref, send_ref):
    even = dp_ref[0] % 2 == 0
    for n in range(2):
        g = dot_tn(d_ref[:, n * 768 : (n + 1) * 768], a_ref[...]).astype(BF)
        for i in range(4):
            p0, p1 = g[i * 192 : i * 192 + 96], g[i * 192 + 96 : i * 192 + 192]
            keep_ref[n * 4 + i] = jnp.where(even, p0, p1)
            send_ref[n * 4 + i] = jnp.where(even, p1, p0)


def dweight_part(dp, dproj, attn):
    return pl.pallas_call(
        dweight_kernel,
        out_shape=(shape((8, 96, 384)), shape((8, 96, 384))),
        in_specs=[SMEM, VMEM, VMEM],
        out_specs=(VMEM, whole((8, 96, 384))),
        compiler_params=PARAMS,
        cost_estimate=cost(4),
        name="dweight_part",
    )(dp, dproj, attn)


def pair_kernel(dp_ref, k0_ref, g0_ref, k1_ref, g1_ref, *out_refs):
    y = dp_ref[0] // 8
    for k, out_ref in enumerate(out_refs):
        at = (y + k) % 4
        for half, (keep_ref, got_ref) in enumerate(((k0_ref, g0_ref), (k1_ref, g1_ref))):

            @pl.when(at // 2 == half)
            def _(keep_ref=keep_ref, got_ref=got_ref, out_ref=out_ref, at=at):
                total = keep_ref[at % 2].astype(F32) + got_ref[at % 2].astype(F32)
                out_ref[...] = total.astype(BF)


def pair_sum(dp, keep0, got0, keep1, got1):
    terms = [t.reshape(2, 4, 96, 384) for t in (keep0, got0, keep1, got1)]
    return pl.pallas_call(
        pair_kernel,
        out_shape=(jax.ShapeDtypeStruct((4, 96, 384), BF),) * 4,
        in_specs=[SMEM] + [VMEM] * 4,
        out_specs=(pl.BlockSpec((4, 96, 384), lambda: (0, 0, 0)),) * 4,
        cost_estimate=cost(3),
        name="pair_sum",
    )(dp, *terms)


def ring_kernel(dp_ref, a_ref, b_ref, c_ref, d_ref, *out_refs):
    zh = dp_ref[0] // 2 % 4
    for k, out_ref in enumerate(out_refs):
        at = (zh + k) % 4
        total = a_ref[at].astype(F32) + b_ref[at].astype(F32)
        out_ref[...] = (total + c_ref[at].astype(F32) + d_ref[at].astype(F32)).astype(BF)


def ring_sum(dp, parts):
    return pl.pallas_call(
        ring_kernel,
        out_shape=(jax.ShapeDtypeStruct((96, 384), BF),) * 4,
        in_specs=[SMEM] + [VMEM] * 4,
        out_specs=(pl.BlockSpec((96, 384), lambda: (0, 0)),) * 4,
        cost_estimate=cost(2),
        name="ring_sum",
    )(dp, *parts)


def piece_moves(dp_count, seq_count):
    half = dp_count // 2
    moves = []
    for dp in range(dp_count):
        for seq in range(seq_count):
            top, z = dp // half, seq % 2
            to_dp = (dp % half) + half * (z ^ top)
            to_seq = seq - z + top
            moves.append((dp * seq_count + seq, to_dp * seq_count + to_seq))
    return moves


def along(x, axis, stride, places):
    size = lax.axis_size(axis)
    moves = []
    for i in range(size):
        at = i // stride % 4
        moves.append((i, i + ((at + places) % 4 - at) * stride))
    return lax.ppermute(x, axis, moves)


def along_x(x, places):
    return along(x, "seq", 2, places)


def along_y(x, places):
    return along(x, "dp", 8, places)


def along_z(x, places):
    return along(x, "dp", 2, places)


def swap_z(x):
    return lax.ppermute(x, "seq", [(i, i ^ 1) for i in range(lax.axis_size("seq"))])


def swap_core(x):
    return lax.ppermute(x, "dp", [(i, i ^ 1) for i in range(lax.axis_size("dp"))])


def body(qkv_input, latents, cotangent, out_weight, gate_table, timesteps, frames):
    seq = lax.axis_index("seq").astype(jnp.int32).reshape(1)
    dp = lax.axis_index("dp").astype(jnp.int32).reshape(1)
    both = ("dp", "seq")
    moves = piece_moves(lax.axis_size("dp"), lax.axis_size("seq"))

    piece = lax.ppermute(out_weight.T, both, moves)
    packed = pack_heads(qkv_input.transpose(1, 0, 2))
    packed, piece, cotangent = lax.optimization_barrier((packed, piece, cotangent))
    weights = lax.all_gather(piece, "dp", axis=0, tiled=True).reshape(2, 1536, 384)
    keep, send = gated_cotangent(frames, timesteps, seq, gate_table, cotangent)
    got = swap_z(send)
    b1_keep, b3_keep = along_x(keep, -1), along_x(keep, 1)
    packed, got, b1_keep, b3_keep = lax.optimization_barrier((packed, got, b1_keep, b3_keep))
    heads = lax.all_to_all(packed, "seq", split_axis=0, concat_axis=0, tiled=True)

    b1 = [b1_keep, along_x(got, -1)]
    b3 = [b3_keep, along_x(got, 1)]
    b2 = [along_x(b3[0], 1), along_x(b1[1], -1)]

    attn, p1, p2 = attention_forward(frames, heads)
    attn_other = swap_z(attn)
    dproj, d_send, d_own = dattn_parts(seq, [keep, got, *b1, *b2, *b3], weights)
    d_recv = swap_z(d_send)
    keep0, send0 = dweight_part(dp, dproj, attn)
    attn_other, keep0 = lax.optimization_barrier((attn_other, keep0))
    got0 = swap_core(send0)
    up, down = project_far(seq, attn, attn_other, weights)
    behind, _ = lax.optimization_barrier((dproj, up))
    keep1, send1 = dweight_part(dp, behind, attn_other)
    got1 = swap_core(send1)
    up, down = along_x(up, 1), along_x(down, -1)
    up, keep1 = lax.optimization_barrier((up, keep1))
    t1, t3 = project_near(seq, attn, attn_other, weights, up, down)
    d_own, d_recv, t1, t3 = lax.optimization_barrier((d_own, d_recv, t1, t3))
    c1, c3 = along_x(t1, 1), along_x(t3, -1)
    terms = pair_sum(dp, keep0, got0, keep1, got1)

    grads = attention_backward(frames, heads, d_own, d_recv, p1, p2)
    grads, c1, c3, terms = lax.optimization_barrier((grads, c1, c3, terms))
    grads = lax.all_to_all(grads, "seq", split_axis=0, concat_axis=0, tiled=True)
    terms = [terms[0]] + [along_y(terms[k], k) for k in range(1, 4)]

    o_keep, o_send = project_home(seq, attn, attn_other, weights, c1, c3)
    terms, o_send = lax.optimization_barrier((terms, o_send))
    terms = ring_sum(dp, terms)
    terms = [terms[0]] + [along_z(terms[k], k) for k in range(1, 4)]
    total = terms[0].astype(F32) + terms[1].astype(F32)
    total = total + terms[2].astype(F32) + terms[3].astype(F32)
    total = lax.ppermute(total, both, [(b, a) for a, b in moves])
    o_got = swap_z(o_send)
    grad_qkv = unpack_heads(grads)
    grad_qkv, o_got = lax.optimization_barrier((grad_qkv, o_got))
    output = gated_output(frames, timesteps, seq, gate_table, latents, o_keep, o_got)
    return (output, grad_qkv.transpose(1, 0, 2), total.T)


def solution(mesh):
    placed = (
        P(("dp", "seq"), None, None),
        P(("dp", "seq"), None),
        P(("dp", "seq"), None),
        P("seq", "dp"),
        P(),
        P("dp", None),
        P("dp", None),
    )
    return jax.shard_map(
        body,
        mesh=mesh,
        in_specs=placed,
        out_specs=(P(("dp", "seq"), None), P(("dp", "seq"), None, None), P("seq", "dp")),
        check_vma=False,
    )
```

```python
import jax
import jax.numpy as jnp
from jax import lax
from jax.experimental import pallas as pl
from jax.experimental.pallas import tpu as pltpu
from jax.sharding import PartitionSpec as P

HD = 128
FRAME = 64
LONG = 640
REST = 384
LOG2E = 1.4426950408889634
VMEM_LIMIT = 32 * 1024 * 1024

BF = jnp.bfloat16
F32 = jnp.float32
VMEM = pl.BlockSpec(memory_space=pltpu.VMEM)
SMEM = pl.BlockSpec(memory_space=pltpu.SMEM)
PARAMS = pltpu.CompilerParams(vmem_limit_bytes=VMEM_LIMIT)


def shape(dims, dtype=BF):
    return jax.ShapeDtypeStruct(dims, dtype)


def whole(dims):
    return pl.BlockSpec(dims, lambda: (0,) * len(dims))


def cost(us):
    return pl.CostEstimate(flops=int(us * 1e9), transcendentals=0, bytes_accessed=int(us * 3e6))


def dot_nt(a, b):
    return lax.dot_general(a, b, (((1,), (1,)), ((), ())), preferred_element_type=F32)


def dot_nn(a, b):
    return lax.dot_general(a, b, (((1,), (0,)), ((), ())), preferred_element_type=F32)


def dot_tn(a, b):
    return lax.dot_general(a, b, (((0,), (0,)), ((), ())), preferred_element_type=F32)


def clip_places(frames_ref):
    f0, f1, f2 = frames_ref[0, 0], frames_ref[0, 1], frames_ref[0, 2]
    first = jnp.logical_and(f0 > f1, f0 > f2)
    second = f1 > f2
    start = jnp.where(first, 0, jnp.where(second, f0, f0 + f1)) * FRAME
    lead = jnp.where(first, f1, f0)
    return start, lead


def gate_bins(frames_ref, steps_ref, seq_ref):
    f0, f1 = frames_ref[0, 0], frames_ref[0, 1]
    bins = []
    for k in range(2):
        frame = seq_ref[0] * 2 + k
        clip = jnp.where(frame >= f0, 1, 0) + jnp.where(frame >= f0 + f1, 1, 0)
        bins.append(steps_ref[0, clip])
    return bins


def spans(total):
    out, at = [], 0
    while at < total:
        size = min(128, total - at)
        out.append((at, size))
        at += size
    return out


def rest_places(start):
    return [
        pl.multiple_of(jnp.where(t * FRAME >= start, t * FRAME + LONG, t * FRAME), FRAME)
        for t in range(REST // FRAME)
    ]


def load_split(src, start):
    main = src[pl.ds(start, LONG), :]
    rest = jnp.concatenate([src[pl.ds(p, FRAME), :] for p in rest_places(start)], axis=0)
    return main, rest


def rest_mask(lead, at, size):
    rows = lax.broadcasted_iota(jnp.int32, (REST, size), 0)
    cols = lax.broadcasted_iota(jnp.int32, (REST, size), 1) + at
    edge = lead * FRAME
    return (rows < edge) == (cols < edge)


def fwd_kernel(frames_ref, qkv_ref, attn_ref, p1_ref, p2_ref, q_s, k_s, v_s):
    start, lead = clip_places(frames_ref)
    start = pl.multiple_of(start, FRAME)
    places = rest_places(start)
    factor = LOG2E / (HD**0.5)

    def head(h, carry):
        lanes = pl.ds(pl.multiple_of(h * HD, HD), HD)
        q_s[...] = qkv_ref[:, 0, :, lanes].reshape(1024, HD)
        k_s[...] = qkv_ref[:, 1, :, lanes].reshape(1024, HD)
        v_s[...] = qkv_ref[:, 2, :, lanes].reshape(1024, HD)
        q1, q2 = load_split(q_s, start)
        k1, k2 = load_split(k_s, start)
        v1, v2 = load_split(v_s, start)
        for long, (q, k, v, p_ref) in ((True, (q1, k1, v1, p1_ref)), (False, (q2, k2, v2, p2_ref))):
            vt = v.astype(F32).T.astype(BF)
            for at, size in spans(LONG if long else REST):
                s = dot_nt(k, q[at : at + size])
                if not long:
                    s = jnp.where(rest_mask(lead, at, size), s, F32(-1e30))
                top = jnp.max(s, axis=0, keepdims=True)
                e = jnp.exp2((s - top) * F32(factor))
                total = jnp.sum(e, axis=0, keepdims=True)
                p = (e * (1.0 / total)).astype(BF)
                p_ref[h, :, at : at + size] = p
                o = dot_nn(vt, p).T.astype(BF)
                if long:
                    attn_ref[pl.ds(start + at, size), lanes] = o
                else:
                    for t in range(size // FRAME):
                        attn_ref[pl.ds(places[at // FRAME + t], FRAME), lanes] = o[
                            t * FRAME : (t + 1) * FRAME
                        ]
        return carry

    lax.fori_loop(0, 3, head, 0)


def attention_forward(frames, heads):
    return pl.pallas_call(
        fwd_kernel,
        out_shape=(shape((1024, 3 * HD)), shape((3, LONG, LONG)), shape((3, REST, REST))),
        in_specs=[SMEM, VMEM],
        out_specs=(whole((1024, 3 * HD)), VMEM, VMEM),
        scratch_shapes=[pltpu.VMEM((1024, HD), BF)] * 3,
        compiler_params=PARAMS,
        cost_estimate=cost(0.1),
        name="attention_forward",
    )(frames, heads)


def bwd_kernel(
    frames_ref, qkv_ref, own_ref, other_ref, p1_ref, p2_ref, out_ref, q_s, k_s, v_s, d_s, ds1, ds2, g_s
):
    start, lead = clip_places(frames_ref)
    start = pl.multiple_of(start, FRAME)
    places = rest_places(start)
    scale = 1.0 / (HD**0.5)

    def put(which, long, value):
        if long:
            g_s[which, pl.ds(start, LONG), :] = value
        else:
            for t in range(REST // FRAME):
                g_s[which, pl.ds(places[t], FRAME), :] = value[t * FRAME : (t + 1) * FRAME]

    def head(h, carry):
        lanes = pl.ds(pl.multiple_of(h * HD, HD), HD)
        q_s[...] = qkv_ref[:, 0, :, lanes].reshape(1024, HD)
        k_s[...] = qkv_ref[:, 1, :, lanes].reshape(1024, HD)
        v_s[...] = qkv_ref[:, 2, :, lanes].reshape(1024, HD)
        d_s[...] = (own_ref[:, lanes] + other_ref[:, lanes].astype(F32)).astype(BF)
        q1, q2 = load_split(q_s, start)
        k1, k2 = load_split(k_s, start)
        v1, v2 = load_split(v_s, start)
        d1, d2 = load_split(d_s, start)
        for long, (q, k, v, d, p_ref, ds_ref) in (
            (True, (q1, k1, v1, d1, p1_ref, ds1)),
            (False, (q2, k2, v2, d2, p2_ref, ds2)),
        ):
            kt = k.astype(F32).T.astype(BF)
            parts = []
            for at, size in spans(LONG if long else REST):
                dp = dot_nt(v, d[at : at + size]).astype(BF).astype(F32)
                p = p_ref[h, :, at : at + size].astype(F32)
                pd = p * dp
                delta = jnp.sum(pd, axis=0, keepdims=True)
                ds = ((pd - p * delta) * F32(scale)).astype(BF)
                ds_ref[:, at : at + size] = ds
                parts.append(dot_nn(kt, ds).T.astype(BF))
            put(0, long, jnp.concatenate(parts, axis=0))
            put(1, long, dot_nn(ds_ref[...], q).astype(BF))
            put(2, long, dot_nn(p_ref[h], d).astype(BF))
        for which in range(3):
            out_ref[:, which, :, lanes] = g_s[which].reshape(8, 128, HD)
        return carry

    lax.fori_loop(0, 3, head, 0)


def attention_backward(frames, heads, own, other, p1, p2):
    return pl.pallas_call(
        bwd_kernel,
        out_shape=shape((8, 3, 128, 3 * HD)),
        in_specs=[SMEM, VMEM, VMEM, VMEM, VMEM, VMEM],
        out_specs=whole((8, 3, 128, 3 * HD)),
        scratch_shapes=[pltpu.VMEM((1024, HD), BF)] * 4
        + [
            pltpu.VMEM((LONG, LONG), BF),
            pltpu.VMEM((REST, REST), BF),
            pltpu.VMEM((3, 1024, HD), BF),
        ],
        compiler_params=PARAMS,
        cost_estimate=cost(10),
        name="attention_backward",
    )(frames, heads, own, other, p1, p2)


def pack_kernel(in_ref, out_ref):
    for j in range(4):
        out_ref[j] = in_ref[:, :, j * 384 : (j + 1) * 384]


def pack_heads(qkv):
    return pl.pallas_call(
        pack_kernel,
        out_shape=jax.ShapeDtypeStruct((8, 3, 128, 384), BF),
        grid=(2,),
        in_specs=[pl.BlockSpec((3, 128, 1536), lambda j: (0, 0, j))],
        out_specs=pl.BlockSpec((4, 3, 128, 384), lambda j: (j, 0, 0, 0)),
        cost_estimate=cost(3),
        name="pack_heads",
    )(qkv)


def unpack_kernel(in_ref, out_ref):
    for j in range(8):
        out_ref[:, :, j * 384 : (j + 1) * 384] = in_ref[j]


def unpack_heads(grads):
    return pl.pallas_call(
        unpack_kernel,
        out_shape=shape((3, 128, 3072)),
        in_specs=[VMEM],
        out_specs=whole((3, 128, 3072)),
        compiler_params=PARAMS,
        cost_estimate=cost(3),
        name="unpack_heads",
    )(grads)


def gated_kernel(frames_ref, steps_ref, seq_ref, t0_ref, t1_ref, c0_ref, c1_ref, keep_ref, send_ref):
    bins = gate_bins(frames_ref, steps_ref, seq_ref)
    for table_ref, cot_ref, out_ref in ((t0_ref, c0_ref, keep_ref), (t1_ref, c1_ref, send_ref)):
        for k, b in enumerate(bins):
            rows = slice(k * FRAME, (k + 1) * FRAME)
            out_ref[rows, :] = (table_ref[pl.ds(b, 1), :] * cot_ref[rows, :].astype(F32)).astype(BF)


def gated_cotangent(frames, steps, seq, table, cotangent):
    def half(rows, flip):
        return pl.BlockSpec((rows, 768), lambda n, f, t, s: (0, 2 * (s[0] % 2 ^ flip) + n))

    out = pl.BlockSpec((128, 768), lambda n, *_: (0, n))
    return pl.pallas_call(
        gated_kernel,
        out_shape=(jax.ShapeDtypeStruct((128, 1536), BF),) * 2,
        grid_spec=pltpu.PrefetchScalarGridSpec(
            num_scalar_prefetch=3,
            grid=(2,),
            in_specs=[half(64, 0), half(64, 1), half(128, 0), half(128, 1)],
            out_specs=(out, out),
        ),
        cost_estimate=cost(3),
        name="gated_cotangent",
    )(frames, steps, seq, table, table, cotangent, cotangent)


def output_kernel(
    frames_ref, steps_ref, seq_ref, t0_ref, t1_ref, l0_ref, l1_ref, own_ref, other_ref, out_ref
):
    bins = gate_bins(frames_ref, steps_ref, seq_ref)
    z = seq_ref[0] % 2
    halves = ((z, t0_ref, l0_ref, own_ref), (1 - z, t1_ref, l1_ref, other_ref))
    for place, table_ref, lat_ref, proj_ref in halves:
        at = pl.multiple_of(place * 1536, 1536)
        for k, b in enumerate(bins):
            rows = slice(k * FRAME, (k + 1) * FRAME)
            proj = proj_ref[rows, :].astype(F32)
            out = lat_ref[rows, :].astype(F32) + table_ref[pl.ds(b, 1), :] * proj
            out_ref[rows, pl.ds(at, 1536)] = out.astype(BF)


def gated_output(frames, steps, seq, table, latents, own, other):
    def half(rows, flip):
        return pl.BlockSpec((rows, 1536), lambda n, f, t, s: (0, s[0] % 2 ^ flip))

    return pl.pallas_call(
        output_kernel,
        out_shape=jax.ShapeDtypeStruct((128, 3072), BF),
        grid_spec=pltpu.PrefetchScalarGridSpec(
            num_scalar_prefetch=3,
            grid=(1,),
            in_specs=[half(64, 0), half(64, 1), half(128, 0), half(128, 1), VMEM, VMEM],
            out_specs=pl.BlockSpec((128, 3072), lambda n, *_: (0, 0)),
        ),
        cost_estimate=cost(3),
        name="gated_output",
    )(frames, steps, seq, table, table, latents, latents, own, other)


def dattn_kernel(seq_ref, *refs):
    blocks, (w_ref, dproj_ref, other_ref, own_ref) = refs[:8], refs[8:]
    x, z = seq_ref[0] // 2, seq_ref[0] % 2
    for i, block in enumerate(blocks):
        place = 2 * ((x + i // 2) % 4) + (z ^ (i % 2))
        dproj_ref[pl.ds(pl.multiple_of(place * 128, 128), 128), :] = block[...]
    for m in range(2):
        rows = slice(m * 512, (m + 1) * 512)
        d = dproj_ref[rows, :]
        other_ref[rows, :] = dot_nn(d, w_ref[1]).astype(BF)
        own_ref[rows, :] = dot_nn(d, w_ref[0])


def dattn_parts(seq, blocks, weights):
    return pl.pallas_call(
        dattn_kernel,
        out_shape=(
            jax.ShapeDtypeStruct((1024, 1536), BF),
            jax.ShapeDtypeStruct((1024, 384), BF),
            jax.ShapeDtypeStruct((1024, 384), F32),
        ),
        in_specs=[SMEM] + [VMEM] * 9,
        out_specs=(VMEM, whole((1024, 384)), VMEM),
        compiler_params=PARAMS,
        cost_estimate=cost(7),
        name="dattn_parts",
    )(seq, *blocks, weights)


def project(seq_ref, k, own_ref, other_ref, w_ref):
    rows = pl.ds(pl.multiple_of((seq_ref[0] // 2 + k) % 4 * 256, 256), 256)
    return dot_nt(own_ref[rows, :], w_ref[0]) + dot_nt(other_ref[rows, :], w_ref[1])


def far_kernel(seq_ref, a_ref, b_ref, w_ref, up_ref, down_ref):
    part = project(seq_ref, 2, a_ref, b_ref, w_ref).astype(BF)
    up_ref[...] = part[:128]
    down_ref[...] = part[128:]


def near_kernel(seq_ref, a_ref, b_ref, w_ref, up_ref, down_ref, t1_ref, t3_ref):
    p1 = project(seq_ref, 1, a_ref, b_ref, w_ref)
    t1_ref[:128] = (p1[:128] + up_ref[...].astype(F32)).astype(BF)
    t1_ref[128:] = p1[128:].astype(BF)
    p3 = project(seq_ref, 3, a_ref, b_ref, w_ref)
    t3_ref[:128] = p3[:128].astype(BF)
    t3_ref[128:] = (p3[128:] + down_ref[...].astype(F32)).astype(BF)


def home_kernel(seq_ref, a_ref, b_ref, w_ref, c1_ref, c3_ref, keep_ref, send_ref):
    part = project(seq_ref, 0, a_ref, b_ref, w_ref)
    part = part + c1_ref[...].astype(F32) + c3_ref[...].astype(F32)
    first = seq_ref[0] % 2 == 0
    keep_ref[...] = jnp.where(first, part[:128], part[128:])
    send_ref[...] = jnp.where(first, part[128:], part[:128]).astype(BF)


def project_call(kernel, name, inputs, out_shape, out_specs):
    return pl.pallas_call(
        kernel,
        out_shape=out_shape,
        in_specs=[SMEM] + [VMEM] * inputs,
        out_specs=out_specs,
        compiler_params=PARAMS,
        cost_estimate=cost(3),
        name=name,
    )


def project_far(seq, own, other, weights):
    one = whole((128, 1536))
    call = project_call(far_kernel, "project_far", 3, (shape((128, 1536)),) * 2, (one, one))
    return call(seq, own, other, weights)


def project_near(seq, own, other, weights, up, down):
    two = whole((256, 1536))
    call = project_call(near_kernel, "project_near", 5, (shape((256, 1536)),) * 2, (two, two))
    return call(seq, own, other, weights, up, down)


def project_home(seq, own, other, weights, c1, c3):
    call = project_call(
        home_kernel,
        "project_home",
        5,
        (shape((128, 1536), F32), shape((128, 1536))),
        (VMEM, whole((128, 1536))),
    )
    return call(seq, own, other, weights, c1, c3)


def dweight_kernel(dp_ref, d_ref, a_ref, keep_ref, send_ref):
    even = dp_ref[0] % 2 == 0
    for n in range(2):
        g = dot_tn(d_ref[:, n * 768 : (n + 1) * 768], a_ref[...]).astype(BF)
        for i in range(4):
            p0, p1 = g[i * 192 : i * 192 + 96], g[i * 192 + 96 : i * 192 + 192]
            keep_ref[n * 4 + i] = jnp.where(even, p0, p1)
            send_ref[n * 4 + i] = jnp.where(even, p1, p0)


def dweight_part(dp, dproj, attn):
    return pl.pallas_call(
        dweight_kernel,
        out_shape=(shape((8, 96, 384)), shape((8, 96, 384))),
        in_specs=[SMEM, VMEM, VMEM],
        out_specs=(VMEM, whole((8, 96, 384))),
        compiler_params=PARAMS,
        cost_estimate=cost(4),
        name="dweight_part",
    )(dp, dproj, attn)


def pair_kernel(dp_ref, k0_ref, g0_ref, k1_ref, g1_ref, *out_refs):
    y = dp_ref[0] // 8
    for k, out_ref in enumerate(out_refs):
        at = (y + k) % 4
        for half, (keep_ref, got_ref) in enumerate(((k0_ref, g0_ref), (k1_ref, g1_ref))):

            @pl.when(at // 2 == half)
            def _(keep_ref=keep_ref, got_ref=got_ref, out_ref=out_ref, at=at):
                total = keep_ref[at % 2].astype(F32) + got_ref[at % 2].astype(F32)
                out_ref[...] = total.astype(BF)


def pair_sum(dp, keep0, got0, keep1, got1):
    terms = [t.reshape(2, 4, 96, 384) for t in (keep0, got0, keep1, got1)]
    return pl.pallas_call(
        pair_kernel,
        out_shape=(jax.ShapeDtypeStruct((4, 96, 384), BF),) * 4,
        in_specs=[SMEM] + [VMEM] * 4,
        out_specs=(pl.BlockSpec((4, 96, 384), lambda: (0, 0, 0)),) * 4,
        compiler_params=PARAMS,
        cost_estimate=cost(3),
        name="pair_sum",
    )(dp, *terms)


def ring_kernel(dp_ref, a_ref, b_ref, c_ref, d_ref, *out_refs):
    zh = dp_ref[0] // 2 % 4
    for k, out_ref in enumerate(out_refs):
        at = (zh + k) % 4
        total = a_ref[at].astype(F32) + b_ref[at].astype(F32)
        out_ref[...] = (total + c_ref[at].astype(F32) + d_ref[at].astype(F32)).astype(BF)


def ring_sum(dp, parts):
    return pl.pallas_call(
        ring_kernel,
        out_shape=(jax.ShapeDtypeStruct((96, 384), BF),) * 4,
        in_specs=[SMEM] + [VMEM] * 4,
        out_specs=(pl.BlockSpec((96, 384), lambda: (0, 0)),) * 4,
        compiler_params=PARAMS,
        cost_estimate=cost(2),
        name="ring_sum",
    )(dp, *parts)


def piece_moves(dp_count, seq_count):
    half = dp_count // 2
    moves = []
    for dp in range(dp_count):
        for seq in range(seq_count):
            top, z = dp // half, seq % 2
            to_dp = (dp % half) + half * (z ^ top)
            to_seq = seq - z + top
            moves.append((dp * seq_count + seq, to_dp * seq_count + to_seq))
    return moves


def along(x, axis, stride, places):
    size = lax.axis_size(axis)
    moves = []
    for i in range(size):
        at = i // stride % 4
        moves.append((i, i + ((at + places) % 4 - at) * stride))
    return lax.ppermute(x, axis, moves)


def along_x(x, places):
    return along(x, "seq", 2, places)


def along_y(x, places):
    return along(x, "dp", 8, places)


def along_z(x, places):
    return along(x, "dp", 2, places)


def swap_z(x):
    return lax.ppermute(x, "seq", [(i, i ^ 1) for i in range(lax.axis_size("seq"))])


def swap_core(x):
    return lax.ppermute(x, "dp", [(i, i ^ 1) for i in range(lax.axis_size("dp"))])


def body(qkv_input, latents, cotangent, out_weight, gate_table, timesteps, frames):
    seq = lax.axis_index("seq").astype(jnp.int32).reshape(1)
    dp = lax.axis_index("dp").astype(jnp.int32).reshape(1)
    both = ("dp", "seq")
    moves = piece_moves(lax.axis_size("dp"), lax.axis_size("seq"))

    piece = lax.ppermute(out_weight.T, both, moves)
    keep, send = gated_cotangent(frames, timesteps, seq, gate_table, cotangent)
    qkv_input, piece, keep, send = lax.optimization_barrier((qkv_input, piece, keep, send))
    weights = lax.all_gather(piece, "dp", axis=0, tiled=True).reshape(2, 1536, 384)
    got = swap_z(send)
    b1_keep, b3_keep = along_x(keep, -1), along_x(keep, 1)
    packed = pack_heads(qkv_input.transpose(1, 0, 2))
    packed, got, b1_keep, b3_keep = lax.optimization_barrier((packed, got, b1_keep, b3_keep))
    heads = lax.all_to_all(packed, "seq", split_axis=0, concat_axis=0, tiled=True)

    b1 = [b1_keep, along_x(got, -1)]
    b3 = [b3_keep, along_x(got, 1)]
    b2 = [along_x(b3[0], 1), along_x(b1[1], -1)]

    attn, p1, p2 = attention_forward(frames, heads)
    attn_other = swap_z(attn)
    dproj, d_send, d_own = dattn_parts(seq, [keep, got, *b1, *b2, *b3], weights)
    d_recv = swap_z(d_send)
    keep0, send0 = dweight_part(dp, dproj, attn)
    attn_other, keep0 = lax.optimization_barrier((attn_other, keep0))
    got0 = swap_core(send0)
    up, down = project_far(seq, attn, attn_other, weights)
    behind, _ = lax.optimization_barrier((dproj, up))
    keep1, send1 = dweight_part(dp, behind, attn_other)
    got1 = swap_core(send1)
    up, down = along_x(up, 1), along_x(down, -1)
    up, keep1 = lax.optimization_barrier((up, keep1))
    t1, t3 = project_near(seq, attn, attn_other, weights, up, down)
    d_own, d_recv, t1, t3 = lax.optimization_barrier((d_own, d_recv, t1, t3))
    c1, c3 = along_x(t1, 1), along_x(t3, -1)
    terms = pair_sum(dp, keep0, got0, keep1, got1)
    d_own, terms = lax.optimization_barrier((d_own, terms))
    terms = [terms[0]] + [along_y(terms[k], k) for k in range(1, 4)]

    grads = attention_backward(frames, heads, d_own, d_recv, p1, p2)
    grads, c1, c3 = lax.optimization_barrier((grads, c1, c3))
    grads = lax.all_to_all(grads, "seq", split_axis=0, concat_axis=0, tiled=True)

    o_keep, o_send = project_home(seq, attn, attn_other, weights, c1, c3)
    o_got = swap_z(o_send)
    terms, o_keep = lax.optimization_barrier((terms, o_keep))
    terms = ring_sum(dp, terms)
    terms = [terms[0]] + [along_z(terms[k], k) for k in range(1, 4)]
    output = gated_output(frames, timesteps, seq, gate_table, latents, o_keep, o_got)
    terms, output = lax.optimization_barrier((terms, output))
    total = terms[0].astype(F32) + terms[1].astype(F32)
    total = total + terms[2].astype(F32) + terms[3].astype(F32)
    total = lax.ppermute(total, both, [(b, a) for a, b in moves])
    grad_qkv = unpack_heads(grads)
    return (output, grad_qkv.transpose(1, 0, 2), total.T)


def solution(mesh):
    placed = (
        P(("dp", "seq"), None, None),
        P(("dp", "seq"), None),
        P(("dp", "seq"), None),
        P("seq", "dp"),
        P(),
        P("dp", None),
        P("dp", None),
    )
    return jax.shard_map(
        body,
        mesh=mesh,
        in_specs=placed,
        out_specs=(P(("dp", "seq"), None), P(("dp", "seq"), None, None), P("seq", "dp")),
        check_vma=False,
    )
```

```python
import jax
import jax.numpy as jnp
from jax import lax
from jax.experimental import pallas as pl
from jax.experimental.pallas import tpu as pltpu
from jax.sharding import PartitionSpec as P

HD = 128
FRAME = 64
LONG = 640
REST = 384
LOG2E = 1.4426950408889634
VMEM_LIMIT = 32 * 1024 * 1024

BF = jnp.bfloat16
F32 = jnp.float32
VMEM = pl.BlockSpec(memory_space=pltpu.VMEM)
SMEM = pl.BlockSpec(memory_space=pltpu.SMEM)
PARAMS = pltpu.CompilerParams(vmem_limit_bytes=VMEM_LIMIT)


def shape(dims, dtype=BF):
    return jax.ShapeDtypeStruct(dims, dtype)


def whole(dims):
    return pl.BlockSpec(dims, lambda: (0,) * len(dims))


def cost(us):
    return pl.CostEstimate(flops=int(us * 1e9), transcendentals=0, bytes_accessed=int(us * 3e6))


def dot_nt(a, b):
    return lax.dot_general(a, b, (((1,), (1,)), ((), ())), preferred_element_type=F32)


def dot_nn(a, b):
    return lax.dot_general(a, b, (((1,), (0,)), ((), ())), preferred_element_type=F32)


def dot_tn(a, b):
    return lax.dot_general(a, b, (((0,), (0,)), ((), ())), preferred_element_type=F32)


def clip_places(frames_ref):
    f0, f1, f2 = frames_ref[0, 0], frames_ref[0, 1], frames_ref[0, 2]
    first = jnp.logical_and(f0 > f1, f0 > f2)
    second = f1 > f2
    start = jnp.where(first, 0, jnp.where(second, f0, f0 + f1)) * FRAME
    lead = jnp.where(first, f1, f0)
    return start, lead


def gate_bins(frames_ref, steps_ref, seq_ref):
    f0, f1 = frames_ref[0, 0], frames_ref[0, 1]
    bins = []
    for k in range(2):
        frame = seq_ref[0] * 2 + k
        clip = jnp.where(frame >= f0, 1, 0) + jnp.where(frame >= f0 + f1, 1, 0)
        bins.append(steps_ref[0, clip])
    return bins


def spans(total):
    out, at = [], 0
    while at < total:
        size = min(128, total - at)
        out.append((at, size))
        at += size
    return out


def rest_places(start):
    return [
        pl.multiple_of(jnp.where(t * FRAME >= start, t * FRAME + LONG, t * FRAME), FRAME)
        for t in range(REST // FRAME)
    ]


def load_split(src, start):
    main = src[pl.ds(start, LONG), :]
    rest = jnp.concatenate([src[pl.ds(p, FRAME), :] for p in rest_places(start)], axis=0)
    return main, rest


def rest_mask(lead, at, size):
    rows = lax.broadcasted_iota(jnp.int32, (REST, size), 0)
    cols = lax.broadcasted_iota(jnp.int32, (REST, size), 1) + at
    edge = lead * FRAME
    return (rows < edge) == (cols < edge)


def fwd_kernel(frames_ref, qkv_ref, attn_ref, p1_ref, p2_ref, q_s, k_s, v_s):
    start, lead = clip_places(frames_ref)
    start = pl.multiple_of(start, FRAME)
    places = rest_places(start)
    factor = LOG2E / (HD**0.5)

    def head(h, carry):
        lanes = pl.ds(pl.multiple_of(h * HD, HD), HD)
        q_s[...] = qkv_ref[:, 0, :, lanes].reshape(1024, HD)
        k_s[...] = qkv_ref[:, 1, :, lanes].reshape(1024, HD)
        v_s[...] = qkv_ref[:, 2, :, lanes].reshape(1024, HD)
        q1, q2 = load_split(q_s, start)
        k1, k2 = load_split(k_s, start)
        v1, v2 = load_split(v_s, start)
        for long, (q, k, v, p_ref) in ((True, (q1, k1, v1, p1_ref)), (False, (q2, k2, v2, p2_ref))):
            vt = v.astype(F32).T.astype(BF)
            for at, size in spans(LONG if long else REST):
                s = dot_nt(k, q[at : at + size])
                if not long:
                    s = jnp.where(rest_mask(lead, at, size), s, F32(-1e30))
                top = jnp.max(s, axis=0, keepdims=True)
                e = jnp.exp2((s - top) * F32(factor))
                total = jnp.sum(e, axis=0, keepdims=True)
                p = (e * (1.0 / total)).astype(BF)
                p_ref[h, :, at : at + size] = p
                o = dot_nn(vt, p).T.astype(BF)
                if long:
                    attn_ref[pl.ds(start + at, size), lanes] = o
                else:
                    for t in range(size // FRAME):
                        attn_ref[pl.ds(places[at // FRAME + t], FRAME), lanes] = o[
                            t * FRAME : (t + 1) * FRAME
                        ]
        return carry

    lax.fori_loop(0, 3, head, 0)


def attention_forward(frames, heads):
    return pl.pallas_call(
        fwd_kernel,
        out_shape=(shape((1024, 3 * HD)), shape((3, LONG, LONG)), shape((3, REST, REST))),
        in_specs=[SMEM, VMEM],
        out_specs=(whole((1024, 3 * HD)), VMEM, VMEM),
        scratch_shapes=[pltpu.VMEM((1024, HD), BF)] * 3,
        compiler_params=PARAMS,
        cost_estimate=cost(0.1),
        name="attention_forward",
    )(frames, heads)


def bwd_kernel(
    frames_ref, qkv_ref, own_ref, other_ref, p1_ref, p2_ref, out_ref, q_s, k_s, v_s, d_s, ds1, ds2, g_s
):
    start, lead = clip_places(frames_ref)
    start = pl.multiple_of(start, FRAME)
    places = rest_places(start)
    scale = 1.0 / (HD**0.5)

    def put(which, long, value):
        if long:
            g_s[which, pl.ds(start, LONG), :] = value
        else:
            for t in range(REST // FRAME):
                g_s[which, pl.ds(places[t], FRAME), :] = value[t * FRAME : (t + 1) * FRAME]

    def head(h, carry):
        lanes = pl.ds(pl.multiple_of(h * HD, HD), HD)
        q_s[...] = qkv_ref[:, 0, :, lanes].reshape(1024, HD)
        k_s[...] = qkv_ref[:, 1, :, lanes].reshape(1024, HD)
        v_s[...] = qkv_ref[:, 2, :, lanes].reshape(1024, HD)
        d_s[...] = (own_ref[:, lanes] + other_ref[:, lanes].astype(F32)).astype(BF)
        q1, q2 = load_split(q_s, start)
        k1, k2 = load_split(k_s, start)
        v1, v2 = load_split(v_s, start)
        d1, d2 = load_split(d_s, start)
        for long, (q, k, v, d, p_ref, ds_ref) in (
            (True, (q1, k1, v1, d1, p1_ref, ds1)),
            (False, (q2, k2, v2, d2, p2_ref, ds2)),
        ):
            kt = k.astype(F32).T.astype(BF)
            parts = []
            for at, size in spans(LONG if long else REST):
                dp = dot_nt(v, d[at : at + size]).astype(BF).astype(F32)
                p = p_ref[h, :, at : at + size].astype(F32)
                pd = p * dp
                delta = jnp.sum(pd, axis=0, keepdims=True)
                ds = ((pd - p * delta) * F32(scale)).astype(BF)
                ds_ref[:, at : at + size] = ds
                parts.append(dot_nn(kt, ds).T.astype(BF))
            put(0, long, jnp.concatenate(parts, axis=0))
            put(1, long, dot_nn(ds_ref[...], q).astype(BF))
            put(2, long, dot_nn(p_ref[h], d).astype(BF))
        for which in range(3):
            out_ref[:, which, :, lanes] = g_s[which].reshape(8, 128, HD)
        return carry

    lax.fori_loop(0, 3, head, 0)


def attention_backward(frames, heads, own, other, p1, p2):
    return pl.pallas_call(
        bwd_kernel,
        out_shape=shape((8, 3, 128, 3 * HD)),
        in_specs=[SMEM, VMEM, VMEM, VMEM, VMEM, VMEM],
        out_specs=whole((8, 3, 128, 3 * HD)),
        scratch_shapes=[pltpu.VMEM((1024, HD), BF)] * 4
        + [
            pltpu.VMEM((LONG, LONG), BF),
            pltpu.VMEM((REST, REST), BF),
            pltpu.VMEM((3, 1024, HD), BF),
        ],
        compiler_params=PARAMS,
        cost_estimate=cost(10),
        name="attention_backward",
    )(frames, heads, own, other, p1, p2)


def pack_kernel(in_ref, out_ref):
    for j in range(4):
        out_ref[j] = in_ref[:, :, j * 384 : (j + 1) * 384]


def pack_heads(qkv):
    return pl.pallas_call(
        pack_kernel,
        out_shape=jax.ShapeDtypeStruct((8, 3, 128, 384), BF),
        grid=(2,),
        in_specs=[pl.BlockSpec((3, 128, 1536), lambda j: (0, 0, j))],
        out_specs=pl.BlockSpec((4, 3, 128, 384), lambda j: (j, 0, 0, 0)),
        cost_estimate=cost(3),
        name="pack_heads",
    )(qkv)


def unpack_kernel(in_ref, out_ref):
    for j in range(8):
        out_ref[:, :, j * 384 : (j + 1) * 384] = in_ref[j]


def unpack_heads(grads):
    return pl.pallas_call(
        unpack_kernel,
        out_shape=shape((3, 128, 3072)),
        in_specs=[VMEM],
        out_specs=whole((3, 128, 3072)),
        compiler_params=PARAMS,
        cost_estimate=cost(3),
        name="unpack_heads",
    )(grads)


def gated_kernel(frames_ref, steps_ref, seq_ref, t0_ref, t1_ref, c0_ref, c1_ref, keep_ref, send_ref):
    bins = gate_bins(frames_ref, steps_ref, seq_ref)
    for table_ref, cot_ref, out_ref in ((t0_ref, c0_ref, keep_ref), (t1_ref, c1_ref, send_ref)):
        for k, b in enumerate(bins):
            rows = slice(k * FRAME, (k + 1) * FRAME)
            out_ref[rows, :] = (table_ref[pl.ds(b, 1), :] * cot_ref[rows, :].astype(F32)).astype(BF)


def gated_cotangent(frames, steps, seq, table, cotangent):
    def half(rows, flip):
        return pl.BlockSpec((rows, 768), lambda n, f, t, s: (0, 2 * (s[0] % 2 ^ flip) + n))

    out = pl.BlockSpec((128, 768), lambda n, *_: (0, n))
    return pl.pallas_call(
        gated_kernel,
        out_shape=(jax.ShapeDtypeStruct((128, 1536), BF),) * 2,
        grid_spec=pltpu.PrefetchScalarGridSpec(
            num_scalar_prefetch=3,
            grid=(2,),
            in_specs=[half(64, 0), half(64, 1), half(128, 0), half(128, 1)],
            out_specs=(out, out),
        ),
        cost_estimate=cost(3),
        name="gated_cotangent",
    )(frames, steps, seq, table, table, cotangent, cotangent)


def output_kernel(
    frames_ref, steps_ref, seq_ref, t0_ref, t1_ref, l0_ref, l1_ref, own_ref, other_ref, out_ref
):
    bins = gate_bins(frames_ref, steps_ref, seq_ref)
    z = seq_ref[0] % 2
    halves = ((z, t0_ref, l0_ref, own_ref), (1 - z, t1_ref, l1_ref, other_ref))
    for place, table_ref, lat_ref, proj_ref in halves:
        at = pl.multiple_of(place * 1536, 1536)
        for k, b in enumerate(bins):
            rows = slice(k * FRAME, (k + 1) * FRAME)
            proj = proj_ref[rows, :].astype(F32)
            out = lat_ref[rows, :].astype(F32) + table_ref[pl.ds(b, 1), :] * proj
            out_ref[rows, pl.ds(at, 1536)] = out.astype(BF)


def gated_output(frames, steps, seq, table, latents, own, other):
    def half(rows, flip):
        return pl.BlockSpec((rows, 1536), lambda n, f, t, s: (0, s[0] % 2 ^ flip))

    return pl.pallas_call(
        output_kernel,
        out_shape=jax.ShapeDtypeStruct((128, 3072), BF),
        grid_spec=pltpu.PrefetchScalarGridSpec(
            num_scalar_prefetch=3,
            grid=(1,),
            in_specs=[half(64, 0), half(64, 1), half(128, 0), half(128, 1), VMEM, VMEM],
            out_specs=pl.BlockSpec((128, 3072), lambda n, *_: (0, 0)),
        ),
        cost_estimate=cost(3),
        name="gated_output",
    )(frames, steps, seq, table, table, latents, latents, own, other)


def dattn_kernel(seq_ref, *refs):
    blocks, (w_ref, dproj_ref, other_ref, own_ref) = refs[:8], refs[8:]
    x, z = seq_ref[0] // 2, seq_ref[0] % 2
    for i, block in enumerate(blocks):
        place = 2 * ((x + i // 2) % 4) + (z ^ (i % 2))
        dproj_ref[pl.ds(pl.multiple_of(place * 128, 128), 128), :] = block[...]
    for m in range(2):
        rows = slice(m * 512, (m + 1) * 512)
        d = dproj_ref[rows, :]
        other_ref[rows, :] = dot_nn(d, w_ref[1]).astype(BF)
        own_ref[rows, :] = dot_nn(d, w_ref[0])


def dattn_parts(seq, blocks, weights):
    return pl.pallas_call(
        dattn_kernel,
        out_shape=(
            jax.ShapeDtypeStruct((1024, 1536), BF),
            jax.ShapeDtypeStruct((1024, 384), BF),
            jax.ShapeDtypeStruct((1024, 384), F32),
        ),
        in_specs=[SMEM] + [VMEM] * 9,
        out_specs=(VMEM, whole((1024, 384)), VMEM),
        compiler_params=PARAMS,
        cost_estimate=cost(7),
        name="dattn_parts",
    )(seq, *blocks, weights)


def project(seq_ref, k, own_ref, other_ref, w_ref):
    rows = pl.ds(pl.multiple_of((seq_ref[0] // 2 + k) % 4 * 256, 256), 256)
    return dot_nt(own_ref[rows, :], w_ref[0]) + dot_nt(other_ref[rows, :], w_ref[1])


def far_kernel(seq_ref, a_ref, b_ref, w_ref, up_ref, down_ref):
    part = project(seq_ref, 2, a_ref, b_ref, w_ref).astype(BF)
    up_ref[...] = part[:128]
    down_ref[...] = part[128:]


def near_kernel(seq_ref, a_ref, b_ref, w_ref, up_ref, down_ref, t1_ref, t3_ref):
    p1 = project(seq_ref, 1, a_ref, b_ref, w_ref)
    t1_ref[:128] = (p1[:128] + up_ref[...].astype(F32)).astype(BF)
    t1_ref[128:] = p1[128:].astype(BF)
    p3 = project(seq_ref, 3, a_ref, b_ref, w_ref)
    t3_ref[:128] = p3[:128].astype(BF)
    t3_ref[128:] = (p3[128:] + down_ref[...].astype(F32)).astype(BF)


def home_kernel(seq_ref, a_ref, b_ref, w_ref, c1_ref, c3_ref, keep_ref, send_ref):
    part = project(seq_ref, 0, a_ref, b_ref, w_ref)
    part = part + c1_ref[...].astype(F32) + c3_ref[...].astype(F32)
    first = seq_ref[0] % 2 == 0
    keep_ref[...] = jnp.where(first, part[:128], part[128:])
    send_ref[...] = jnp.where(first, part[128:], part[:128]).astype(BF)


def project_call(kernel, name, inputs, out_shape, out_specs):
    return pl.pallas_call(
        kernel,
        out_shape=out_shape,
        in_specs=[SMEM] + [VMEM] * inputs,
        out_specs=out_specs,
        compiler_params=PARAMS,
        cost_estimate=cost(3),
        name=name,
    )


def project_far(seq, own, other, weights):
    one = whole((128, 1536))
    call = project_call(far_kernel, "project_far", 3, (shape((128, 1536)),) * 2, (one, one))
    return call(seq, own, other, weights)


def project_near(seq, own, other, weights, up, down):
    two = whole((256, 1536))
    call = project_call(near_kernel, "project_near", 5, (shape((256, 1536)),) * 2, (two, two))
    return call(seq, own, other, weights, up, down)


def project_home(seq, own, other, weights, c1, c3):
    call = project_call(
        home_kernel,
        "project_home",
        5,
        (shape((128, 1536), F32), shape((128, 1536))),
        (VMEM, whole((128, 1536))),
    )
    return call(seq, own, other, weights, c1, c3)


def dweight_kernel(dp_ref, d_ref, a_ref, keep_ref, send_ref):
    even = dp_ref[0] % 2 == 0
    for n in range(2):
        g = dot_tn(d_ref[:, n * 768 : (n + 1) * 768], a_ref[...]).astype(BF)
        for i in range(4):
            p0, p1 = g[i * 192 : i * 192 + 96], g[i * 192 + 96 : i * 192 + 192]
            keep_ref[n * 4 + i] = jnp.where(even, p0, p1)
            send_ref[n * 4 + i] = jnp.where(even, p1, p0)


def dweight_part(dp, dproj, attn):
    return pl.pallas_call(
        dweight_kernel,
        out_shape=(shape((8, 96, 384)), shape((8, 96, 384))),
        in_specs=[SMEM, VMEM, VMEM],
        out_specs=(VMEM, whole((8, 96, 384))),
        compiler_params=PARAMS,
        cost_estimate=cost(4),
        name="dweight_part",
    )(dp, dproj, attn)


def pair_kernel(dp_ref, k0_ref, g0_ref, k1_ref, g1_ref, *out_refs):
    y = dp_ref[0] // 8
    for k, out_ref in enumerate(out_refs):
        at = (y + k) % 4
        for half, (keep_ref, got_ref) in enumerate(((k0_ref, g0_ref), (k1_ref, g1_ref))):

            @pl.when(at // 2 == half)
            def _(keep_ref=keep_ref, got_ref=got_ref, out_ref=out_ref, at=at):
                total = keep_ref[at % 2].astype(F32) + got_ref[at % 2].astype(F32)
                out_ref[...] = total.astype(BF)


def pair_sum(dp, keep0, got0, keep1, got1):
    terms = [t.reshape(2, 4, 96, 384) for t in (keep0, got0, keep1, got1)]
    return pl.pallas_call(
        pair_kernel,
        out_shape=(jax.ShapeDtypeStruct((4, 96, 384), BF),) * 4,
        in_specs=[SMEM] + [VMEM] * 4,
        out_specs=(pl.BlockSpec((4, 96, 384), lambda: (0, 0, 0)),) * 4,
        compiler_params=PARAMS,
        cost_estimate=cost(3),
        name="pair_sum",
    )(dp, *terms)


def ring_kernel(dp_ref, a_ref, b_ref, c_ref, d_ref, *out_refs):
    zh = dp_ref[0] // 2 % 4
    for k, out_ref in enumerate(out_refs):
        at = (zh + k) % 4
        total = a_ref[at].astype(F32) + b_ref[at].astype(F32)
        out_ref[...] = (total + c_ref[at].astype(F32) + d_ref[at].astype(F32)).astype(BF)


def ring_sum(dp, parts):
    return pl.pallas_call(
        ring_kernel,
        out_shape=(jax.ShapeDtypeStruct((96, 384), BF),) * 4,
        in_specs=[SMEM] + [VMEM] * 4,
        out_specs=(pl.BlockSpec((96, 384), lambda: (0, 0)),) * 4,
        compiler_params=PARAMS,
        cost_estimate=cost(2),
        name="ring_sum",
    )(dp, *parts)


def piece_moves(dp_count, seq_count):
    half = dp_count // 2
    moves = []
    for dp in range(dp_count):
        for seq in range(seq_count):
            top, z = dp // half, seq % 2
            to_dp = (dp % half) + half * (z ^ top)
            to_seq = seq - z + top
            moves.append((dp * seq_count + seq, to_dp * seq_count + to_seq))
    return moves


def along(x, axis, stride, places):
    size = lax.axis_size(axis)
    moves = []
    for i in range(size):
        at = i // stride % 4
        moves.append((i, i + ((at + places) % 4 - at) * stride))
    return lax.ppermute(x, axis, moves)


def along_x(x, places):
    return along(x, "seq", 2, places)


def along_y(x, places):
    return along(x, "dp", 8, places)


def along_z(x, places):
    return along(x, "dp", 2, places)


def swap_z(x):
    return lax.ppermute(x, "seq", [(i, i ^ 1) for i in range(lax.axis_size("seq"))])


def swap_core(x):
    return lax.ppermute(x, "dp", [(i, i ^ 1) for i in range(lax.axis_size("dp"))])


def body(qkv_input, latents, cotangent, out_weight, gate_table, timesteps, frames):
    seq = lax.axis_index("seq").astype(jnp.int32).reshape(1)
    dp = lax.axis_index("dp").astype(jnp.int32).reshape(1)
    both = ("dp", "seq")
    moves = piece_moves(lax.axis_size("dp"), lax.axis_size("seq"))

    piece = lax.ppermute(out_weight.T, both, moves)
    keep, send = gated_cotangent(frames, timesteps, seq, gate_table, cotangent)
    qkv_input, piece, keep, send = lax.optimization_barrier((qkv_input, piece, keep, send))
    weights = lax.all_gather(piece, "dp", axis=0, tiled=True).reshape(2, 1536, 384)
    got = swap_z(send)
    b1_keep, b3_keep = along_x(keep, -1), along_x(keep, 1)
    packed = pack_heads(qkv_input.transpose(1, 0, 2))
    packed, got, b1_keep, b3_keep = lax.optimization_barrier((packed, got, b1_keep, b3_keep))
    heads = lax.all_to_all(packed, "seq", split_axis=0, concat_axis=0, tiled=True)

    b1 = [b1_keep, along_x(got, -1)]
    b3 = [b3_keep, along_x(got, 1)]
    b2 = [along_x(b3[0], 1), along_x(b1[1], -1)]

    attn, p1, p2 = attention_forward(frames, heads)
    attn_other = swap_z(attn)
    dproj, d_send, d_own = dattn_parts(seq, [keep, got, *b1, *b2, *b3], weights)
    d_recv = swap_z(d_send)
    keep0, send0 = dweight_part(dp, dproj, attn)
    attn_other, keep0 = lax.optimization_barrier((attn_other, keep0))
    got0 = swap_core(send0)
    up, down = project_far(seq, attn, attn_other, weights)
    behind, _ = lax.optimization_barrier((dproj, up))
    keep1, send1 = dweight_part(dp, behind, attn_other)
    got1 = swap_core(send1)
    up, down = along_x(up, 1), along_x(down, -1)
    up, keep1 = lax.optimization_barrier((up, keep1))
    t1, t3 = project_near(seq, attn, attn_other, weights, up, down)
    d_own, d_recv, t1, t3 = lax.optimization_barrier((d_own, d_recv, t1, t3))
    c1, c3 = along_x(t1, 1), along_x(t3, -1)
    terms = pair_sum(dp, keep0, got0, keep1, got1)
    d_own, terms = lax.optimization_barrier((d_own, terms))
    terms = [terms[0]] + [along_y(terms[k], k) for k in range(1, 4)]

    grads = attention_backward(frames, heads, d_own, d_recv, p1, p2)
    terms, grads = lax.optimization_barrier((terms, grads))
    terms = ring_sum(dp, terms)
    terms = [terms[0]] + [along_z(terms[k], k) for k in range(1, 4)]
    o_keep, o_send = project_home(seq, attn, attn_other, weights, c1, c3)
    grads, o_send, terms = lax.optimization_barrier((grads, o_send, terms))
    o_got = swap_z(o_send)
    grads = lax.all_to_all(grads, "seq", split_axis=0, concat_axis=0, tiled=True)

    total = terms[0].astype(F32) + terms[1].astype(F32)
    total = total + terms[2].astype(F32) + terms[3].astype(F32)
    total = lax.ppermute(total, both, [(b, a) for a, b in moves])
    total, o_got = lax.optimization_barrier((total, o_got))
    output = gated_output(frames, timesteps, seq, gate_table, latents, o_keep, o_got)
    grad_qkv = unpack_heads(grads)
    return (output, grad_qkv.transpose(1, 0, 2), total.T)


def solution(mesh):
    placed = (
        P(("dp", "seq"), None, None),
        P(("dp", "seq"), None),
        P(("dp", "seq"), None),
        P("seq", "dp"),
        P(),
        P("dp", None),
        P("dp", None),
    )
    return jax.shard_map(
        body,
        mesh=mesh,
        in_specs=placed,
        out_specs=(P(("dp", "seq"), None), P(("dp", "seq"), None, None), P("seq", "dp")),
        check_vma=False,
    )
```

```python
import jax
import jax.numpy as jnp
from jax import lax
from jax.experimental import pallas as pl
from jax.experimental.pallas import tpu as pltpu
from jax.sharding import PartitionSpec as P

HD = 128
FRAME = 64
LONG = 640
REST = 384
LOG2E = 1.4426950408889634
VMEM_LIMIT = 32 * 1024 * 1024

BF = jnp.bfloat16
F32 = jnp.float32
VMEM = pl.BlockSpec(memory_space=pltpu.VMEM)
SMEM = pl.BlockSpec(memory_space=pltpu.SMEM)
PARAMS = pltpu.CompilerParams(vmem_limit_bytes=VMEM_LIMIT)


def shape(dims, dtype=BF):
    return jax.ShapeDtypeStruct(dims, dtype)


def whole(dims):
    return pl.BlockSpec(dims, lambda: (0,) * len(dims))


def cost(us):
    return pl.CostEstimate(flops=int(us * 1e9), transcendentals=0, bytes_accessed=int(us * 3e6))


def dot_nt(a, b):
    return lax.dot_general(a, b, (((1,), (1,)), ((), ())), preferred_element_type=F32)


def dot_nn(a, b):
    return lax.dot_general(a, b, (((1,), (0,)), ((), ())), preferred_element_type=F32)


def dot_tn(a, b):
    return lax.dot_general(a, b, (((0,), (0,)), ((), ())), preferred_element_type=F32)


def clip_places(frames_ref):
    f0, f1, f2 = frames_ref[0, 0], frames_ref[0, 1], frames_ref[0, 2]
    first = jnp.logical_and(f0 > f1, f0 > f2)
    second = f1 > f2
    start = jnp.where(first, 0, jnp.where(second, f0, f0 + f1)) * FRAME
    lead = jnp.where(first, f1, f0)
    return start, lead


def gate_bins(frames_ref, steps_ref, seq_ref):
    f0, f1 = frames_ref[0, 0], frames_ref[0, 1]
    bins = []
    for k in range(2):
        frame = seq_ref[0] * 2 + k
        clip = jnp.where(frame >= f0, 1, 0) + jnp.where(frame >= f0 + f1, 1, 0)
        bins.append(steps_ref[0, clip])
    return bins


def spans(total):
    out, at = [], 0
    while at < total:
        size = min(128, total - at)
        out.append((at, size))
        at += size
    return out


def rest_places(start):
    return [
        pl.multiple_of(jnp.where(t * FRAME >= start, t * FRAME + LONG, t * FRAME), FRAME)
        for t in range(REST // FRAME)
    ]


def load_split(src, start):
    main = src[pl.ds(start, LONG), :]
    rest = jnp.concatenate([src[pl.ds(p, FRAME), :] for p in rest_places(start)], axis=0)
    return main, rest


def rest_mask(lead, at, size):
    rows = lax.broadcasted_iota(jnp.int32, (REST, size), 0)
    cols = lax.broadcasted_iota(jnp.int32, (REST, size), 1) + at
    edge = lead * FRAME
    return (rows < edge) == (cols < edge)


def fwd_kernel(frames_ref, qkv_ref, attn_ref, p1_ref, p2_ref, q_s, k_s, v_s):
    start, lead = clip_places(frames_ref)
    start = pl.multiple_of(start, FRAME)
    places = rest_places(start)
    factor = LOG2E / (HD**0.5)

    def head(h, carry):
        lanes = pl.ds(pl.multiple_of(h * HD, HD), HD)
        q_s[...] = qkv_ref[:, 0, :, lanes].reshape(1024, HD)
        k_s[...] = qkv_ref[:, 1, :, lanes].reshape(1024, HD)
        v_s[...] = qkv_ref[:, 2, :, lanes].reshape(1024, HD)
        q1, q2 = load_split(q_s, start)
        k1, k2 = load_split(k_s, start)
        v1, v2 = load_split(v_s, start)
        for long, (q, k, v, p_ref) in ((True, (q1, k1, v1, p1_ref)), (False, (q2, k2, v2, p2_ref))):
            vt = v.astype(F32).T.astype(BF)
            for at, size in spans(LONG if long else REST):
                s = dot_nt(k, q[at : at + size])
                if not long:
                    s = jnp.where(rest_mask(lead, at, size), s, F32(-1e30))
                top = jnp.max(s, axis=0, keepdims=True)
                e = jnp.exp2((s - top) * F32(factor))
                total = jnp.sum(e, axis=0, keepdims=True)
                p = (e * (1.0 / total)).astype(BF)
                p_ref[h, :, at : at + size] = p
                o = dot_nn(vt, p).T.astype(BF)
                if long:
                    attn_ref[pl.ds(start + at, size), lanes] = o
                else:
                    for t in range(size // FRAME):
                        attn_ref[pl.ds(places[at // FRAME + t], FRAME), lanes] = o[
                            t * FRAME : (t + 1) * FRAME
                        ]
        return carry

    lax.fori_loop(0, 3, head, 0)


def attention_forward(frames, heads):
    return pl.pallas_call(
        fwd_kernel,
        out_shape=(shape((1024, 3 * HD)), shape((3, LONG, LONG)), shape((3, REST, REST))),
        in_specs=[SMEM, VMEM],
        out_specs=(whole((1024, 3 * HD)), VMEM, VMEM),
        scratch_shapes=[pltpu.VMEM((1024, HD), BF)] * 3,
        compiler_params=PARAMS,
        cost_estimate=cost(0.1),
        name="attention_forward",
    )(frames, heads)


def bwd_kernel(
    frames_ref, qkv_ref, own_ref, other_ref, p1_ref, p2_ref, out_ref, q_s, k_s, v_s, d_s, ds1, ds2, g_s
):
    start, lead = clip_places(frames_ref)
    start = pl.multiple_of(start, FRAME)
    places = rest_places(start)
    scale = 1.0 / (HD**0.5)

    def put(which, long, value):
        if long:
            g_s[which, pl.ds(start, LONG), :] = value
        else:
            for t in range(REST // FRAME):
                g_s[which, pl.ds(places[t], FRAME), :] = value[t * FRAME : (t + 1) * FRAME]

    def head(h, carry):
        lanes = pl.ds(pl.multiple_of(h * HD, HD), HD)
        q_s[...] = qkv_ref[:, 0, :, lanes].reshape(1024, HD)
        k_s[...] = qkv_ref[:, 1, :, lanes].reshape(1024, HD)
        v_s[...] = qkv_ref[:, 2, :, lanes].reshape(1024, HD)
        d_s[...] = (own_ref[:, lanes] + other_ref[:, lanes].astype(F32)).astype(BF)
        q1, q2 = load_split(q_s, start)
        k1, k2 = load_split(k_s, start)
        v1, v2 = load_split(v_s, start)
        d1, d2 = load_split(d_s, start)
        for long, (q, k, v, d, p_ref, ds_ref) in (
            (True, (q1, k1, v1, d1, p1_ref, ds1)),
            (False, (q2, k2, v2, d2, p2_ref, ds2)),
        ):
            kt = k.astype(F32).T.astype(BF)
            parts = []
            for at, size in spans(LONG if long else REST):
                dp = dot_nt(v, d[at : at + size]).astype(BF).astype(F32)
                p = p_ref[h, :, at : at + size].astype(F32)
                pd = p * dp
                delta = jnp.sum(pd, axis=0, keepdims=True)
                ds = ((pd - p * delta) * F32(scale)).astype(BF)
                ds_ref[:, at : at + size] = ds
                parts.append(dot_nn(kt, ds).T.astype(BF))
            put(0, long, jnp.concatenate(parts, axis=0))
            put(1, long, dot_nn(ds_ref[...], q).astype(BF))
            put(2, long, dot_nn(p_ref[h], d).astype(BF))
        for which in range(3):
            out_ref[:, which, :, lanes] = g_s[which].reshape(8, 128, HD)
        return carry

    lax.fori_loop(0, 3, head, 0)


def attention_backward(frames, heads, own, other, p1, p2):
    return pl.pallas_call(
        bwd_kernel,
        out_shape=shape((8, 3, 128, 3 * HD)),
        in_specs=[SMEM, VMEM, VMEM, VMEM, VMEM, VMEM],
        out_specs=whole((8, 3, 128, 3 * HD)),
        scratch_shapes=[pltpu.VMEM((1024, HD), BF)] * 4
        + [
            pltpu.VMEM((LONG, LONG), BF),
            pltpu.VMEM((REST, REST), BF),
            pltpu.VMEM((3, 1024, HD), BF),
        ],
        compiler_params=PARAMS,
        cost_estimate=cost(10),
        name="attention_backward",
    )(frames, heads, own, other, p1, p2)


def pack_kernel(in_ref, out_ref):
    for j in range(4):
        out_ref[j] = in_ref[:, :, j * 384 : (j + 1) * 384]


def pack_heads(qkv):
    return pl.pallas_call(
        pack_kernel,
        out_shape=jax.ShapeDtypeStruct((8, 3, 128, 384), BF),
        grid=(2,),
        in_specs=[pl.BlockSpec((3, 128, 1536), lambda j: (0, 0, j))],
        out_specs=pl.BlockSpec((4, 3, 128, 384), lambda j: (j, 0, 0, 0)),
        cost_estimate=cost(3),
        name="pack_heads",
    )(qkv)


def unpack_kernel(in_ref, out_ref):
    for j in range(8):
        out_ref[:, :, j * 384 : (j + 1) * 384] = in_ref[j]


def unpack_heads(grads):
    return pl.pallas_call(
        unpack_kernel,
        out_shape=shape((3, 128, 3072)),
        in_specs=[VMEM],
        out_specs=whole((3, 128, 3072)),
        compiler_params=PARAMS,
        cost_estimate=cost(3),
        name="unpack_heads",
    )(grads)


def gated_kernel(frames_ref, steps_ref, seq_ref, t0_ref, t1_ref, c0_ref, c1_ref, keep_ref, send_ref):
    bins = gate_bins(frames_ref, steps_ref, seq_ref)
    for table_ref, cot_ref, out_ref in ((t0_ref, c0_ref, keep_ref), (t1_ref, c1_ref, send_ref)):
        for k, b in enumerate(bins):
            rows = slice(k * FRAME, (k + 1) * FRAME)
            out_ref[rows, :] = (table_ref[pl.ds(b, 1), :] * cot_ref[rows, :].astype(F32)).astype(BF)


def gated_cotangent(frames, steps, seq, table, cotangent):
    def half(rows, flip):
        return pl.BlockSpec((rows, 768), lambda n, f, t, s: (0, 2 * (s[0] % 2 ^ flip) + n))

    out = pl.BlockSpec((128, 768), lambda n, *_: (0, n))
    return pl.pallas_call(
        gated_kernel,
        out_shape=(jax.ShapeDtypeStruct((128, 1536), BF),) * 2,
        grid_spec=pltpu.PrefetchScalarGridSpec(
            num_scalar_prefetch=3,
            grid=(2,),
            in_specs=[half(64, 0), half(64, 1), half(128, 0), half(128, 1)],
            out_specs=(out, out),
        ),
        cost_estimate=cost(3),
        name="gated_cotangent",
    )(frames, steps, seq, table, table, cotangent, cotangent)


def output_kernel(
    frames_ref, steps_ref, seq_ref, t0_ref, t1_ref, l0_ref, l1_ref, own_ref, other_ref, out_ref
):
    bins = gate_bins(frames_ref, steps_ref, seq_ref)
    z = seq_ref[0] % 2
    halves = ((z, t0_ref, l0_ref, own_ref), (1 - z, t1_ref, l1_ref, other_ref))
    for place, table_ref, lat_ref, proj_ref in halves:
        at = pl.multiple_of(place * 1536, 1536)
        for k, b in enumerate(bins):
            rows = slice(k * FRAME, (k + 1) * FRAME)
            proj = proj_ref[rows, :].astype(F32)
            out = lat_ref[rows, :].astype(F32) + table_ref[pl.ds(b, 1), :] * proj
            out_ref[rows, pl.ds(at, 1536)] = out.astype(BF)


def gated_output(frames, steps, seq, table, latents, own, other):
    def half(rows, flip):
        return pl.BlockSpec((rows, 1536), lambda n, f, t, s: (0, s[0] % 2 ^ flip))

    return pl.pallas_call(
        output_kernel,
        out_shape=jax.ShapeDtypeStruct((128, 3072), BF),
        grid_spec=pltpu.PrefetchScalarGridSpec(
            num_scalar_prefetch=3,
            grid=(1,),
            in_specs=[half(64, 0), half(64, 1), half(128, 0), half(128, 1), VMEM, VMEM],
            out_specs=pl.BlockSpec((128, 3072), lambda n, *_: (0, 0)),
        ),
        cost_estimate=cost(3),
        name="gated_output",
    )(frames, steps, seq, table, table, latents, latents, own, other)


def dattn_kernel(seq_ref, *refs):
    blocks, (w_ref, dproj_ref, other_ref, own_ref) = refs[:8], refs[8:]
    x, z = seq_ref[0] // 2, seq_ref[0] % 2
    for i, block in enumerate(blocks):
        place = 2 * ((x + i // 2) % 4) + (z ^ (i % 2))
        dproj_ref[pl.ds(pl.multiple_of(place * 128, 128), 128), :] = block[...]
    for m in range(2):
        rows = slice(m * 512, (m + 1) * 512)
        d = dproj_ref[rows, :]
        other_ref[rows, :] = dot_nn(d, w_ref[1]).astype(BF)
        own_ref[rows, :] = dot_nn(d, w_ref[0])


def dattn_parts(seq, blocks, weights):
    return pl.pallas_call(
        dattn_kernel,
        out_shape=(
            jax.ShapeDtypeStruct((1024, 1536), BF),
            jax.ShapeDtypeStruct((1024, 384), BF),
            jax.ShapeDtypeStruct((1024, 384), F32),
        ),
        in_specs=[SMEM] + [VMEM] * 9,
        out_specs=(VMEM, whole((1024, 384)), VMEM),
        compiler_params=PARAMS,
        cost_estimate=cost(7),
        name="dattn_parts",
    )(seq, *blocks, weights)


def project(seq_ref, k, own_ref, other_ref, w_ref):
    rows = pl.ds(pl.multiple_of((seq_ref[0] // 2 + k) % 4 * 256, 256), 256)
    return dot_nt(own_ref[rows, :], w_ref[0]) + dot_nt(other_ref[rows, :], w_ref[1])


def far_kernel(seq_ref, a_ref, b_ref, w_ref, up_ref, down_ref):
    part = project(seq_ref, 2, a_ref, b_ref, w_ref).astype(BF)
    up_ref[...] = part[:128]
    down_ref[...] = part[128:]


def near_kernel(seq_ref, a_ref, b_ref, w_ref, up_ref, down_ref, t1_ref, t3_ref):
    p1 = project(seq_ref, 1, a_ref, b_ref, w_ref)
    t1_ref[:128] = (p1[:128] + up_ref[...].astype(F32)).astype(BF)
    t1_ref[128:] = p1[128:].astype(BF)
    p3 = project(seq_ref, 3, a_ref, b_ref, w_ref)
    t3_ref[:128] = p3[:128].astype(BF)
    t3_ref[128:] = (p3[128:] + down_ref[...].astype(F32)).astype(BF)


def home_kernel(seq_ref, a_ref, b_ref, w_ref, c1_ref, c3_ref, keep_ref, send_ref):
    part = project(seq_ref, 0, a_ref, b_ref, w_ref)
    part = part + c1_ref[...].astype(F32) + c3_ref[...].astype(F32)
    first = seq_ref[0] % 2 == 0
    keep_ref[...] = jnp.where(first, part[:128], part[128:])
    send_ref[...] = jnp.where(first, part[128:], part[:128]).astype(BF)


def project_call(kernel, name, inputs, out_shape, out_specs):
    return pl.pallas_call(
        kernel,
        out_shape=out_shape,
        in_specs=[SMEM] + [VMEM] * inputs,
        out_specs=out_specs,
        compiler_params=PARAMS,
        cost_estimate=cost(3),
        name=name,
    )


def project_far(seq, own, other, weights):
    one = whole((128, 1536))
    call = project_call(far_kernel, "project_far", 3, (shape((128, 1536)),) * 2, (one, one))
    return call(seq, own, other, weights)


def project_near(seq, own, other, weights, up, down):
    two = whole((256, 1536))
    call = project_call(near_kernel, "project_near", 5, (shape((256, 1536)),) * 2, (two, two))
    return call(seq, own, other, weights, up, down)


def project_home(seq, own, other, weights, c1, c3):
    call = project_call(
        home_kernel,
        "project_home",
        5,
        (shape((128, 1536), F32), shape((128, 1536))),
        (VMEM, whole((128, 1536))),
    )
    return call(seq, own, other, weights, c1, c3)


def dweight_kernel(dp_ref, d_ref, a_ref, keep_ref, send_ref):
    even = dp_ref[0] % 2 == 0
    for n in range(2):
        g = dot_tn(d_ref[:, n * 768 : (n + 1) * 768], a_ref[...]).astype(BF)
        for i in range(4):
            p0, p1 = g[i * 192 : i * 192 + 96], g[i * 192 + 96 : i * 192 + 192]
            keep_ref[n * 4 + i] = jnp.where(even, p0, p1)
            send_ref[n * 4 + i] = jnp.where(even, p1, p0)


def dweight_part(dp, dproj, attn):
    return pl.pallas_call(
        dweight_kernel,
        out_shape=(shape((8, 96, 384)), shape((8, 96, 384))),
        in_specs=[SMEM, VMEM, VMEM],
        out_specs=(VMEM, whole((8, 96, 384))),
        compiler_params=PARAMS,
        cost_estimate=cost(4),
        name="dweight_part",
    )(dp, dproj, attn)


def pair_kernel(dp_ref, k0_ref, g0_ref, k1_ref, g1_ref, *out_refs):
    y = dp_ref[0] // 8
    for k, out_ref in enumerate(out_refs):
        at = (y + k) % 4
        for half, (keep_ref, got_ref) in enumerate(((k0_ref, g0_ref), (k1_ref, g1_ref))):

            @pl.when(at // 2 == half)
            def _(keep_ref=keep_ref, got_ref=got_ref, out_ref=out_ref, at=at):
                total = keep_ref[at % 2].astype(F32) + got_ref[at % 2].astype(F32)
                out_ref[...] = total.astype(BF)


def pair_sum(dp, keep0, got0, keep1, got1):
    terms = [t.reshape(2, 4, 96, 384) for t in (keep0, got0, keep1, got1)]
    return pl.pallas_call(
        pair_kernel,
        out_shape=(jax.ShapeDtypeStruct((4, 96, 384), BF),) * 4,
        in_specs=[SMEM] + [VMEM] * 4,
        out_specs=(pl.BlockSpec((4, 96, 384), lambda: (0, 0, 0)),) * 4,
        compiler_params=PARAMS,
        cost_estimate=cost(3),
        name="pair_sum",
    )(dp, *terms)


def ring_kernel(dp_ref, a_ref, b_ref, c_ref, d_ref, *out_refs):
    zh = dp_ref[0] // 2 % 4
    for k, out_ref in enumerate(out_refs):
        at = (zh + k) % 4
        total = a_ref[at].astype(F32) + b_ref[at].astype(F32)
        out_ref[...] = (total + c_ref[at].astype(F32) + d_ref[at].astype(F32)).astype(BF)


def ring_sum(dp, parts):
    return pl.pallas_call(
        ring_kernel,
        out_shape=(jax.ShapeDtypeStruct((96, 384), BF),) * 4,
        in_specs=[SMEM] + [VMEM] * 4,
        out_specs=(pl.BlockSpec((96, 384), lambda: (0, 0)),) * 4,
        compiler_params=PARAMS,
        cost_estimate=cost(2),
        name="ring_sum",
    )(dp, *parts)


def piece_moves(dp_count, seq_count):
    half = dp_count // 2
    moves = []
    for dp in range(dp_count):
        for seq in range(seq_count):
            top, z = dp // half, seq % 2
            to_dp = (dp % half) + half * (z ^ top)
            to_seq = seq - z + top
            moves.append((dp * seq_count + seq, to_dp * seq_count + to_seq))
    return moves


def along(x, axis, stride, places):
    size = lax.axis_size(axis)
    moves = []
    for i in range(size):
        at = i // stride % 4
        moves.append((i, i + ((at + places) % 4 - at) * stride))
    return lax.ppermute(x, axis, moves)


def along_x(x, places):
    return along(x, "seq", 2, places)


def along_y(x, places):
    return along(x, "dp", 8, places)


def along_z(x, places):
    return along(x, "dp", 2, places)


def swap_z(x):
    return lax.ppermute(x, "seq", [(i, i ^ 1) for i in range(lax.axis_size("seq"))])


def swap_core(x):
    return lax.ppermute(x, "dp", [(i, i ^ 1) for i in range(lax.axis_size("dp"))])


def body(qkv_input, latents, cotangent, out_weight, gate_table, timesteps, frames):
    seq = lax.axis_index("seq").astype(jnp.int32).reshape(1)
    dp = lax.axis_index("dp").astype(jnp.int32).reshape(1)
    both = ("dp", "seq")
    moves = piece_moves(lax.axis_size("dp"), lax.axis_size("seq"))

    piece = lax.ppermute(out_weight.T, both, moves)
    keep, send = gated_cotangent(frames, timesteps, seq, gate_table, cotangent)
    qkv_input, piece, keep, send = lax.optimization_barrier((qkv_input, piece, keep, send))
    weights = lax.all_gather(piece, "dp", axis=0, tiled=True).reshape(2, 1536, 384)
    got = swap_z(send)
    b1_keep, b3_keep = along_x(keep, -1), along_x(keep, 1)
    packed = pack_heads(qkv_input.transpose(1, 0, 2))
    packed, got, b1_keep, b3_keep = lax.optimization_barrier((packed, got, b1_keep, b3_keep))
    heads = lax.all_to_all(packed, "seq", split_axis=0, concat_axis=0, tiled=True)

    b1 = [b1_keep, along_x(got, -1)]
    b3 = [b3_keep, along_x(got, 1)]
    b2 = [along_x(b3[0], 1), along_x(b1[1], -1)]

    attn, p1, p2 = attention_forward(frames, heads)
    attn_other = swap_z(attn)
    dproj, d_send, d_own = dattn_parts(seq, [keep, got, *b1, *b2, *b3], weights)
    d_recv = swap_z(d_send)
    keep0, send0 = dweight_part(dp, dproj, attn)
    attn_other, keep0 = lax.optimization_barrier((attn_other, keep0))
    got0 = swap_core(send0)
    up, down = project_far(seq, attn, attn_other, weights)
    behind, _ = lax.optimization_barrier((dproj, up))
    keep1, send1 = dweight_part(dp, behind, attn_other)
    got1 = swap_core(send1)
    up, down = along_x(up, 1), along_x(down, -1)
    up, keep1 = lax.optimization_barrier((up, keep1))
    t1, t3 = project_near(seq, attn, attn_other, weights, up, down)
    d_own, d_recv, t1, t3 = lax.optimization_barrier((d_own, d_recv, t1, t3))
    c1, c3 = along_x(t1, 1), along_x(t3, -1)
    terms = pair_sum(dp, keep0, got0, keep1, got1)
    d_own, terms = lax.optimization_barrier((d_own, terms))
    terms = [terms[0]] + [along_y(terms[k], k) for k in range(1, 4)]

    grads = attention_backward(frames, heads, d_own, d_recv, p1, p2)
    terms, grads = lax.optimization_barrier((terms, grads))
    terms = ring_sum(dp, terms)
    o_keep, o_send = project_home(seq, attn, attn_other, weights, c1, c3)
    grads, o_send, terms = lax.optimization_barrier((grads, o_send, terms))
    o_got = swap_z(o_send)
    grads = lax.all_to_all(grads, "seq", split_axis=0, concat_axis=0, tiled=True)

    terms = [terms[0]] + [along_z(terms[k], k) for k in range(1, 4)]
    output = gated_output(frames, timesteps, seq, gate_table, latents, o_keep, o_got)
    terms, output = lax.optimization_barrier((terms, output))
    total = terms[0].astype(F32) + terms[1].astype(F32)
    total = total + terms[2].astype(F32) + terms[3].astype(F32)
    total = lax.ppermute(total, both, [(b, a) for a, b in moves])
    grad_qkv = unpack_heads(grads)
    return (output, grad_qkv.transpose(1, 0, 2), total.T)


def solution(mesh):
    placed = (
        P(("dp", "seq"), None, None),
        P(("dp", "seq"), None),
        P(("dp", "seq"), None),
        P("seq", "dp"),
        P(),
        P("dp", None),
        P("dp", None),
    )
    return jax.shard_map(
        body,
        mesh=mesh,
        in_specs=placed,
        out_specs=(P(("dp", "seq"), None), P(("dp", "seq"), None, None), P("seq", "dp")),
        check_vma=False,
    )
```
